32 devices in a mesh: gx: 8 (over z, core), gy: 2 (over x), ga: 2 (over y).
Axes of the slice: x: 2, y: 2, z: 4, core: 2. Of those that a mesh axis runs over, the one named last changes fastest.
Arguments:
- euler_table: float32 [3, 2048], replicated, may hold values from -3.140625 to 3.140625
- crystal: float32 [21], replicated, may hold values from -0.08 to 3.4
- orient: int32 [32, 8, 2, 512], P('ga', 'gx', 'gy'), may hold values from 0 to 2047
- weight: bfloat16 [32, 8, 2, 512], P('ga', 'gx', 'gy'), may hold values from 0.099609375 to 1
- cell_map: int32 [8, 2, 512], P('gx', 'gy'), may hold values from 0 to 511, each once within a row
- density: float32 [64, 8, 16], P('gx', 'gy', 'ga'), may hold values from 0.5 to 2
- velocity: float32 [3, 64, 8, 16], P(None, 'gx', 'gy', 'ga'), may hold values from -6 to 6
- stress: float32 [6, 64, 8, 16], P(None, 'gx', 'gy', 'ga'), may hold values from -6 to 6
Outputs:
- stiffness: float32 [21, 64, 8, 16], P(None, 'gx', 'gy', 'ga')
- final_velocity: float32 [3, 64, 8, 16], P(None, 'gx', 'gy', 'ga')
- final_stress: float32 [6, 64, 8, 16], P(None, 'gx', 'gy', 'ga')
The draws below stay inside these ranges and needn't reach their ends.
Inputs may be any that keep to these rules, and one draw needn't show every extreme that they name: `cell_map`: each partition's row is a permutation of the 512 canonical indices.
All inputs are finite; a program needn't handle non-finite values.
Results may differ from the reference program's by a relative error of at most 0.0003.
Values sent between devices are 32-bit elements; how exact they have to be, the bound alone decides.
No kernel may reach another device: no remote copies, remote signals or barrier semaphores. Data moves between devices by JAX's collectives and lax.ppermute only.
A program may use at most 128 MiB of HBM per device.

```python
import math
import jax
import jax.numpy as jnp
from jax import lax

GRAINS = 32
ORIENTS = 2048
SUB_X = 1
SUB_Y = 2
STEPS = 2
PART_X = 8
PART_Y = 2
NX = 64
NY = 8
NZ = 16
CELLS = 512


def crystal_ranges():
    lower_ends = []
    upper_ends = []
    for row_index in range(6):
        for col_index in range(row_index, 6):
            if row_index == col_index and row_index < 3:
                lower_ends.append(2.4)
                upper_ends.append(3.4)
            elif row_index == col_index:
                lower_ends.append(0.6)
                upper_ends.append(0.9)
            elif col_index < 3:
                lower_ends.append(0.5)
                upper_ends.append(0.8)
            else:
                lower_ends.append(-0.08)
                upper_ends.append(0.08)
    return (jnp.array(lower_ends, jnp.float32), jnp.array(upper_ends, jnp.float32))


def draw_crystal(key, part):
    lower_ends, upper_ends = crystal_ranges()
    fresh = jax.random.uniform(jax.random.fold_in(key, 11), (21,), jnp.float32)
    return lower_ends + (upper_ends - lower_ends) * fresh


def place_ends(drawn, own_key, least, high):
    longest = drawn.shape.index(max(drawn.shape))
    spots = []
    for shift in (0, 1):
        where = [jax.random.randint(jax.random.fold_in(own_key, axis), (), 0, length) for axis, length in enumerate(drawn.shape)]
        where[longest] = (where[longest] + shift) % drawn.shape[longest]
        spots.append(tuple(where))
    return drawn.at[spots[0]].set(least).at[spots[1]].set(high)


def block_levels(stream_key, shape, split, low, high):
    gain = 1.0
    for axis_at, shards_of in split:
        draws = jax.random.uniform(jax.random.fold_in(jax.random.fold_in(stream_key, 6), axis_at), (shards_of,), jnp.float32, low / len(split), high / len(split))
        gain = gain * jnp.repeat(jnp.exp(draws), shape[axis_at] // shards_of).reshape((-1,) + (1,) * (len(shape) - 1 - axis_at))
    return gain


def centred(stream_key, shape, scale, bound, split=(), kind=jnp.bfloat16):
    drawn = jax.random.normal(stream_key, shape, jnp.float32) * scale
    if len(split) > 0:
        drawn = block_levels(stream_key, shape, split, -0.22, 0.18) * drawn
    return jnp.clip(drawn, min=-bound, max=bound).astype(kind)


def setup_inputs(seed: int = 0) -> dict:
    key_list = jax.random.split(jax.random.key(seed), 9)
    return {
        "euler_table": jnp.clip(jax.random.uniform(key_list[0], (3, ORIENTS), jnp.float32, -3.140625, 3.140625), -3.140625, 3.140625),
        "crystal": draw_crystal(jax.random.fold_in(key_list[8], 71), 0),
        "orient": place_ends(jax.random.randint(key_list[2], (GRAINS, PART_X, PART_Y, CELLS), 0, ORIENTS), jax.random.fold_in(key_list[2], 1), 0, ORIENTS - 1).astype(jnp.int32),
        "weight": jnp.clip(jnp.exp(math.log(1.0) - 2.306499 * jax.random.uniform(key_list[3], (GRAINS, PART_X, PART_Y, CELLS), jnp.float32) ** block_levels(key_list[3], (GRAINS, PART_X, PART_Y, CELLS), ((0, 2), (1, 8), (2, 2)), -0.2, 0.2)), 0.099609375, 1.0).astype(jnp.bfloat16),
        "cell_map": jax.vmap(lambda own: jax.random.permutation(own, CELLS))(jax.random.split(key_list[4], PART_X * PART_Y)).reshape((PART_X, PART_Y, CELLS)).astype(jnp.int32),
        "density": jnp.clip(jnp.exp(math.log(2.0) - 1.3862944 * jax.random.uniform(key_list[5], (NX, NY, NZ), jnp.float32) ** block_levels(key_list[5], (NX, NY, NZ), ((0, 8), (1, 2), (2, 2)), -0.2, 0.2)), 0.5, 2.0),
        "velocity": centred(key_list[6], (3, NX, NY, NZ), 1.0, 6.0, ((1, 8), (2, 2), (3, 2)), jnp.float32),
        "stress": centred(key_list[7], (6, NX, NY, NZ), 1.0, 6.0, ((1, 8), (2, 2), (3, 2)), jnp.float32),
    }


stencil_weights = (0.8, -0.2, 4.0 / 105.0, -1.0 / 280.0)
time_step = 0.2
grain_block = 4
voigt_pairs = ((0, 0), (1, 1), (2, 2), (1, 2), (0, 2), (0, 1))
upper_pairs = [(row_index, col_index) for row_index in range(6) for col_index in range(row_index, 6)]


def symmetric_index(first_index, second_index):
    return upper_pairs.index((min(first_index, second_index), max(first_index, second_index)))


def ordered_sum(summands):
    running = summands[0]
    for summand in summands[1:]:
        running = running + summand
    return running


def rotated_table(euler_table, crystal):
    cos_one, sin_one = jnp.cos(euler_table[0]), jnp.sin(euler_table[0])
    cos_mid, sin_mid = jnp.cos(euler_table[1]), jnp.sin(euler_table[1])
    cos_two, sin_two = jnp.cos(euler_table[2]), jnp.sin(euler_table[2])
    bunge = [[cos_one * cos_two - sin_one * sin_two * cos_mid, sin_one * cos_two + cos_one * sin_two * cos_mid, sin_two * sin_mid],
             [-cos_one * sin_two - sin_one * cos_two * cos_mid, -sin_one * sin_two + cos_one * cos_two * cos_mid, cos_two * sin_mid],
             [sin_one * sin_mid, -cos_one * sin_mid, cos_mid]]
    rotation = [[bunge[col_index][row_index] for col_index in range(3)] for row_index in range(3)]
    bond = []
    for out_index in range(6):
        first, second = voigt_pairs[out_index]
        bond_row = []
        for in_index in range(6):
            third, fourth = voigt_pairs[in_index]
            if in_index < 3:
                bond_row.append(rotation[first][third] * rotation[second][third])
            else:
                bond_row.append(rotation[first][third] * rotation[second][fourth] + rotation[first][fourth] * rotation[second][third])
        bond.append(bond_row)
    entries = [[crystal[symmetric_index(row_index, col_index)] for col_index in range(6)] for row_index in range(6)]
    product = [[ordered_sum([bond[row_index][inner] * entries[inner][col_index] for inner in range(6)]) for col_index in range(6)] for row_index in range(6)]
    rotated = [ordered_sum([product[row_index][inner] * bond[col_index][inner] for inner in range(6)]) for row_index, col_index in upper_pairs]
    return jnp.stack(rotated)


def accumulate(table, orient_rows, weight_rows):
    blocks = orient_rows.shape[0] // grain_block
    count_cells = orient_rows.shape[1]

    def absorb(carry, inputs):
        chosen, masses = inputs
        picked = jnp.take(table, chosen, axis=1)
        masses_wide = masses.astype(jnp.float32)
        return (carry[0] + jnp.sum(picked * masses_wide[None], axis=1), carry[1] + jnp.sum(masses_wide, axis=0)), None

    initial = (jnp.zeros((21, count_cells), jnp.float32), jnp.zeros((count_cells,), jnp.float32))
    result, unused = lax.scan(absorb, initial, (orient_rows.reshape(blocks, grain_block, count_cells), weight_rows.reshape(blocks, grain_block, count_cells)))
    return result


def derivative(padded, direction):
    interior = [padded.shape[0]] + [extent - 8 for extent in padded.shape[1:]]

    def window(offset):
        starts = [0, 4, 4, 4]
        starts[direction] = 4 + offset
        return lax.slice(padded, starts, [begin + extent for begin, extent in zip(starts, interior)])

    result = stencil_weights[0] * (window(1) - window(-1))
    for order_index in range(1, 4):
        result = result + stencil_weights[order_index] * (window(order_index + 1) - window(-order_index - 1))
    return result


def advance_velocity(velocity, padded_stress, density):
    along_x = derivative(jnp.stack([padded_stress[0], padded_stress[5], padded_stress[4]]), 1)
    along_y = derivative(jnp.stack([padded_stress[5], padded_stress[1], padded_stress[3]]), 2)
    along_z = derivative(jnp.stack([padded_stress[4], padded_stress[3], padded_stress[2]]), 3)
    return velocity + time_step * (along_x + along_y + along_z) / density[None]


def advance_stress(stress, padded_velocity, stiffness):
    grad_x = derivative(padded_velocity, 1)
    grad_y = derivative(padded_velocity, 2)
    grad_z = derivative(padded_velocity, 3)
    strain = [grad_x[0], grad_y[1], grad_z[2], grad_y[2] + grad_z[1], grad_x[2] + grad_z[0], grad_x[1] + grad_y[0]]
    updated = []
    for row_index in range(6):
        change = ordered_sum([stiffness[symmetric_index(row_index, col_index)] * strain[col_index] for col_index in range(6)])
        updated.append(stress[row_index] + time_step * change)
    return jnp.stack(updated)


def pad_field(field):
    return jnp.pad(field, ((0, 0), (4, 4), (4, 4), (4, 4)))


def reference(euler_table, crystal, orient, weight, cell_map, density, velocity, stress):
    table = rotated_table(euler_table, crystal)
    partitions = PART_X * PART_Y
    orient_all = orient.reshape(GRAINS, partitions, CELLS)
    weight_all = weight.reshape(GRAINS, partitions, CELLS)
    maps_all = cell_map.reshape(partitions, CELLS)

    def one_part(part_index):
        orient_rows = lax.dynamic_index_in_dim(orient_all, part_index, 1, keepdims=False)
        weight_rows = lax.dynamic_index_in_dim(weight_all, part_index, 1, keepdims=False)
        summed, total = accumulate(table, orient_rows, weight_rows)
        average = summed / total[None]
        slots = lax.dynamic_index_in_dim(maps_all, part_index, 0, keepdims=False)
        return jnp.zeros((21, CELLS), jnp.float32).at[:, slots].set(average)

    placed = lax.map(one_part, jnp.arange(partitions, dtype=jnp.int32))
    placed = placed.reshape(PART_X, PART_Y, 21, PART_X, SUB_X, PART_Y, SUB_Y, NZ)
    stiffness = placed.transpose(2, 3, 0, 4, 5, 1, 6, 7).reshape(21, NX, NY, NZ)
    for step_index in range(STEPS):
        velocity = advance_velocity(velocity, pad_field(stress), density)
        stress = advance_stress(stress, pad_field(velocity), stiffness)
    return (stiffness, velocity, stress)
```

```python
import functools

import jax
import jax.numpy as jnp
from jax import lax
from jax.experimental import pallas as pl
from jax.experimental.pallas import tpu as pltpu
from jax.sharding import PartitionSpec as P

STEPS = 2


stencil_weights = (0.8, -0.2, 4.0 / 105.0, -1.0 / 280.0)
time_step = 0.2
grain_block = 4
voigt_pairs = ((0, 0), (1, 1), (2, 2), (1, 2), (0, 2), (0, 1))
upper_pairs = [
    (row_index, col_index) for row_index in range(6) for col_index in range(row_index, 6)
]


def with_halo(cells, sides, width):
    for axis, dim in sides:
        count = lax.axis_size(axis)
        ends = count - 1
        head = lax.slice_in_dim(cells, 0, width, axis=dim)
        tail = lax.slice_in_dim(cells, cells.shape[dim] - width, cells.shape[dim], axis=dim)
        cells = jnp.concatenate(
            [
                lax.ppermute(tail, axis, [(i, (i + 1) % count) for i in range(ends)]),
                cells,
                lax.ppermute(head, axis, [((i + 1) % count, i) for i in range(ends)]),
            ],
            axis=dim,
        )
    return cells


def symmetric_index(first_index, second_index):
    return upper_pairs.index((min(first_index, second_index), max(first_index, second_index)))


def ordered_sum(summands):
    running = summands[0]
    for summand in summands[1:]:
        running = running + summand
    return running


def rotated_table(euler_table, crystal):
    cos_one, sin_one = (jnp.cos(euler_table[0]), jnp.sin(euler_table[0]))
    cos_mid, sin_mid = (jnp.cos(euler_table[1]), jnp.sin(euler_table[1]))
    cos_two, sin_two = (jnp.cos(euler_table[2]), jnp.sin(euler_table[2]))
    bunge = [
        [
            cos_one * cos_two - sin_one * sin_two * cos_mid,
            sin_one * cos_two + cos_one * sin_two * cos_mid,
            sin_two * sin_mid,
        ],
        [
            -cos_one * sin_two - sin_one * cos_two * cos_mid,
            -sin_one * sin_two + cos_one * cos_two * cos_mid,
            cos_two * sin_mid,
        ],
        [sin_one * sin_mid, -cos_one * sin_mid, cos_mid],
    ]
    rotation = [[bunge[col_index][row_index] for col_index in range(3)] for row_index in range(3)]
    bond = []
    for out_index in range(6):
        first, second = voigt_pairs[out_index]
        bond_row = []
        for in_index in range(6):
            third, fourth = voigt_pairs[in_index]
            if in_index < 3:
                bond_row.append(rotation[first][third] * rotation[second][third])
            else:
                bond_row.append(
                    rotation[first][third] * rotation[second][fourth]
                    + rotation[first][fourth] * rotation[second][third]
                )
        bond.append(bond_row)
    entries = [
        [crystal[symmetric_index(row_index, col_index)] for col_index in range(6)]
        for row_index in range(6)
    ]
    product = [
        [
            ordered_sum([bond[row_index][inner] * entries[inner][col_index] for inner in range(6)])
            for col_index in range(6)
        ]
        for row_index in range(6)
    ]
    rotated = [
        ordered_sum([product[row_index][inner] * bond[col_index][inner] for inner in range(6)])
        for row_index, col_index in upper_pairs
    ]
    return jnp.stack(rotated)


def accumulate(table, orient_rows, weight_rows):
    blocks = orient_rows.shape[0] // grain_block
    count_cells = orient_rows.shape[1]

    def absorb(carry, inputs):
        chosen, masses = inputs
        picked = jnp.take(table, chosen, axis=1)
        masses_wide = masses.astype(jnp.float32)
        return (
            (
                carry[0] + jnp.sum(picked * masses_wide[None], axis=1),
                carry[1] + jnp.sum(masses_wide, axis=0),
            ),
            None,
        )

    initial = (jnp.zeros((21, count_cells), jnp.float32), jnp.zeros((count_cells,), jnp.float32))
    result, unused = lax.scan(
        absorb,
        initial,
        (
            orient_rows.reshape(blocks, grain_block, count_cells),
            weight_rows.reshape(blocks, grain_block, count_cells),
        ),
    )
    return result


def derivative(padded, direction):
    interior = [padded.shape[0]] + [extent - 8 for extent in padded.shape[1:]]

    def window(offset):
        starts = [0, 4, 4, 4]
        starts[direction] = 4 + offset
        return lax.slice(
            padded, starts, [begin + extent for begin, extent in zip(starts, interior)]
        )

    result = stencil_weights[0] * (window(1) - window(-1))
    for order_index in range(1, 4):
        result = result + stencil_weights[order_index] * (
            window(order_index + 1) - window(-order_index - 1)
        )
    return result


def advance_velocity(velocity, padded_stress, density):
    along_x = derivative(jnp.stack([padded_stress[0], padded_stress[5], padded_stress[4]]), 1)
    along_y = derivative(jnp.stack([padded_stress[5], padded_stress[1], padded_stress[3]]), 2)
    along_z = derivative(jnp.stack([padded_stress[4], padded_stress[3], padded_stress[2]]), 3)
    return velocity + time_step * (along_x + along_y + along_z) / density[None]


def advance_stress(stress, padded_velocity, stiffness):
    grad_x = derivative(padded_velocity, 1)
    grad_y = derivative(padded_velocity, 2)
    grad_z = derivative(padded_velocity, 3)
    strain = [
        grad_x[0],
        grad_y[1],
        grad_z[2],
        grad_y[2] + grad_z[1],
        grad_x[2] + grad_z[0],
        grad_x[1] + grad_y[0],
    ]
    updated = []
    for row_index in range(6):
        change = ordered_sum(
            [
                stiffness[symmetric_index(row_index, col_index)] * strain[col_index]
                for col_index in range(6)
            ]
        )
        updated.append(stress[row_index] + time_step * change)
    return jnp.stack(updated)


def on_device_general(euler_table, crystal, orient, weight, cell_map, density, velocity, stress):
    part_x = lax.axis_size("gx")
    part_y = lax.axis_size("gy")
    layers = lax.axis_size("ga")
    brick_x, brick_y, brick_z = (stress.shape[1], stress.shape[2], stress.shape[3])
    sub_x = brick_x // part_x
    sub_y = brick_y // part_y
    depth = brick_z * layers
    grains = orient.shape[0]
    count_cells = orient.shape[3]
    table = rotated_table(euler_table, crystal)
    summed, total = accumulate(
        table, orient.reshape(grains, count_cells), weight.reshape(grains, count_cells)
    )
    slots = cell_map.reshape(count_cells)
    layer_pos = slots % depth
    remainder = slots // depth
    sub_y_pos = remainder % sub_y
    remainder = remainder // sub_y
    brick_y_pos = remainder % part_y
    remainder = remainder // part_y
    sub_x_pos = remainder % sub_x
    brick_x_pos = remainder // sub_x
    target = (
        ((brick_x_pos * part_y + brick_y_pos) * sub_x + sub_x_pos) * sub_y + sub_y_pos
    ) * depth + layer_pos
    placed = jnp.zeros((21, count_cells), jnp.float32).at[:, target].set(summed)
    counted = jnp.zeros((count_cells,), jnp.float32).at[target].set(total)
    placed = placed.reshape(21, part_x * part_y, sub_x, sub_y, depth)
    counted = counted.reshape(part_x * part_y, sub_x, sub_y, depth)
    placed, counted = (
        lax.psum_scatter(placed, "ga", scatter_dimension=4, tiled=True),
        lax.psum_scatter(counted, "ga", scatter_dimension=3, tiled=True),
    )
    averaged = placed / counted[None]
    moved = lax.all_to_all(averaged, ("gx", "gy"), split_axis=1, concat_axis=1, tiled=True)
    moved = moved.reshape(21, part_x, part_y, sub_x, sub_y, brick_z)
    stiffness = moved.transpose(0, 1, 3, 2, 4, 5).reshape(21, brick_x, brick_y, brick_z)
    for step_index in range(STEPS):
        padded_stress = with_halo(stress, (("gx", 1), ("gy", 2), ("ga", 3)), 4)
        velocity = advance_velocity(velocity, padded_stress, density)
        padded_velocity = with_halo(velocity, (("gx", 1), ("gy", 2), ("ga", 3)), 4)
        stress = advance_stress(stress, padded_velocity, stiffness)
    return (stiffness, velocity, stress)


SUB = 8
LANES = 128
BLOCK_ROWS = 32
FIELDS = 10
LOW_ROWS = tuple(range(8)) + (16, 17, 18)
HIGH_ROWS = tuple(range(8, 16)) + (19, 20, 21)


def fits_plane(part_x, part_y, layers, orient, stress, euler_table):
    brick_x, brick_y, brick_z = stress.shape[1:]
    return (
        part_x % 2 == 0
        and part_y == 2
        and layers == 2
        and brick_x == SUB
        and part_x == SUB
        and brick_y == 4
        and brick_z == 8
        and orient.shape[3] == part_x * 64
        and orient.shape[0] % 8 == 0
        and euler_table.shape[1] % LANES == 0
    )


def lanes_of(shape):
    return lax.broadcasted_iota(jnp.int32, shape, len(shape) - 1)


def rows_of(shape):
    return lax.broadcasted_iota(jnp.int32, shape, len(shape) - 2)


def bond_matrix(trig):
    cos_one, cos_mid, cos_two, sin_one, sin_mid, sin_two = trig
    cos_two_mid = cos_two * cos_mid
    sin_two_mid = sin_two * cos_mid
    bunge = [
        [
            cos_one * cos_two - sin_one * sin_two_mid,
            sin_one * cos_two + cos_one * sin_two_mid,
            sin_two * sin_mid,
        ],
        [
            -cos_one * sin_two - sin_one * cos_two_mid,
            -sin_one * sin_two + cos_one * cos_two_mid,
            cos_two * sin_mid,
        ],
        [sin_one * sin_mid, -cos_one * sin_mid, cos_mid],
    ]
    rotation = [[bunge[col][row] for col in range(3)] for row in range(3)]
    bond = []
    for first, second in voigt_pairs:
        row = []
        for in_index, (third, fourth) in enumerate(voigt_pairs):
            if in_index < 3:
                row.append(rotation[first][third] * rotation[second][third])
            else:
                row.append(
                    rotation[first][third] * rotation[second][fourth]
                    + rotation[first][fourth] * rotation[second][third]
                )
        bond.append(row)
    return bond


def grain_kernel(
    crystal_ref,
    euler_ref,
    orient_ref,
    weight_ref,
    map_ref,
    density_ref,
    velocity_ref,
    stress_ref,
    send_ref,
    trig_ref,
    picked_ref,
    sums_ref,
    place_ref,
    acc_ref,
):
    row_part = lax.axis_index("gy")
    layer = lax.axis_index("ga")
    grains = weight_ref.shape[0]
    cells = weight_ref.shape[1]
    tiles = cells // LANES
    octets = grains // SUB
    table_tiles = euler_ref.shape[1] // LANES
    destinations = send_ref.shape[0]

    angles = euler_ref[...]
    trig_ref[0:3, :] = jnp.cos(angles)
    trig_ref[3:6, :] = jnp.sin(angles)
    groups = [(octet, tile) for tile in range(tiles) for octet in range(octets)]
    low, high = [], []
    for octet, tile in groups:
        index = orient_ref[pl.ds(octet * SUB * tiles + tile, SUB, stride=tiles), :]
        low.append(index & (LANES - 1))
        high.append(index >> 7)
    for which in range(6):
        values = [None] * len(groups)
        for tile in range(table_tiles):
            source = jnp.broadcast_to(
                trig_ref[which : which + 1, tile * LANES : (tile + 1) * LANES], (SUB, LANES)
            )
            for at in range(len(groups)):
                found = jnp.take_along_axis(source, low[at], axis=1, mode="promise_in_bounds")
                values[at] = found if tile == 0 else jnp.where(high[at] == tile, found, values[at])
        for at in range(len(groups)):
            picked_ref[which * len(groups) + at] = values[at]

    sums_ref[...] = jnp.zeros_like(sums_ref)
    entries = [
        [crystal_ref[symmetric_index(row, col)] for col in range(6)] for row in range(6)
    ]
    row_of = {}
    for k in range(len(LOW_ROWS)):
        row_of[LOW_ROWS[k]] = k
        row_of[HIGH_ROWS[k]] = 16 + k

    def one_tile(tile, unused):
        for octet in range(octets):
            at = tile * octets + octet
            bond = bond_matrix([picked_ref[which * len(groups) + at] for which in range(6)])
            mass = weight_ref[
                octet * SUB : (octet + 1) * SUB, pl.ds(pl.multiple_of(tile * LANES, LANES), LANES)
            ].astype(jnp.float32)
            pair = 0
            for row in range(6):
                product = [
                    ordered_sum([bond[row][inner] * entries[inner][col] for inner in range(6)])
                    * mass
                    for col in range(6)
                ]
                for col in range(row, 6):
                    value = ordered_sum([product[inner] * bond[col][inner] for inner in range(6)])
                    acc_ref[pair] = value if octet == 0 else acc_ref[pair] + value
                    pair += 1
            acc_ref[21] = mass if octet == 0 else acc_ref[21] + mass
        for pair in range(22):
            sums_ref[
                row_of[pair] : row_of[pair] + 1, pl.ds(pl.multiple_of(tile * LANES, LANES), LANES)
            ] = jnp.sum(acc_ref[pair], axis=0, keepdims=True)
        return unused

    lax.fori_loop(0, tiles, one_tile, 0)

    slots = map_ref[...]
    half = cells // (cells // 32)
    place_ref[...] = jnp.zeros_like(place_ref)
    for chunk in range(cells // half):
        wanted = rows_of((half, cells)) + chunk * half
        hit = jnp.where(jnp.broadcast_to(slots, (half, cells)) == wanted, 1.0, 0.0)
        start = pl.multiple_of(chunk * 2 * half + row_part * half, half)
        place_ref[pl.ds(start, half), :] = hit.astype(jnp.bfloat16)
    sums = sums_ref[...]
    part_one = sums.astype(jnp.bfloat16)
    rest = sums - part_one.astype(jnp.float32)
    part_two = rest.astype(jnp.bfloat16)
    part_three = (rest - part_two.astype(jnp.float32)).astype(jnp.bfloat16)
    parts = jnp.concatenate([part_one, part_two, part_three], axis=0)
    placed = lax.dot_general(
        parts, place_ref[...], (((1,), (1,)), ((), ())), preferred_element_type=jnp.float32
    )
    placed = placed[0:32] + placed[32:64] + placed[64:96]

    own = row_part * 2 + layer
    lane = lanes_of((SUB, LANES))
    row = rows_of((SUB, LANES))

    def field_rows(component, y):
        if component < 6:
            return stress_ref[pl.ds(component * 32 + y, SUB, stride=4), :]
        if component < 9:
            return velocity_ref[pl.ds((component - 6) * 32 + y, SUB, stride=4), :]
        return density_ref[pl.ds(y, SUB, stride=4), :]

    def spread(component, slot, into):
        goal = own ^ slot
        for y in range(4):
            start = (goal // 2) * 64 + y * 16 + (goal % 2) * 8
            narrow = jnp.concatenate(
                [field_rows(component, y), jnp.zeros((SUB, LANES - 8), jnp.float32)], axis=1
            )
            into = into + pltpu.roll(narrow, start, 1)
        return into

    nothing = jnp.zeros((SUB, LANES), jnp.float32)
    group_one, group_two, tail_low, tail_high = nothing, nothing, nothing, nothing
    for slot in range(4):
        group_one = spread(slot, slot, group_one)
        group_two = spread(4 + slot, slot, group_two)
    tail_low = spread(9, 2, spread(8, 0, tail_low))
    tail_high = spread(9, 3, spread(8, 1, tail_high))
    tail = pltpu.roll(tail_low, 4, 0) + tail_high

    shift = 32 + row_part * 64
    for brick in range(destinations // 4):
        low_half = placed[0:16, brick * LANES : (brick + 1) * LANES]
        high_half = placed[16:32, brick * LANES : (brick + 1) * LANES]
        packed = low_half + pltpu.roll(high_half, shift, 1)
        last = jnp.where(row < 4, packed[8:16], tail)
        for inner in range(4):
            at = brick * 4 + inner
            send_ref[at, 0:8, :] = packed[0:8]
            send_ref[at, 8:16, :] = last
            send_ref[at, 16:24, :] = group_one
            send_ref[at, 24:32, :] = group_two


def plane_derivative(field, dim, lane):
    position = lane // 16 if dim == 1 else lane % 16
    extent = 8 if dim == 1 else 16
    unit = 16 if dim == 1 else 1
    total = None
    for order in range(1, 5):
        ahead = pltpu.roll(field, LANES - order * unit, 1)
        behind = pltpu.roll(field, order * unit, 1)
        term = stencil_weights[order - 1] * (
            jnp.where(position + order < extent, ahead, 0.0)
            - jnp.where(position - order >= 0, behind, 0.0)
        )
        total = term if total is None else total + term
    return total


def row_derivative(read, start, count):
    total = stencil_weights[0] * (read(start + 1, count) - read(start - 1, count))
    for order in range(2, 5):
        total = total + stencil_weights[order - 1] * (
            read(start + order, count) - read(start - order, count)
        )
    return total


def velocity_update(wide_stress, old_velocity, density, inside):
    count = 16
    lane = lanes_of((count, LANES))

    def along(component, dim):
        if dim == 0:
            return row_derivative(
                lambda at, size: wide_stress[component, at : at + size, :], 4, count
            )
        return plane_derivative(wide_stress[component, 4 : 4 + count, :], dim, lane)

    sums = [
        along(0, 0) + along(5, 1) + along(4, 2),
        along(5, 0) + along(1, 1) + along(3, 2),
        along(4, 0) + along(3, 1) + along(2, 2),
    ]
    return [
        jnp.where(inside, old_velocity[at] + time_step * sums[at] / density, 0.0)
        for at in range(3)
    ]


def stress_update(wide_velocity, old_stress, stiff):
    lane = lanes_of((SUB, LANES))

    def along(component, dim):
        if dim == 0:
            return row_derivative(
                lambda at, size: wide_velocity[component, at : at + size, :], 4, SUB
            )
        return plane_derivative(wide_velocity[component, 4 : 4 + SUB, :], dim, lane)

    strain = [
        along(0, 0),
        along(1, 1),
        along(2, 2),
        along(2, 1) + along(1, 2),
        along(2, 0) + along(0, 2),
        along(1, 0) + along(0, 1),
    ]
    return [
        old_stress[row]
        + time_step
        * ordered_sum([stiff(symmetric_index(row, col)) * strain[col] for col in range(6)])
        for row in range(6)
    ]


def inside_rows(brick, bricks):
    place = rows_of((16, LANES)) - 4
    return ((brick > 0) | (place >= 0)) & ((brick < bricks - 1) | (place < SUB))


def first_step_kernel(
    got_ref, stiff_ref, stress_ref, velocity_ref, density_ref, wide_ref, moving_ref
):
    brick = lax.axis_index("gx")
    bricks = got_ref.shape[0] // 4
    lane = lanes_of((SUB, LANES))
    row = rows_of((SUB, LANES))

    lane_two = lanes_of((16, LANES))
    own_slot = (lane_two // 32) % 2 == 0
    for p in range(bricks):
        zero = got_ref[p * 4, 0:16, :] + got_ref[p * 4 + 1, 0:16, :]
        one = got_ref[p * 4 + 2, 0:16, :] + got_ref[p * 4 + 3, 0:16, :]
        low = jnp.where(own_slot, zero, one)
        high = jnp.where(own_slot, one, zero)
        high = jnp.where(own_slot, pltpu.roll(high, LANES - 32, 1), pltpu.roll(high, 32, 1))
        total = jnp.broadcast_to(high[10:11], (SUB, LANES))
        stiff_ref[p * 24 : p * 24 + 8, :] = low[0:8] / total
        stiff_ref[p * 24 + 8 : p * 24 + 16, :] = high[0:8] / total
        last = jnp.where(row < 3, low[8:16], pltpu.roll(high[8:16], 3, 0))
        stiff_ref[p * 24 + 16 : p * 24 + 24, :] = last / total

    kind = (lane // 64) * 2 + (lane // 8) % 2

    def settle(value, slot):
        if slot & 1:
            value = jnp.where(
                (lane // 8) % 2 == 0,
                pltpu.roll(value, LANES - 8, 1),
                pltpu.roll(value, 8, 1),
            )
        if slot & 2:
            value = pltpu.roll(value, 64, 1)
        return value

    for side in range(3):
        source = jnp.clip(brick + side - 1, 0, bricks - 1)
        valid = source == brick + side - 1

        def collect(rows, slot):
            pieces = [got_ref[source * 4 + (q ^ slot), rows : rows + 8, :] for q in range(4)]
            value = jnp.where(
                kind < 2,
                jnp.where(kind == 0, pieces[0], pieces[1]),
                jnp.where(kind == 2, pieces[2], pieces[3]),
            )
            return settle(value, slot)

        def keep(component, value):
            value = jnp.where(valid, value, 1.0 if component == 9 else 0.0)
            wide_ref[component, side * SUB : (side + 1) * SUB, :] = value

        for slot in range(4):
            keep(slot, collect(16, slot))
            keep(4 + slot, collect(24, slot))
        for component in (8, 9):
            slot = (component - 8) * 2
            upper = pltpu.roll(collect(8, slot), 4, 0)
            keep(component, jnp.where(row < 4, upper, collect(8, slot + 1)))

    density = wide_ref[9, 4:20, :]
    density_ref[...] = density
    fresh = velocity_update(
        wide_ref,
        [wide_ref[6 + at, 4:20, :] for at in range(3)],
        density,
        inside_rows(brick, bricks),
    )
    for at in range(3):
        velocity_ref[at] = fresh[at]
        moving_ref[at] = fresh[at]
    fresh = stress_update(
        moving_ref,
        [wide_ref[at, 8:16, :] for at in range(6)],
        lambda pair: stiff_ref[pl.ds(pair, SUB, stride=24), :],
    )
    for at in range(6):
        stress_ref[at] = fresh[at]


def stiffness_kernel(stiff_ref, out_ref, turned_ref):
    own = lax.axis_index("gy") * 64 + lax.axis_index("ga") * 8
    for p in range(SUB):
        turned_ref[...] = jnp.transpose(stiff_ref[p * 24 : (p + 1) * 24, :])
        for y in range(4):
            rows = pl.ds(pl.multiple_of(own + y * 16, 8), 8)
            out_ref[p * 32 + y * 8 : p * 32 + y * 8 + 8, :] = turned_ref[rows, 0:21]


def last_step_kernel(
    stress_ref,
    pair_ref,
    cross_ref,
    velocity_ref,
    density_ref,
    stiff_ref,
    out_velocity_ref,
    out_stress_ref,
    wide_ref,
    moving_ref,
    *,
    bricks,
):
    brick = lax.axis_index("gx")
    even = brick % 2 == 0
    for at in range(6):
        pair, cross = pair_ref[at], cross_ref[at]
        wide_ref[at, 0:8, :] = jnp.where(even, cross, pair)
        wide_ref[at, 8:16, :] = stress_ref[at]
        wide_ref[at, 16:24, :] = jnp.where(even, pair, cross)
    velocity = velocity_update(
        wide_ref,
        [velocity_ref[at] for at in range(3)],
        density_ref[...],
        inside_rows(brick, bricks),
    )
    for at in range(3):
        moving_ref[at] = velocity[at]
    stress = stress_update(
        moving_ref,
        [stress_ref[at] for at in range(6)],
        lambda pair: stiff_ref[pl.ds(pair, SUB, stride=24), :],
    )
    own = lax.axis_index("gy") * 64 + lax.axis_index("ga") * 8

    def put(out_ref, at, value):
        for y in range(4):
            turned = pltpu.roll(value, (LANES - own - y * 16) % LANES, 1)
            out_ref[pl.ds(at * 32 + y, SUB, stride=4), :] = turned[:, 0:8]

    for at in range(3):
        put(out_velocity_ref, at, moving_ref[at, 4:12, :])
    for at in range(6):
        put(out_stress_ref, at, stress[at])


def on_plane(euler_table, crystal, orient, weight, cell_map, density, velocity, stress):
    part_x = lax.axis_size("gx")
    devices = part_x * lax.axis_size("gy") * lax.axis_size("ga")
    grains, cells = orient.shape[0], orient.shape[3]
    tiles = cells // LANES
    octets = grains // SUB
    vmem = pl.BlockSpec(memory_space=pltpu.VMEM)
    smem = pl.BlockSpec(memory_space=pltpu.SMEM)
    f32 = jnp.float32

    send = pl.pallas_call(
        grain_kernel,
        out_shape=jax.ShapeDtypeStruct((devices, BLOCK_ROWS, LANES), f32),
        in_specs=[smem] + [vmem] * 7,
        out_specs=vmem,
        scratch_shapes=[
            pltpu.VMEM((SUB, euler_table.shape[1]), f32),
            pltpu.VMEM((6 * tiles * octets, SUB, LANES), f32),
            pltpu.VMEM((32, cells), f32),
            pltpu.VMEM((2 * cells, cells), jnp.bfloat16),
            pltpu.VMEM((22, SUB, LANES), f32),
        ],
    )(
        crystal,
        euler_table,
        orient.reshape(grains * tiles, LANES),
        weight.reshape(grains, cells),
        cell_map.reshape(1, cells),
        density.reshape(SUB * 4, 8),
        velocity.reshape(3 * SUB * 4, 8),
        stress.reshape(6 * SUB * 4, 8),
    )
    got = lax.all_to_all(send, ("gx", "gy", "ga"), split_axis=0, concat_axis=0, tiled=True)
    stiff, middle_stress, middle_velocity, wide_density = pl.pallas_call(
        first_step_kernel,
        out_shape=(
            jax.ShapeDtypeStruct((part_x * 24, LANES), f32),
            jax.ShapeDtypeStruct((6, SUB, LANES), f32),
            jax.ShapeDtypeStruct((3, 16, LANES), f32),
            jax.ShapeDtypeStruct((16, LANES), f32),
        ),
        in_specs=[vmem],
        out_specs=(vmem,) * 4,
        scratch_shapes=[
            pltpu.VMEM((FIELDS, 24, LANES), f32),
            pltpu.VMEM((3, 16, LANES), f32),
        ],
    )(got)
    pair = lax.ppermute(middle_stress, "gx", [(i, i ^ 1) for i in range(part_x)])
    swaps = [(i, i + 1) for i in range(1, part_x - 1, 2)]
    cross = lax.ppermute(middle_stress, "gx", swaps + [(b, a) for a, b in swaps])
    stiffness = pl.pallas_call(
        stiffness_kernel,
        out_shape=jax.ShapeDtypeStruct((SUB * 4 * 8, 21), f32),
        in_specs=[vmem],
        out_specs=vmem,
        scratch_shapes=[pltpu.VMEM((LANES, 24), f32)],
        cost_estimate=pl.CostEstimate(flops=100000, bytes_accessed=200000, transcendentals=0),
    )(stiff)
    new_velocity, new_stress = pl.pallas_call(
        functools.partial(last_step_kernel, bricks=part_x),
        out_shape=(
            jax.ShapeDtypeStruct((3 * SUB * 4, 8), f32),
            jax.ShapeDtypeStruct((6 * SUB * 4, 8), f32),
        ),
        in_specs=[vmem] * 6,
        out_specs=(vmem,) * 2,
        scratch_shapes=[
            pltpu.VMEM((6, 24, LANES), f32),
            pltpu.VMEM((3, 16, LANES), f32),
        ],
    )(middle_stress, pair, cross, middle_velocity, wide_density, stiff)
    return (
        stiffness.reshape(SUB, 4, 8, 21).transpose(3, 0, 1, 2),
        new_velocity.reshape(3, SUB, 4, 8),
        new_stress.reshape(6, SUB, 4, 8),
    )


def on_device(euler_table, crystal, orient, weight, cell_map, density, velocity, stress):
    sizes = (lax.axis_size("gx"), lax.axis_size("gy"), lax.axis_size("ga"))
    form = on_plane if fits_plane(*sizes, orient, stress, euler_table) else on_device_general
    return form(euler_table, crystal, orient, weight, cell_map, density, velocity, stress)


def solution(mesh):
    return jax.shard_map(
        on_device,
        mesh=mesh,
        in_specs=(
            P(),
            P(),
            P("ga", "gx", "gy", None),
            P("ga", "gx", "gy", None),
            P("gx", "gy", None),
            P("gx", "gy", "ga"),
            P(None, "gx", "gy", "ga"),
            P(None, "gx", "gy", "ga"),
        ),
        out_specs=(P(None, "gx", "gy", "ga"), P(None, "gx", "gy", "ga"), P(None, "gx", "gy", "ga")),
        check_vma=False,
    )
```

```python
import functools

import jax
import jax.numpy as jnp
from jax import lax
from jax.experimental import pallas as pl
from jax.experimental.pallas import tpu as pltpu
from jax.sharding import PartitionSpec as P

STEPS = 2


stencil_weights = (0.8, -0.2, 4.0 / 105.0, -1.0 / 280.0)
time_step = 0.2
grain_block = 4
voigt_pairs = ((0, 0), (1, 1), (2, 2), (1, 2), (0, 2), (0, 1))
upper_pairs = [
    (row_index, col_index) for row_index in range(6) for col_index in range(row_index, 6)
]


def with_halo(cells, sides, width):
    for axis, dim in sides:
        count = lax.axis_size(axis)
        ends = count - 1
        head = lax.slice_in_dim(cells, 0, width, axis=dim)
        tail = lax.slice_in_dim(cells, cells.shape[dim] - width, cells.shape[dim], axis=dim)
        cells = jnp.concatenate(
            [
                lax.ppermute(tail, axis, [(i, (i + 1) % count) for i in range(ends)]),
                cells,
                lax.ppermute(head, axis, [((i + 1) % count, i) for i in range(ends)]),
            ],
            axis=dim,
        )
    return cells


def symmetric_index(first_index, second_index):
    return upper_pairs.index((min(first_index, second_index), max(first_index, second_index)))


def ordered_sum(summands):
    running = summands[0]
    for summand in summands[1:]:
        running = running + summand
    return running


def rotated_table(euler_table, crystal):
    cos_one, sin_one = (jnp.cos(euler_table[0]), jnp.sin(euler_table[0]))
    cos_mid, sin_mid = (jnp.cos(euler_table[1]), jnp.sin(euler_table[1]))
    cos_two, sin_two = (jnp.cos(euler_table[2]), jnp.sin(euler_table[2]))
    bunge = [
        [
            cos_one * cos_two - sin_one * sin_two * cos_mid,
            sin_one * cos_two + cos_one * sin_two * cos_mid,
            sin_two * sin_mid,
        ],
        [
            -cos_one * sin_two - sin_one * cos_two * cos_mid,
            -sin_one * sin_two + cos_one * cos_two * cos_mid,
            cos_two * sin_mid,
        ],
        [sin_one * sin_mid, -cos_one * sin_mid, cos_mid],
    ]
    rotation = [[bunge[col_index][row_index] for col_index in range(3)] for row_index in range(3)]
    bond = []
    for out_index in range(6):
        first, second = voigt_pairs[out_index]
        bond_row = []
        for in_index in range(6):
            third, fourth = voigt_pairs[in_index]
            if in_index < 3:
                bond_row.append(rotation[first][third] * rotation[second][third])
            else:
                bond_row.append(
                    rotation[first][third] * rotation[second][fourth]
                    + rotation[first][fourth] * rotation[second][third]
                )
        bond.append(bond_row)
    entries = [
        [crystal[symmetric_index(row_index, col_index)] for col_index in range(6)]
        for row_index in range(6)
    ]
    product = [
        [
            ordered_sum([bond[row_index][inner] * entries[inner][col_index] for inner in range(6)])
            for col_index in range(6)
        ]
        for row_index in range(6)
    ]
    rotated = [
        ordered_sum([product[row_index][inner] * bond[col_index][inner] for inner in range(6)])
        for row_index, col_index in upper_pairs
    ]
    return jnp.stack(rotated)


def accumulate(table, orient_rows, weight_rows):
    blocks = orient_rows.shape[0] // grain_block
    count_cells = orient_rows.shape[1]

    def absorb(carry, inputs):
        chosen, masses = inputs
        picked = jnp.take(table, chosen, axis=1)
        masses_wide = masses.astype(jnp.float32)
        return (
            (
                carry[0] + jnp.sum(picked * masses_wide[None], axis=1),
                carry[1] + jnp.sum(masses_wide, axis=0),
            ),
            None,
        )

    initial = (jnp.zeros((21, count_cells), jnp.float32), jnp.zeros((count_cells,), jnp.float32))
    result, unused = lax.scan(
        absorb,
        initial,
        (
            orient_rows.reshape(blocks, grain_block, count_cells),
            weight_rows.reshape(blocks, grain_block, count_cells),
        ),
    )
    return result


def derivative(padded, direction):
    interior = [padded.shape[0]] + [extent - 8 for extent in padded.shape[1:]]

    def window(offset):
        starts = [0, 4, 4, 4]
        starts[direction] = 4 + offset
        return lax.slice(
            padded, starts, [begin + extent for begin, extent in zip(starts, interior)]
        )

    result = stencil_weights[0] * (window(1) - window(-1))
    for order_index in range(1, 4):
        result = result + stencil_weights[order_index] * (
            window(order_index + 1) - window(-order_index - 1)
        )
    return result


def advance_velocity(velocity, padded_stress, density):
    along_x = derivative(jnp.stack([padded_stress[0], padded_stress[5], padded_stress[4]]), 1)
    along_y = derivative(jnp.stack([padded_stress[5], padded_stress[1], padded_stress[3]]), 2)
    along_z = derivative(jnp.stack([padded_stress[4], padded_stress[3], padded_stress[2]]), 3)
    return velocity + time_step * (along_x + along_y + along_z) / density[None]


def advance_stress(stress, padded_velocity, stiffness):
    grad_x = derivative(padded_velocity, 1)
    grad_y = derivative(padded_velocity, 2)
    grad_z = derivative(padded_velocity, 3)
    strain = [
        grad_x[0],
        grad_y[1],
        grad_z[2],
        grad_y[2] + grad_z[1],
        grad_x[2] + grad_z[0],
        grad_x[1] + grad_y[0],
    ]
    updated = []
    for row_index in range(6):
        change = ordered_sum(
            [
                stiffness[symmetric_index(row_index, col_index)] * strain[col_index]
                for col_index in range(6)
            ]
        )
        updated.append(stress[row_index] + time_step * change)
    return jnp.stack(updated)


def on_device_general(euler_table, crystal, orient, weight, cell_map, density, velocity, stress):
    part_x = lax.axis_size("gx")
    part_y = lax.axis_size("gy")
    layers = lax.axis_size("ga")
    brick_x, brick_y, brick_z = (stress.shape[1], stress.shape[2], stress.shape[3])
    sub_x = brick_x // part_x
    sub_y = brick_y // part_y
    depth = brick_z * layers
    grains = orient.shape[0]
    count_cells = orient.shape[3]
    table = rotated_table(euler_table, crystal)
    summed, total = accumulate(
        table, orient.reshape(grains, count_cells), weight.reshape(grains, count_cells)
    )
    slots = cell_map.reshape(count_cells)
    layer_pos = slots % depth
    remainder = slots // depth
    sub_y_pos = remainder % sub_y
    remainder = remainder // sub_y
    brick_y_pos = remainder % part_y
    remainder = remainder // part_y
    sub_x_pos = remainder % sub_x
    brick_x_pos = remainder // sub_x
    target = (
        ((brick_x_pos * part_y + brick_y_pos) * sub_x + sub_x_pos) * sub_y + sub_y_pos
    ) * depth + layer_pos
    placed = jnp.zeros((21, count_cells), jnp.float32).at[:, target].set(summed)
    counted = jnp.zeros((count_cells,), jnp.float32).at[target].set(total)
    placed = placed.reshape(21, part_x * part_y, sub_x, sub_y, depth)
    counted = counted.reshape(part_x * part_y, sub_x, sub_y, depth)
    placed, counted = (
        lax.psum_scatter(placed, "ga", scatter_dimension=4, tiled=True),
        lax.psum_scatter(counted, "ga", scatter_dimension=3, tiled=True),
    )
    averaged = placed / counted[None]
    moved = lax.all_to_all(averaged, ("gx", "gy"), split_axis=1, concat_axis=1, tiled=True)
    moved = moved.reshape(21, part_x, part_y, sub_x, sub_y, brick_z)
    stiffness = moved.transpose(0, 1, 3, 2, 4, 5).reshape(21, brick_x, brick_y, brick_z)
    for step_index in range(STEPS):
        padded_stress = with_halo(stress, (("gx", 1), ("gy", 2), ("ga", 3)), 4)
        velocity = advance_velocity(velocity, padded_stress, density)
        padded_velocity = with_halo(velocity, (("gx", 1), ("gy", 2), ("ga", 3)), 4)
        stress = advance_stress(stress, padded_velocity, stiffness)
    return (stiffness, velocity, stress)


SUB = 8
LANES = 128
BLOCK_ROWS = 32
FIELDS = 10
LOW_ROWS = tuple(range(8)) + (16, 17, 18)
HIGH_ROWS = tuple(range(8, 16)) + (19, 20, 21)


def fits_plane(part_x, part_y, layers, orient, stress, euler_table):
    brick_x, brick_y, brick_z = stress.shape[1:]
    return (
        part_x % 2 == 0
        and part_y == 2
        and layers == 2
        and brick_x == SUB
        and part_x == SUB
        and brick_y == 4
        and brick_z == 8
        and orient.shape[3] == part_x * 64
        and orient.shape[0] % 8 == 0
        and euler_table.shape[1] % LANES == 0
    )


def lanes_of(shape):
    return lax.broadcasted_iota(jnp.int32, shape, len(shape) - 1)


def rows_of(shape):
    return lax.broadcasted_iota(jnp.int32, shape, len(shape) - 2)


def bond_matrix(trig):
    cos_one, cos_mid, cos_two, sin_one, sin_mid, sin_two = trig
    cos_two_mid = cos_two * cos_mid
    sin_two_mid = sin_two * cos_mid
    bunge = [
        [
            cos_one * cos_two - sin_one * sin_two_mid,
            sin_one * cos_two + cos_one * sin_two_mid,
            sin_two * sin_mid,
        ],
        [
            -cos_one * sin_two - sin_one * cos_two_mid,
            -sin_one * sin_two + cos_one * cos_two_mid,
            cos_two * sin_mid,
        ],
        [sin_one * sin_mid, -cos_one * sin_mid, cos_mid],
    ]
    rotation = [[bunge[col][row] for col in range(3)] for row in range(3)]
    bond = []
    for first, second in voigt_pairs:
        row = []
        for in_index, (third, fourth) in enumerate(voigt_pairs):
            if in_index < 3:
                row.append(rotation[first][third] * rotation[second][third])
            else:
                row.append(
                    rotation[first][third] * rotation[second][fourth]
                    + rotation[first][fourth] * rotation[second][third]
                )
        bond.append(row)
    return bond


def grain_kernel(
    crystal_hbm,
    euler_hbm,
    orient_hbm,
    weight_hbm,
    map_hbm,
    density_hbm,
    velocity_hbm,
    stress_hbm,
    send_ref,
    crystal_ref,
    euler_ref,
    orient_ref,
    weight_ref,
    map_ref,
    density_ref,
    velocity_ref,
    stress_ref,
    trig_ref,
    sums_ref,
    place_ref,
    acc_ref,
    arrived,
):
    row_part = lax.axis_index("gy")
    layer = lax.axis_index("ga")
    grains = weight_ref.shape[0]
    cells = weight_ref.shape[1]
    tiles = cells // LANES
    octets = grains // SUB
    table_tiles = euler_ref.shape[1] // LANES
    destinations = send_ref.shape[0]

    copies = [
        pltpu.make_async_copy(source, target, arrived.at[at])
        for at, (source, target) in enumerate(
            [
                (euler_hbm, euler_ref),
                (orient_hbm, orient_ref),
                (weight_hbm, weight_ref),
                (crystal_hbm, crystal_ref),
                (map_hbm, map_ref),
                (stress_hbm, stress_ref),
                (velocity_hbm, velocity_ref),
                (density_hbm, density_ref),
            ]
        )
    ]
    for copy in copies:
        copy.start()
    sums_ref[...] = jnp.zeros_like(sums_ref)
    place_ref[...] = jnp.zeros_like(place_ref)

    copies[0].wait()
    angles = euler_ref[...]
    trig_ref[0:3, :] = jnp.cos(angles)
    trig_ref[3:6, :] = jnp.sin(angles)

    for copy in copies[1:4]:
        copy.wait()
    entries = [
        [crystal_ref[symmetric_index(row, col)] for col in range(6)] for row in range(6)
    ]
    row_of = {}
    for k in range(len(LOW_ROWS)):
        row_of[LOW_ROWS[k]] = k
        row_of[HIGH_ROWS[k]] = 16 + k

    def pick(tile, octet):
        index = orient_ref[pl.ds(octet * SUB * tiles + tile, SUB, stride=tiles), :]
        low, high = index & (LANES - 1), index >> 7
        values = [None] * 6
        for table_tile in range(table_tiles):
            here = high == table_tile
            for which in range(6):
                source = jnp.broadcast_to(
                    trig_ref[
                        which : which + 1, table_tile * LANES : (table_tile + 1) * LANES
                    ],
                    (SUB, LANES),
                )
                found = jnp.take_along_axis(source, low, axis=1, mode="promise_in_bounds")
                values[which] = found if table_tile == 0 else jnp.where(here, found, values[which])
        return values

    def one_tile(tile, unused):
        for octet in range(octets):
            bond = bond_matrix(pick(tile, octet))
            mass = weight_ref[
                octet * SUB : (octet + 1) * SUB, pl.ds(pl.multiple_of(tile * LANES, LANES), LANES)
            ].astype(jnp.float32)
            pair = 0
            for row in range(6):
                product = [
                    ordered_sum([bond[row][inner] * entries[inner][col] for inner in range(6)])
                    * mass
                    for col in range(6)
                ]
                for col in range(row, 6):
                    value = ordered_sum([product[inner] * bond[col][inner] for inner in range(6)])
                    acc_ref[pair] = value if octet == 0 else acc_ref[pair] + value
                    pair += 1
            acc_ref[21] = mass if octet == 0 else acc_ref[21] + mass
        for pair in range(22):
            sums_ref[
                row_of[pair] : row_of[pair] + 1, pl.ds(pl.multiple_of(tile * LANES, LANES), LANES)
            ] = jnp.sum(acc_ref[pair], axis=0, keepdims=True)
        return unused

    lax.fori_loop(0, tiles, one_tile, 0)
    for copy in copies[4:]:
        copy.wait()

    slots = map_ref[...]
    half = cells // (cells // 32)
    for chunk in range(cells // half):
        wanted = rows_of((half, cells)) + chunk * half
        hit = jnp.where(jnp.broadcast_to(slots, (half, cells)) == wanted, 1.0, 0.0)
        start = pl.multiple_of(chunk * 2 * half + row_part * half, half)
        place_ref[pl.ds(start, half), :] = hit.astype(jnp.bfloat16)
    sums = sums_ref[...]
    part_one = sums.astype(jnp.bfloat16)
    rest = sums - part_one.astype(jnp.float32)
    part_two = rest.astype(jnp.bfloat16)
    part_three = (rest - part_two.astype(jnp.float32)).astype(jnp.bfloat16)
    parts = jnp.concatenate([part_one, part_two, part_three], axis=0)
    placed = lax.dot_general(
        parts, place_ref[...], (((1,), (1,)), ((), ())), preferred_element_type=jnp.float32
    )
    placed = placed[0:32] + placed[32:64] + placed[64:96]

    own = row_part * 2 + layer
    lane = lanes_of((SUB, LANES))
    row = rows_of((SUB, LANES))

    def field_rows(component, y):
        if component < 6:
            return stress_ref[pl.ds(component * 32 + y, SUB, stride=4), :]
        if component < 9:
            return velocity_ref[pl.ds((component - 6) * 32 + y, SUB, stride=4), :]
        return density_ref[pl.ds(y, SUB, stride=4), :]

    def spread(component, slot, into):
        goal = own ^ slot
        for y in range(4):
            start = (goal // 2) * 64 + y * 16 + (goal % 2) * 8
            narrow = jnp.concatenate(
                [field_rows(component, y), jnp.zeros((SUB, LANES - 8), jnp.float32)], axis=1
            )
            into = into + pltpu.roll(narrow, start, 1)
        return into

    nothing = jnp.zeros((SUB, LANES), jnp.float32)
    group_one, group_two, tail_low, tail_high = nothing, nothing, nothing, nothing
    for slot in range(4):
        group_one = spread(slot, slot, group_one)
        group_two = spread(4 + slot, slot, group_two)
    tail_low = spread(9, 2, spread(8, 0, tail_low))
    tail_high = spread(9, 3, spread(8, 1, tail_high))
    tail = pltpu.roll(tail_low, 4, 0) + tail_high

    shift = 32 + row_part * 64
    for brick in range(destinations // 4):
        low_half = placed[0:16, brick * LANES : (brick + 1) * LANES]
        high_half = placed[16:32, brick * LANES : (brick + 1) * LANES]
        packed = low_half + pltpu.roll(high_half, shift, 1)
        last = jnp.where(row < 4, packed[8:16], tail)
        for inner in range(4):
            at = brick * 4 + inner
            send_ref[at, 0:8, :] = packed[0:8]
            send_ref[at, 8:16, :] = last
            send_ref[at, 16:24, :] = group_one
            send_ref[at, 24:32, :] = group_two


def plane_derivative(field, dim, lane):
    position = lane // 16 if dim == 1 else lane % 16
    extent = 8 if dim == 1 else 16
    unit = 16 if dim == 1 else 1
    total = None
    for order in range(1, 5):
        ahead = pltpu.roll(field, LANES - order * unit, 1)
        behind = pltpu.roll(field, order * unit, 1)
        term = stencil_weights[order - 1] * (
            jnp.where(position + order < extent, ahead, 0.0)
            - jnp.where(position - order >= 0, behind, 0.0)
        )
        total = term if total is None else total + term
    return total


def row_derivative(read, start, count):
    total = stencil_weights[0] * (read(start + 1, count) - read(start - 1, count))
    for order in range(2, 5):
        total = total + stencil_weights[order - 1] * (
            read(start + order, count) - read(start - order, count)
        )
    return total


def velocity_update(wide_stress, old_velocity, density, inside):
    count = 16
    lane = lanes_of((count, LANES))

    def along(component, dim):
        if dim == 0:
            return row_derivative(
                lambda at, size: wide_stress[component, at : at + size, :], 4, count
            )
        return plane_derivative(wide_stress[component, 4 : 4 + count, :], dim, lane)

    sums = [
        along(0, 0) + along(5, 1) + along(4, 2),
        along(5, 0) + along(1, 1) + along(3, 2),
        along(4, 0) + along(3, 1) + along(2, 2),
    ]
    return [
        jnp.where(inside, old_velocity[at] + time_step * sums[at] / density, 0.0)
        for at in range(3)
    ]


def stress_update(wide_velocity, old_stress, stiff):
    lane = lanes_of((SUB, LANES))

    def along(component, dim):
        if dim == 0:
            return row_derivative(
                lambda at, size: wide_velocity[component, at : at + size, :], 4, SUB
            )
        return plane_derivative(wide_velocity[component, 4 : 4 + SUB, :], dim, lane)

    strain = [
        along(0, 0),
        along(1, 1),
        along(2, 2),
        along(2, 1) + along(1, 2),
        along(2, 0) + along(0, 2),
        along(1, 0) + along(0, 1),
    ]
    return [
        old_stress[row]
        + time_step
        * ordered_sum([stiff(symmetric_index(row, col)) * strain[col] for col in range(6)])
        for row in range(6)
    ]


def inside_rows(brick, bricks):
    place = rows_of((16, LANES)) - 4
    return ((brick > 0) | (place >= 0)) & ((brick < bricks - 1) | (place < SUB))


def first_step_kernel(
    got_ref, stiff_ref, stress_ref, velocity_ref, density_ref, wide_ref, moving_ref
):
    brick = lax.axis_index("gx")
    bricks = got_ref.shape[0] // 4
    lane = lanes_of((SUB, LANES))
    row = rows_of((SUB, LANES))

    lane_two = lanes_of((16, LANES))
    own_slot = (lane_two // 32) % 2 == 0
    for p in range(bricks):
        zero = got_ref[p * 4, 0:16, :] + got_ref[p * 4 + 1, 0:16, :]
        one = got_ref[p * 4 + 2, 0:16, :] + got_ref[p * 4 + 3, 0:16, :]
        low = jnp.where(own_slot, zero, one)
        high = jnp.where(own_slot, one, zero)
        high = jnp.where(own_slot, pltpu.roll(high, LANES - 32, 1), pltpu.roll(high, 32, 1))
        total = jnp.broadcast_to(high[10:11], (SUB, LANES))
        stiff_ref[p * 24 : p * 24 + 8, :] = low[0:8] / total
        stiff_ref[p * 24 + 8 : p * 24 + 16, :] = high[0:8] / total
        last = jnp.where(row < 3, low[8:16], pltpu.roll(high[8:16], 3, 0))
        stiff_ref[p * 24 + 16 : p * 24 + 24, :] = last / total

    kind = (lane // 64) * 2 + (lane // 8) % 2

    def settle(value, slot):
        if slot & 1:
            value = jnp.where(
                (lane // 8) % 2 == 0,
                pltpu.roll(value, LANES - 8, 1),
                pltpu.roll(value, 8, 1),
            )
        if slot & 2:
            value = pltpu.roll(value, 64, 1)
        return value

    for side in range(3):
        source = jnp.clip(brick + side - 1, 0, bricks - 1)
        valid = source == brick + side - 1

        def collect(rows, slot):
            pieces = [got_ref[source * 4 + (q ^ slot), rows : rows + 8, :] for q in range(4)]
            value = jnp.where(
                kind < 2,
                jnp.where(kind == 0, pieces[0], pieces[1]),
                jnp.where(kind == 2, pieces[2], pieces[3]),
            )
            return settle(value, slot)

        def keep(component, value):
            value = jnp.where(valid, value, 1.0 if component == 9 else 0.0)
            wide_ref[component, side * SUB : (side + 1) * SUB, :] = value

        for slot in range(4):
            keep(slot, collect(16, slot))
            keep(4 + slot, collect(24, slot))
        for component in (8, 9):
            slot = (component - 8) * 2
            upper = pltpu.roll(collect(8, slot), 4, 0)
            keep(component, jnp.where(row < 4, upper, collect(8, slot + 1)))

    density = wide_ref[9, 4:20, :]
    density_ref[...] = density
    fresh = velocity_update(
        wide_ref,
        [wide_ref[6 + at, 4:20, :] for at in range(3)],
        density,
        inside_rows(brick, bricks),
    )
    for at in range(3):
        velocity_ref[at] = fresh[at]
        moving_ref[at] = fresh[at]
    fresh = stress_update(
        moving_ref,
        [wide_ref[at, 8:16, :] for at in range(6)],
        lambda pair: stiff_ref[pl.ds(pair, SUB, stride=24), :],
    )
    for at in range(6):
        stress_ref[at] = fresh[at]


def stiffness_kernel(stiff_ref, out_ref, turned_ref):
    own = lax.axis_index("gy") * 64 + lax.axis_index("ga") * 8
    for p in range(SUB):
        turned_ref[...] = jnp.transpose(stiff_ref[p * 24 : (p + 1) * 24, :])
        for y in range(4):
            rows = pl.ds(pl.multiple_of(own + y * 16, 8), 8)
            out_ref[p * 32 + y * 8 : p * 32 + y * 8 + 8, :] = turned_ref[rows, 0:21]


def last_step_kernel(
    stress_ref,
    pair_ref,
    cross_ref,
    velocity_ref,
    density_ref,
    stiff_ref,
    out_velocity_ref,
    out_stress_ref,
    wide_ref,
    moving_ref,
    *,
    bricks,
):
    brick = lax.axis_index("gx")
    even = brick % 2 == 0
    for at in range(6):
        pair, cross = pair_ref[at], cross_ref[at]
        wide_ref[at, 0:8, :] = jnp.where(even, cross, pair)
        wide_ref[at, 8:16, :] = stress_ref[at]
        wide_ref[at, 16:24, :] = jnp.where(even, pair, cross)
    velocity = velocity_update(
        wide_ref,
        [velocity_ref[at] for at in range(3)],
        density_ref[...],
        inside_rows(brick, bricks),
    )
    for at in range(3):
        moving_ref[at] = velocity[at]
    stress = stress_update(
        moving_ref,
        [stress_ref[at] for at in range(6)],
        lambda pair: stiff_ref[pl.ds(pair, SUB, stride=24), :],
    )
    own = lax.axis_index("gy") * 64 + lax.axis_index("ga") * 8

    def put(out_ref, at, value):
        for y in range(4):
            turned = pltpu.roll(value, (LANES - own - y * 16) % LANES, 1)
            out_ref[pl.ds(at * 32 + y, SUB, stride=4), :] = turned[:, 0:8]

    for at in range(3):
        put(out_velocity_ref, at, moving_ref[at, 4:12, :])
    for at in range(6):
        put(out_stress_ref, at, stress[at])


def on_plane(euler_table, crystal, orient, weight, cell_map, density, velocity, stress):
    part_x = lax.axis_size("gx")
    devices = part_x * lax.axis_size("gy") * lax.axis_size("ga")
    grains, cells = orient.shape[0], orient.shape[3]
    tiles = cells // LANES
    octets = grains // SUB
    vmem = pl.BlockSpec(memory_space=pltpu.VMEM)
    hbm = pl.BlockSpec(memory_space=pltpu.HBM)
    f32 = jnp.float32

    send = pl.pallas_call(
        grain_kernel,
        out_shape=jax.ShapeDtypeStruct((devices, BLOCK_ROWS, LANES), f32),
        in_specs=[hbm] * 8,
        out_specs=vmem,
        scratch_shapes=[
            pltpu.SMEM((21,), f32),
            pltpu.VMEM(euler_table.shape, f32),
            pltpu.VMEM((grains * tiles, LANES), jnp.int32),
            pltpu.VMEM((grains, cells), weight.dtype),
            pltpu.VMEM((1, cells), jnp.int32),
            pltpu.VMEM((SUB * 4, 8), f32),
            pltpu.VMEM((3 * SUB * 4, 8), f32),
            pltpu.VMEM((6 * SUB * 4, 8), f32),
            pltpu.VMEM((SUB, euler_table.shape[1]), f32),
            pltpu.VMEM((32, cells), f32),
            pltpu.VMEM((2 * cells, cells), jnp.bfloat16),
            pltpu.VMEM((22, SUB, LANES), f32),
            pltpu.SemaphoreType.DMA((8,)),
        ],
        compiler_params=pltpu.CompilerParams(vmem_limit_bytes=8 * 2**20),
    )(*[pltpu.with_memory_space_constraint(x, pltpu.HBM) for x in (
        crystal,
        euler_table,
        orient.reshape(grains * tiles, LANES),
        weight.reshape(grains, cells),
        cell_map.reshape(1, cells),
        density.reshape(SUB * 4, 8),
        velocity.reshape(3 * SUB * 4, 8),
        stress.reshape(6 * SUB * 4, 8),
    )])
    got = lax.all_to_all(send, ("gx", "gy", "ga"), split_axis=0, concat_axis=0, tiled=True)
    stiff, middle_stress, middle_velocity, wide_density = pl.pallas_call(
        first_step_kernel,
        out_shape=(
            jax.ShapeDtypeStruct((part_x * 24, LANES), f32),
            jax.ShapeDtypeStruct((6, SUB, LANES), f32),
            jax.ShapeDtypeStruct((3, 16, LANES), f32),
            jax.ShapeDtypeStruct((16, LANES), f32),
        ),
        in_specs=[vmem],
        out_specs=(vmem,) * 4,
        scratch_shapes=[
            pltpu.VMEM((FIELDS, 24, LANES), f32),
            pltpu.VMEM((3, 16, LANES), f32),
        ],
        compiler_params=pltpu.CompilerParams(vmem_limit_bytes=8 * 2**20),
    )(got)
    pair = lax.ppermute(middle_stress, "gx", [(i, i ^ 1) for i in range(part_x)])
    swaps = [(i, i + 1) for i in range(1, part_x - 1, 2)]
    cross = lax.ppermute(middle_stress, "gx", swaps + [(b, a) for a, b in swaps])
    stiffness = pl.pallas_call(
        stiffness_kernel,
        out_shape=jax.ShapeDtypeStruct((SUB * 4 * 8, 21), f32),
        in_specs=[vmem],
        out_specs=vmem,
        scratch_shapes=[pltpu.VMEM((LANES, 24), f32)],
        cost_estimate=pl.CostEstimate(flops=100000, bytes_accessed=200000, transcendentals=0),
        compiler_params=pltpu.CompilerParams(vmem_limit_bytes=8 * 2**20),
    )(stiff)
    new_velocity, new_stress = pl.pallas_call(
        functools.partial(last_step_kernel, bricks=part_x),
        out_shape=(
            jax.ShapeDtypeStruct((3 * SUB * 4, 8), f32),
            jax.ShapeDtypeStruct((6 * SUB * 4, 8), f32),
        ),
        in_specs=[vmem] * 6,
        out_specs=(vmem,) * 2,
        scratch_shapes=[
            pltpu.VMEM((6, 24, LANES), f32),
            pltpu.VMEM((3, 16, LANES), f32),
        ],
        compiler_params=pltpu.CompilerParams(vmem_limit_bytes=8 * 2**20),
    )(middle_stress, pair, cross, middle_velocity, wide_density, stiff)
    return (
        stiffness.reshape(SUB, 4, 8, 21).transpose(3, 0, 1, 2),
        new_velocity.reshape(3, SUB, 4, 8),
        new_stress.reshape(6, SUB, 4, 8),
    )


def on_device(euler_table, crystal, orient, weight, cell_map, density, velocity, stress):
    sizes = (lax.axis_size("gx"), lax.axis_size("gy"), lax.axis_size("ga"))
    form = on_plane if fits_plane(*sizes, orient, stress, euler_table) else on_device_general
    return form(euler_table, crystal, orient, weight, cell_map, density, velocity, stress)


def solution(mesh):
    return jax.shard_map(
        on_device,
        mesh=mesh,
        in_specs=(
            P(),
            P(),
            P("ga", "gx", "gy", None),
            P("ga", "gx", "gy", None),
            P("gx", "gy", None),
            P("gx", "gy", "ga"),
            P(None, "gx", "gy", "ga"),
            P(None, "gx", "gy", "ga"),
        ),
        out_specs=(P(None, "gx", "gy", "ga"), P(None, "gx", "gy", "ga"), P(None, "gx", "gy", "ga")),
        check_vma=False,
    )
```

```python
import functools

import jax
import jax.numpy as jnp
from jax import lax
from jax.experimental import pallas as pl
from jax.experimental.pallas import tpu as pltpu
from jax.sharding import PartitionSpec as P

STEPS = 2


stencil_weights = (0.8, -0.2, 4.0 / 105.0, -1.0 / 280.0)
time_step = 0.2
grain_block = 4
voigt_pairs = ((0, 0), (1, 1), (2, 2), (1, 2), (0, 2), (0, 1))
upper_pairs = [
    (row_index, col_index) for row_index in range(6) for col_index in range(row_index, 6)
]


def with_halo(cells, sides, width):
    for axis, dim in sides:
        count = lax.axis_size(axis)
        ends = count - 1
        head = lax.slice_in_dim(cells, 0, width, axis=dim)
        tail = lax.slice_in_dim(cells, cells.shape[dim] - width, cells.shape[dim], axis=dim)
        cells = jnp.concatenate(
            [
                lax.ppermute(tail, axis, [(i, (i + 1) % count) for i in range(ends)]),
                cells,
                lax.ppermute(head, axis, [((i + 1) % count, i) for i in range(ends)]),
            ],
            axis=dim,
        )
    return cells


def symmetric_index(first_index, second_index):
    return upper_pairs.index((min(first_index, second_index), max(first_index, second_index)))


def ordered_sum(summands):
    running = summands[0]
    for summand in summands[1:]:
        running = running + summand
    return running


def rotated_table(euler_table, crystal):
    cos_one, sin_one = (jnp.cos(euler_table[0]), jnp.sin(euler_table[0]))
    cos_mid, sin_mid = (jnp.cos(euler_table[1]), jnp.sin(euler_table[1]))
    cos_two, sin_two = (jnp.cos(euler_table[2]), jnp.sin(euler_table[2]))
    bunge = [
        [
            cos_one * cos_two - sin_one * sin_two * cos_mid,
            sin_one * cos_two + cos_one * sin_two * cos_mid,
            sin_two * sin_mid,
        ],
        [
            -cos_one * sin_two - sin_one * cos_two * cos_mid,
            -sin_one * sin_two + cos_one * cos_two * cos_mid,
            cos_two * sin_mid,
        ],
        [sin_one * sin_mid, -cos_one * sin_mid, cos_mid],
    ]
    rotation = [[bunge[col_index][row_index] for col_index in range(3)] for row_index in range(3)]
    bond = []
    for out_index in range(6):
        first, second = voigt_pairs[out_index]
        bond_row = []
        for in_index in range(6):
            third, fourth = voigt_pairs[in_index]
            if in_index < 3:
                bond_row.append(rotation[first][third] * rotation[second][third])
            else:
                bond_row.append(
                    rotation[first][third] * rotation[second][fourth]
                    + rotation[first][fourth] * rotation[second][third]
                )
        bond.append(bond_row)
    entries = [
        [crystal[symmetric_index(row_index, col_index)] for col_index in range(6)]
        for row_index in range(6)
    ]
    product = [
        [
            ordered_sum([bond[row_index][inner] * entries[inner][col_index] for inner in range(6)])
            for col_index in range(6)
        ]
        for row_index in range(6)
    ]
    rotated = [
        ordered_sum([product[row_index][inner] * bond[col_index][inner] for inner in range(6)])
        for row_index, col_index in upper_pairs
    ]
    return jnp.stack(rotated)


def accumulate(table, orient_rows, weight_rows):
    blocks = orient_rows.shape[0] // grain_block
    count_cells = orient_rows.shape[1]

    def absorb(carry, inputs):
        chosen, masses = inputs
        picked = jnp.take(table, chosen, axis=1)
        masses_wide = masses.astype(jnp.float32)
        return (
            (
                carry[0] + jnp.sum(picked * masses_wide[None], axis=1),
                carry[1] + jnp.sum(masses_wide, axis=0),
            ),
            None,
        )

    initial = (jnp.zeros((21, count_cells), jnp.float32), jnp.zeros((count_cells,), jnp.float32))
    result, unused = lax.scan(
        absorb,
        initial,
        (
            orient_rows.reshape(blocks, grain_block, count_cells),
            weight_rows.reshape(blocks, grain_block, count_cells),
        ),
    )
    return result


def derivative(padded, direction):
    interior = [padded.shape[0]] + [extent - 8 for extent in padded.shape[1:]]

    def window(offset):
        starts = [0, 4, 4, 4]
        starts[direction] = 4 + offset
        return lax.slice(
            padded, starts, [begin + extent for begin, extent in zip(starts, interior)]
        )

    result = stencil_weights[0] * (window(1) - window(-1))
    for order_index in range(1, 4):
        result = result + stencil_weights[order_index] * (
            window(order_index + 1) - window(-order_index - 1)
        )
    return result


def advance_velocity(velocity, padded_stress, density):
    along_x = derivative(jnp.stack([padded_stress[0], padded_stress[5], padded_stress[4]]), 1)
    along_y = derivative(jnp.stack([padded_stress[5], padded_stress[1], padded_stress[3]]), 2)
    along_z = derivative(jnp.stack([padded_stress[4], padded_stress[3], padded_stress[2]]), 3)
    return velocity + time_step * (along_x + along_y + along_z) / density[None]


def advance_stress(stress, padded_velocity, stiffness):
    grad_x = derivative(padded_velocity, 1)
    grad_y = derivative(padded_velocity, 2)
    grad_z = derivative(padded_velocity, 3)
    strain = [
        grad_x[0],
        grad_y[1],
        grad_z[2],
        grad_y[2] + grad_z[1],
        grad_x[2] + grad_z[0],
        grad_x[1] + grad_y[0],
    ]
    updated = []
    for row_index in range(6):
        change = ordered_sum(
            [
                stiffness[symmetric_index(row_index, col_index)] * strain[col_index]
                for col_index in range(6)
            ]
        )
        updated.append(stress[row_index] + time_step * change)
    return jnp.stack(updated)


def on_device_general(euler_table, crystal, orient, weight, cell_map, density, velocity, stress):
    part_x = lax.axis_size("gx")
    part_y = lax.axis_size("gy")
    layers = lax.axis_size("ga")
    brick_x, brick_y, brick_z = (stress.shape[1], stress.shape[2], stress.shape[3])
    sub_x = brick_x // part_x
    sub_y = brick_y // part_y
    depth = brick_z * layers
    grains = orient.shape[0]
    count_cells = orient.shape[3]
    table = rotated_table(euler_table, crystal)
    summed, total = accumulate(
        table, orient.reshape(grains, count_cells), weight.reshape(grains, count_cells)
    )
    slots = cell_map.reshape(count_cells)
    layer_pos = slots % depth
    remainder = slots // depth
    sub_y_pos = remainder % sub_y
    remainder = remainder // sub_y
    brick_y_pos = remainder % part_y
    remainder = remainder // part_y
    sub_x_pos = remainder % sub_x
    brick_x_pos = remainder // sub_x
    target = (
        ((brick_x_pos * part_y + brick_y_pos) * sub_x + sub_x_pos) * sub_y + sub_y_pos
    ) * depth + layer_pos
    placed = jnp.zeros((21, count_cells), jnp.float32).at[:, target].set(summed)
    counted = jnp.zeros((count_cells,), jnp.float32).at[target].set(total)
    placed = placed.reshape(21, part_x * part_y, sub_x, sub_y, depth)
    counted = counted.reshape(part_x * part_y, sub_x, sub_y, depth)
    placed, counted = (
        lax.psum_scatter(placed, "ga", scatter_dimension=4, tiled=True),
        lax.psum_scatter(counted, "ga", scatter_dimension=3, tiled=True),
    )
    averaged = placed / counted[None]
    moved = lax.all_to_all(averaged, ("gx", "gy"), split_axis=1, concat_axis=1, tiled=True)
    moved = moved.reshape(21, part_x, part_y, sub_x, sub_y, brick_z)
    stiffness = moved.transpose(0, 1, 3, 2, 4, 5).reshape(21, brick_x, brick_y, brick_z)
    for step_index in range(STEPS):
        padded_stress = with_halo(stress, (("gx", 1), ("gy", 2), ("ga", 3)), 4)
        velocity = advance_velocity(velocity, padded_stress, density)
        padded_velocity = with_halo(velocity, (("gx", 1), ("gy", 2), ("ga", 3)), 4)
        stress = advance_stress(stress, padded_velocity, stiffness)
    return (stiffness, velocity, stress)


SUB = 8
LANES = 128
SUM_ROWS = 11
BLOCK_ROWS = 21
FIELDS = 10
HALF = FIELDS // 2
LOW_ROWS = tuple(range(8)) + (16, 17, 18)
HIGH_ROWS = tuple(range(8, 16)) + (19, 20, 21)


def fits_plane(part_x, part_y, layers, orient, stress, euler_table):
    brick_x, brick_y, brick_z = stress.shape[1:]
    return (
        part_x % 2 == 0
        and part_y == 2
        and layers == 2
        and brick_x == SUB
        and part_x == SUB
        and brick_y == 4
        and brick_z == 8
        and orient.shape[3] == part_x * 64
        and orient.shape[0] % 8 == 0
        and euler_table.shape[1] % LANES == 0
    )


def lanes_of(shape):
    return lax.broadcasted_iota(jnp.int32, shape, len(shape) - 1)


def rows_of(shape):
    return lax.broadcasted_iota(jnp.int32, shape, len(shape) - 2)


def bond_matrix(trig):
    cos_one, cos_mid, cos_two, sin_one, sin_mid, sin_two = trig
    cos_two_mid = cos_two * cos_mid
    sin_two_mid = sin_two * cos_mid
    bunge = [
        [
            cos_one * cos_two - sin_one * sin_two_mid,
            sin_one * cos_two + cos_one * sin_two_mid,
            sin_two * sin_mid,
        ],
        [
            -cos_one * sin_two - sin_one * cos_two_mid,
            -sin_one * sin_two + cos_one * cos_two_mid,
            cos_two * sin_mid,
        ],
        [sin_one * sin_mid, -cos_one * sin_mid, cos_mid],
    ]
    rotation = [[bunge[col][row] for col in range(3)] for row in range(3)]
    bond = []
    for first, second in voigt_pairs:
        row = []
        for in_index, (third, fourth) in enumerate(voigt_pairs):
            if in_index < 3:
                row.append(rotation[first][third] * rotation[second][third])
            else:
                row.append(
                    rotation[first][third] * rotation[second][fourth]
                    + rotation[first][fourth] * rotation[second][third]
                )
        bond.append(row)
    return bond


def grain_kernel(
    crystal_hbm,
    euler_hbm,
    orient_hbm,
    weight_hbm,
    map_hbm,
    density_hbm,
    velocity_hbm,
    stress_hbm,
    send_ref,
    crystal_ref,
    euler_ref,
    orient_ref,
    weight_ref,
    map_ref,
    density_ref,
    velocity_ref,
    stress_ref,
    trig_ref,
    sums_ref,
    place_ref,
    acc_ref,
    arrived,
):
    row_part = lax.axis_index("gy")
    layer = lax.axis_index("ga")
    grains = weight_ref.shape[0]
    cells = weight_ref.shape[1]
    tiles = cells // LANES
    octets = grains // SUB
    table_tiles = euler_ref.shape[1] // LANES
    destinations = send_ref.shape[0] // BLOCK_ROWS

    copies = [
        pltpu.make_async_copy(source, target, arrived.at[at])
        for at, (source, target) in enumerate(
            [
                (euler_hbm, euler_ref),
                (orient_hbm, orient_ref),
                (weight_hbm, weight_ref),
                (crystal_hbm, crystal_ref),
                (map_hbm, map_ref),
                (stress_hbm, stress_ref),
                (velocity_hbm, velocity_ref),
                (density_hbm, density_ref),
            ]
        )
    ]
    for copy in copies:
        copy.start()
    sums_ref[...] = jnp.zeros_like(sums_ref)
    place_ref[...] = jnp.zeros_like(place_ref)

    copies[0].wait()
    angles = euler_ref[...]
    trig_ref[0:3, :] = jnp.cos(angles)
    trig_ref[3:6, :] = jnp.sin(angles)

    for copy in copies[1:4]:
        copy.wait()
    entries = [
        [crystal_ref[symmetric_index(row, col)] for col in range(6)] for row in range(6)
    ]
    row_of = {}
    for k in range(len(LOW_ROWS)):
        row_of[LOW_ROWS[k]] = k
        row_of[HIGH_ROWS[k]] = 16 + k

    def pick(tile, octet):
        index = orient_ref[pl.ds(octet * SUB * tiles + tile, SUB, stride=tiles), :]
        low, high = index & (LANES - 1), index >> 7
        values = [None] * 6
        for table_tile in range(table_tiles):
            here = high == table_tile
            for which in range(6):
                source = jnp.broadcast_to(
                    trig_ref[
                        which : which + 1, table_tile * LANES : (table_tile + 1) * LANES
                    ],
                    (SUB, LANES),
                )
                found = jnp.take_along_axis(source, low, axis=1, mode="promise_in_bounds")
                values[which] = found if table_tile == 0 else jnp.where(here, found, values[which])
        return values

    def one_tile(tile, unused):
        for octet in range(octets):
            bond = bond_matrix(pick(tile, octet))
            mass = weight_ref[
                octet * SUB : (octet + 1) * SUB, pl.ds(pl.multiple_of(tile * LANES, LANES), LANES)
            ].astype(jnp.float32)
            pair = 0
            for row in range(6):
                product = [
                    ordered_sum([bond[row][inner] * entries[inner][col] for inner in range(6)])
                    * mass
                    for col in range(6)
                ]
                for col in range(row, 6):
                    value = ordered_sum([product[inner] * bond[col][inner] for inner in range(6)])
                    acc_ref[pair] = value if octet == 0 else acc_ref[pair] + value
                    pair += 1
            acc_ref[21] = mass if octet == 0 else acc_ref[21] + mass
        for pair in range(22):
            sums_ref[
                row_of[pair] : row_of[pair] + 1, pl.ds(pl.multiple_of(tile * LANES, LANES), LANES)
            ] = jnp.sum(acc_ref[pair], axis=0, keepdims=True)
        return unused

    lax.fori_loop(0, tiles, one_tile, 0)
    for copy in copies[4:]:
        copy.wait()

    slots = map_ref[...]
    half = cells // (cells // 32)
    for chunk in range(cells // half):
        wanted = rows_of((half, cells)) + chunk * half
        hit = jnp.where(jnp.broadcast_to(slots, (half, cells)) == wanted, 1.0, 0.0)
        start = pl.multiple_of(chunk * 2 * half + row_part * half, half)
        place_ref[pl.ds(start, half), :] = hit.astype(jnp.bfloat16)
    sums = sums_ref[...]
    part_one = sums.astype(jnp.bfloat16)
    rest = sums - part_one.astype(jnp.float32)
    part_two = rest.astype(jnp.bfloat16)
    part_three = (rest - part_two.astype(jnp.float32)).astype(jnp.bfloat16)
    parts = jnp.concatenate([part_one, part_two, part_three], axis=0)
    placed = lax.dot_general(
        parts, place_ref[...], (((1,), (1,)), ((), ())), preferred_element_type=jnp.float32
    )
    placed = placed[0:32] + placed[32:64] + placed[64:96]

    own = row_part * 2 + layer

    def field_rows(component, y):
        if component < 6:
            return stress_ref[pl.ds(component * 32 + y, SUB, stride=4), :]
        if component < 9:
            return velocity_ref[pl.ds((component - 6) * 32 + y, SUB, stride=4), :]
        return density_ref[pl.ds(y, SUB, stride=4), :]

    def spread(component, slot, into):
        goal = own ^ slot
        for y in range(4):
            start = (goal // 2) * 64 + y * 16 + (goal % 2) * 8
            narrow = jnp.concatenate(
                [field_rows(component, y), jnp.zeros((SUB, LANES - 8), jnp.float32)], axis=1
            )
            into = into + pltpu.roll(narrow, start, 1)
        return into

    nothing = jnp.zeros((SUB, LANES), jnp.float32)
    groups, tails = [], []
    for half in range(2):
        group, tail = nothing, nothing
        for slot in range(4):
            group = spread(half * HALF + slot, slot, group)
            piece = spread(half * HALF + 4, slot, nothing)
            tail = tail + (piece if slot == 0 else pltpu.roll(piece, SUB - 2 * slot, 0))
        groups.append(group)
        tails.append(tail[0:2])

    shift = 32 + row_part * 64
    for brick in range(destinations // 4):
        low_half = placed[0:16, brick * LANES : (brick + 1) * LANES]
        high_half = placed[16:32, brick * LANES : (brick + 1) * LANES]
        packed = low_half + pltpu.roll(high_half, shift, 1)
        for inner in range(4):
            at = (brick * 4 + inner) * BLOCK_ROWS
            send_ref[at : at + SUM_ROWS, :] = packed[0:SUM_ROWS]
            send_ref[at + SUM_ROWS : at + SUM_ROWS + SUB, :] = groups[brick % 2]
            send_ref[at + SUM_ROWS + SUB : at + BLOCK_ROWS, :] = tails[brick % 2]


def plane_derivative(field, dim, lane):
    position = lane // 16 if dim == 1 else lane % 16
    extent = 8 if dim == 1 else 16
    unit = 16 if dim == 1 else 1
    total = None
    for order in range(1, 5):
        ahead = pltpu.roll(field, LANES - order * unit, 1)
        behind = pltpu.roll(field, order * unit, 1)
        term = stencil_weights[order - 1] * (
            jnp.where(position + order < extent, ahead, 0.0)
            - jnp.where(position - order >= 0, behind, 0.0)
        )
        total = term if total is None else total + term
    return total


def row_derivative(read, start, count):
    total = stencil_weights[0] * (read(start + 1, count) - read(start - 1, count))
    for order in range(2, 5):
        total = total + stencil_weights[order - 1] * (
            read(start + order, count) - read(start - order, count)
        )
    return total


def velocity_update(wide_stress, old_velocity, density, inside):
    count = 16
    lane = lanes_of((count, LANES))

    def along(component, dim):
        if dim == 0:
            return row_derivative(
                lambda at, size: wide_stress[component, at : at + size, :], 4, count
            )
        return plane_derivative(wide_stress[component, 4 : 4 + count, :], dim, lane)

    sums = [
        along(0, 0) + along(5, 1) + along(4, 2),
        along(5, 0) + along(1, 1) + along(3, 2),
        along(4, 0) + along(3, 1) + along(2, 2),
    ]
    return [
        jnp.where(inside, old_velocity[at] + time_step * sums[at] / density, 0.0)
        for at in range(3)
    ]


def stress_update(wide_velocity, old_stress, stiff):
    lane = lanes_of((SUB, LANES))

    def along(component, dim):
        if dim == 0:
            return row_derivative(
                lambda at, size: wide_velocity[component, at : at + size, :], 4, SUB
            )
        return plane_derivative(wide_velocity[component, 4 : 4 + SUB, :], dim, lane)

    strain = [
        along(0, 0),
        along(1, 1),
        along(2, 2),
        along(2, 1) + along(1, 2),
        along(2, 0) + along(0, 2),
        along(1, 0) + along(0, 1),
    ]
    return [
        old_stress[row]
        + time_step
        * ordered_sum([stiff(symmetric_index(row, col)) * strain[col] for col in range(6)])
        for row in range(6)
    ]


def inside_rows(brick, bricks):
    place = rows_of((16, LANES)) - 4
    return ((brick > 0) | (place >= 0)) & ((brick < bricks - 1) | (place < SUB))


def field_kernel(got_ref, half_ref):
    brick = lax.axis_index("gx")
    bricks = got_ref.shape[0] // BLOCK_ROWS // 4

    def collect(source, offset, count, slot):
        lane = lanes_of((count, LANES))
        kind = (lane // 64) * 2 + (lane // 8) % 2
        pieces = [
            got_ref[pl.ds((source * 4 + (q ^ slot)) * BLOCK_ROWS + offset, count), :]
            for q in range(4)
        ]
        value = jnp.where(
            kind < 2,
            jnp.where(kind == 0, pieces[0], pieces[1]),
            jnp.where(kind == 2, pieces[2], pieces[3]),
        )
        if slot & 1:
            value = jnp.where(
                (lane // 8) % 2 == 0,
                pltpu.roll(value, LANES - 8, 1),
                pltpu.roll(value, 8, 1),
            )
        if slot & 2:
            value = pltpu.roll(value, 64, 1)
        return value

    for side in range(4):
        wanted = (brick // 2) * 2 + side - 1
        source = jnp.clip(wanted, 0, bricks - 1)
        valid = source == wanted
        first = side * SUB
        for slot in range(4):
            value = collect(source, SUM_ROWS, SUB, slot)
            half_ref[slot, first : first + SUB, :] = jnp.where(valid, value, 0.0)
            value = collect(source, SUM_ROWS + SUB, 2, slot)
            half_ref[4, first + 2 * slot : first + 2 * slot + 2, :] = jnp.where(valid, value, 0.0)


def sums_kernel(got_ref, stiff_ref):
    row = rows_of((SUB, LANES))
    own_slot = (lanes_of((SUM_ROWS, LANES)) // 32) % 2 == 0
    for p in range(got_ref.shape[0] // BLOCK_ROWS // 4):
        zero, one = [
            got_ref[at : at + SUM_ROWS, :] + got_ref[at + BLOCK_ROWS : at + BLOCK_ROWS + SUM_ROWS, :]
            for at in (p * 4 * BLOCK_ROWS, (p * 4 + 2) * BLOCK_ROWS)
        ]
        low = jnp.where(own_slot, zero, one)
        high = jnp.where(own_slot, one, zero)
        high = jnp.where(own_slot, pltpu.roll(high, LANES - 32, 1), pltpu.roll(high, 32, 1))
        total = jnp.broadcast_to(high[10:11], (SUB, LANES))
        stiff_ref[p * 24 : p * 24 + 8, :] = low[0:8] / total
        stiff_ref[p * 24 + 8 : p * 24 + 16, :] = high[0:8] / total
        stiff_ref[p * 24 + 16 : p * 24 + 19, :] = low[8:11] / total[0:3]
        stiff_ref[p * 24 + 19 : p * 24 + 22, :] = high[8:11] / total[0:3]


def first_step_kernel(
    own_ref,
    other_ref,
    stiff_ref,
    stress_ref,
    velocity_ref,
    density_ref,
    wide_ref,
    moving_ref,
    *,
    bricks,
):
    brick = lax.axis_index("gx")
    odd = brick % 2
    rows = pl.ds(pl.multiple_of(odd * SUB, SUB), 24)
    for at in range(HALF):
        wide_ref[odd * HALF + at] = own_ref[at, rows, :]
        wide_ref[(1 - odd) * HALF + at] = other_ref[at, rows, :]
    inside = inside_rows(brick, bricks)
    density = jnp.where(inside, wide_ref[9, 4:20, :], 1.0)
    density_ref[...] = density
    fresh = velocity_update(
        wide_ref, [wide_ref[6 + at, 4:20, :] for at in range(3)], density, inside
    )
    for at in range(3):
        velocity_ref[at] = fresh[at]
        moving_ref[at] = fresh[at]
    fresh = stress_update(
        moving_ref,
        [wide_ref[at, 8:16, :] for at in range(6)],
        lambda pair: stiff_ref[pl.ds(pair, SUB, stride=24), :],
    )
    for at in range(6):
        stress_ref[at] = fresh[at]


def stiffness_kernel(stiff_ref, out_ref, turned_ref):
    own = lax.axis_index("gy") * 64 + lax.axis_index("ga") * 8
    for p in range(SUB):
        turned_ref[...] = jnp.transpose(stiff_ref[p * 24 : (p + 1) * 24, :])
        for y in range(4):
            rows = pl.ds(pl.multiple_of(own + y * 16, 8), 8)
            out_ref[p * 32 + y * 8 : p * 32 + y * 8 + 8, :] = turned_ref[rows, 0:21]


def last_step_kernel(
    stress_ref,
    pair_ref,
    cross_ref,
    velocity_ref,
    density_ref,
    stiff_ref,
    out_velocity_ref,
    out_stress_ref,
    wide_ref,
    moving_ref,
    *,
    bricks,
):
    brick = lax.axis_index("gx")
    even = brick % 2 == 0
    for at in range(6):
        pair, cross = pair_ref[at], cross_ref[at]
        wide_ref[at, 0:8, :] = jnp.where(even, cross, pair)
        wide_ref[at, 8:16, :] = stress_ref[at]
        wide_ref[at, 16:24, :] = jnp.where(even, pair, cross)
    velocity = velocity_update(
        wide_ref,
        [velocity_ref[at] for at in range(3)],
        density_ref[...],
        inside_rows(brick, bricks),
    )
    for at in range(3):
        moving_ref[at] = velocity[at]
    stress = stress_update(
        moving_ref,
        [stress_ref[at] for at in range(6)],
        lambda pair: stiff_ref[pl.ds(pair, SUB, stride=24), :],
    )
    own = lax.axis_index("gy") * 64 + lax.axis_index("ga") * 8

    def put(out_ref, at, value):
        for y in range(4):
            turned = pltpu.roll(value, (LANES - own - y * 16) % LANES, 1)
            out_ref[pl.ds(at * 32 + y, SUB, stride=4), :] = turned[:, 0:8]

    for at in range(3):
        put(out_velocity_ref, at, moving_ref[at, 4:12, :])
    for at in range(6):
        put(out_stress_ref, at, stress[at])


def on_plane(euler_table, crystal, orient, weight, cell_map, density, velocity, stress):
    part_x = lax.axis_size("gx")
    devices = part_x * lax.axis_size("gy") * lax.axis_size("ga")
    grains, cells = orient.shape[0], orient.shape[3]
    tiles = cells // LANES
    octets = grains // SUB
    vmem = pl.BlockSpec(memory_space=pltpu.VMEM)
    hbm = pl.BlockSpec(memory_space=pltpu.HBM)
    f32 = jnp.float32

    send = pl.pallas_call(
        grain_kernel,
        out_shape=jax.ShapeDtypeStruct((devices * BLOCK_ROWS, LANES), f32),
        in_specs=[hbm] * 8,
        out_specs=vmem,
        scratch_shapes=[
            pltpu.SMEM((21,), f32),
            pltpu.VMEM(euler_table.shape, f32),
            pltpu.VMEM((grains * tiles, LANES), jnp.int32),
            pltpu.VMEM((grains, cells), weight.dtype),
            pltpu.VMEM((1, cells), jnp.int32),
            pltpu.VMEM((SUB * 4, 8), f32),
            pltpu.VMEM((3 * SUB * 4, 8), f32),
            pltpu.VMEM((6 * SUB * 4, 8), f32),
            pltpu.VMEM((SUB, euler_table.shape[1]), f32),
            pltpu.VMEM((32, cells), f32),
            pltpu.VMEM((2 * cells, cells), jnp.bfloat16),
            pltpu.VMEM((22, SUB, LANES), f32),
            pltpu.SemaphoreType.DMA((8,)),
        ],
        compiler_params=pltpu.CompilerParams(vmem_limit_bytes=8 * 2**20),
    )(*[pltpu.with_memory_space_constraint(x, pltpu.HBM) for x in (
        crystal,
        euler_table,
        orient.reshape(grains * tiles, LANES),
        weight.reshape(grains, cells),
        cell_map.reshape(1, cells),
        density.reshape(SUB * 4, 8),
        velocity.reshape(3 * SUB * 4, 8),
        stress.reshape(6 * SUB * 4, 8),
    )])
    got = lax.all_to_all(
        send.reshape(devices, 1, BLOCK_ROWS * LANES),
        ("gx", "gy", "ga"),
        split_axis=0,
        concat_axis=0,
        tiled=True,
    ).reshape(devices * BLOCK_ROWS, LANES)
    small = pltpu.CompilerParams(vmem_limit_bytes=8 * 2**20)
    own_half = pl.pallas_call(
        field_kernel,
        out_shape=jax.ShapeDtypeStruct((HALF, 4 * SUB, LANES), f32),
        in_specs=[vmem],
        out_specs=vmem,
        compiler_params=small,
    )(got)
    partners = [(i, i ^ 1) for i in range(part_x)]
    other_half = lax.ppermute(own_half, "gx", partners)
    stiff = pl.pallas_call(
        sums_kernel,
        out_shape=jax.ShapeDtypeStruct((part_x * 24, LANES), f32),
        in_specs=[vmem],
        out_specs=vmem,
        cost_estimate=pl.CostEstimate(flops=100000, bytes_accessed=200000, transcendentals=0),
        compiler_params=small,
    )(got)
    middle_stress, middle_velocity, wide_density = pl.pallas_call(
        functools.partial(first_step_kernel, bricks=part_x),
        out_shape=(
            jax.ShapeDtypeStruct((6, SUB, LANES), f32),
            jax.ShapeDtypeStruct((3, 16, LANES), f32),
            jax.ShapeDtypeStruct((16, LANES), f32),
        ),
        in_specs=[vmem] * 3,
        out_specs=(vmem,) * 3,
        scratch_shapes=[
            pltpu.VMEM((FIELDS, 24, LANES), f32),
            pltpu.VMEM((3, 16, LANES), f32),
        ],
        compiler_params=small,
    )(own_half, other_half, stiff)
    pair = lax.ppermute(middle_stress, "gx", partners)
    swaps = [(i, i + 1) for i in range(1, part_x - 1, 2)]
    cross = lax.ppermute(middle_stress, "gx", swaps + [(b, a) for a, b in swaps])
    stiffness = pl.pallas_call(
        stiffness_kernel,
        out_shape=jax.ShapeDtypeStruct((SUB * 4 * 8, 21), f32),
        in_specs=[vmem],
        out_specs=vmem,
        scratch_shapes=[pltpu.VMEM((LANES, 24), f32)],
        cost_estimate=pl.CostEstimate(flops=100000, bytes_accessed=200000, transcendentals=0),
        compiler_params=pltpu.CompilerParams(vmem_limit_bytes=8 * 2**20),
    )(stiff)
    new_velocity, new_stress = pl.pallas_call(
        functools.partial(last_step_kernel, bricks=part_x),
        out_shape=(
            jax.ShapeDtypeStruct((3 * SUB * 4, 8), f32),
            jax.ShapeDtypeStruct((6 * SUB * 4, 8), f32),
        ),
        in_specs=[vmem] * 6,
        out_specs=(vmem,) * 2,
        scratch_shapes=[
            pltpu.VMEM((6, 24, LANES), f32),
            pltpu.VMEM((3, 16, LANES), f32),
        ],
        compiler_params=pltpu.CompilerParams(vmem_limit_bytes=8 * 2**20),
    )(middle_stress, pair, cross, middle_velocity, wide_density, stiff)
    return (
        stiffness.reshape(SUB, 4, 8, 21).transpose(3, 0, 1, 2),
        new_velocity.reshape(3, SUB, 4, 8),
        new_stress.reshape(6, SUB, 4, 8),
    )


def on_device(euler_table, crystal, orient, weight, cell_map, density, velocity, stress):
    sizes = (lax.axis_size("gx"), lax.axis_size("gy"), lax.axis_size("ga"))
    form = on_plane if fits_plane(*sizes, orient, stress, euler_table) else on_device_general
    return form(euler_table, crystal, orient, weight, cell_map, density, velocity, stress)


def solution(mesh):
    return jax.shard_map(
        on_device,
        mesh=mesh,
        in_specs=(
            P(),
            P(),
            P("ga", "gx", "gy", None),
            P("ga", "gx", "gy", None),
            P("gx", "gy", None),
            P("gx", "gy", "ga"),
            P(None, "gx", "gy", "ga"),
            P(None, "gx", "gy", "ga"),
        ),
        out_specs=(P(None, "gx", "gy", "ga"), P(None, "gx", "gy", "ga"), P(None, "gx", "gy", "ga")),
        check_vma=False,
    )
```

```python
import functools

import jax
import jax.numpy as jnp
from jax import lax
from jax.experimental import pallas as pl
from jax.experimental.pallas import tpu as pltpu
from jax.sharding import PartitionSpec as P

STEPS = 2


stencil_weights = (0.8, -0.2, 4.0 / 105.0, -1.0 / 280.0)
time_step = 0.2
grain_block = 4
voigt_pairs = ((0, 0), (1, 1), (2, 2), (1, 2), (0, 2), (0, 1))
upper_pairs = [
    (row_index, col_index) for row_index in range(6) for col_index in range(row_index, 6)
]


def with_halo(cells, sides, width):
    for axis, dim in sides:
        count = lax.axis_size(axis)
        ends = count - 1
        head = lax.slice_in_dim(cells, 0, width, axis=dim)
        tail = lax.slice_in_dim(cells, cells.shape[dim] - width, cells.shape[dim], axis=dim)
        cells = jnp.concatenate(
            [
                lax.ppermute(tail, axis, [(i, (i + 1) % count) for i in range(ends)]),
                cells,
                lax.ppermute(head, axis, [((i + 1) % count, i) for i in range(ends)]),
            ],
            axis=dim,
        )
    return cells


def symmetric_index(first_index, second_index):
    return upper_pairs.index((min(first_index, second_index), max(first_index, second_index)))


def ordered_sum(summands):
    running = summands[0]
    for summand in summands[1:]:
        running = running + summand
    return running


def rotated_table(euler_table, crystal):
    cos_one, sin_one = (jnp.cos(euler_table[0]), jnp.sin(euler_table[0]))
    cos_mid, sin_mid = (jnp.cos(euler_table[1]), jnp.sin(euler_table[1]))
    cos_two, sin_two = (jnp.cos(euler_table[2]), jnp.sin(euler_table[2]))
    bunge = [
        [
            cos_one * cos_two - sin_one * sin_two * cos_mid,
            sin_one * cos_two + cos_one * sin_two * cos_mid,
            sin_two * sin_mid,
        ],
        [
            -cos_one * sin_two - sin_one * cos_two * cos_mid,
            -sin_one * sin_two + cos_one * cos_two * cos_mid,
            cos_two * sin_mid,
        ],
        [sin_one * sin_mid, -cos_one * sin_mid, cos_mid],
    ]
    rotation = [[bunge[col_index][row_index] for col_index in range(3)] for row_index in range(3)]
    bond = []
    for out_index in range(6):
        first, second = voigt_pairs[out_index]
        bond_row = []
        for in_index in range(6):
            third, fourth = voigt_pairs[in_index]
            if in_index < 3:
                bond_row.append(rotation[first][third] * rotation[second][third])
            else:
                bond_row.append(
                    rotation[first][third] * rotation[second][fourth]
                    + rotation[first][fourth] * rotation[second][third]
                )
        bond.append(bond_row)
    entries = [
        [crystal[symmetric_index(row_index, col_index)] for col_index in range(6)]
        for row_index in range(6)
    ]
    product = [
        [
            ordered_sum([bond[row_index][inner] * entries[inner][col_index] for inner in range(6)])
            for col_index in range(6)
        ]
        for row_index in range(6)
    ]
    rotated = [
        ordered_sum([product[row_index][inner] * bond[col_index][inner] for inner in range(6)])
        for row_index, col_index in upper_pairs
    ]
    return jnp.stack(rotated)


def accumulate(table, orient_rows, weight_rows):
    blocks = orient_rows.shape[0] // grain_block
    count_cells = orient_rows.shape[1]

    def absorb(carry, inputs):
        chosen, masses = inputs
        picked = jnp.take(table, chosen, axis=1)
        masses_wide = masses.astype(jnp.float32)
        return (
            (
                carry[0] + jnp.sum(picked * masses_wide[None], axis=1),
                carry[1] + jnp.sum(masses_wide, axis=0),
            ),
            None,
        )

    initial = (jnp.zeros((21, count_cells), jnp.float32), jnp.zeros((count_cells,), jnp.float32))
    result, unused = lax.scan(
        absorb,
        initial,
        (
            orient_rows.reshape(blocks, grain_block, count_cells),
            weight_rows.reshape(blocks, grain_block, count_cells),
        ),
    )
    return result


def derivative(padded, direction):
    interior = [padded.shape[0]] + [extent - 8 for extent in padded.shape[1:]]

    def window(offset):
        starts = [0, 4, 4, 4]
        starts[direction] = 4 + offset
        return lax.slice(
            padded, starts, [begin + extent for begin, extent in zip(starts, interior)]
        )

    result = stencil_weights[0] * (window(1) - window(-1))
    for order_index in range(1, 4):
        result = result + stencil_weights[order_index] * (
            window(order_index + 1) - window(-order_index - 1)
        )
    return result


def advance_velocity(velocity, padded_stress, density):
    along_x = derivative(jnp.stack([padded_stress[0], padded_stress[5], padded_stress[4]]), 1)
    along_y = derivative(jnp.stack([padded_stress[5], padded_stress[1], padded_stress[3]]), 2)
    along_z = derivative(jnp.stack([padded_stress[4], padded_stress[3], padded_stress[2]]), 3)
    return velocity + time_step * (along_x + along_y + along_z) / density[None]


def advance_stress(stress, padded_velocity, stiffness):
    grad_x = derivative(padded_velocity, 1)
    grad_y = derivative(padded_velocity, 2)
    grad_z = derivative(padded_velocity, 3)
    strain = [
        grad_x[0],
        grad_y[1],
        grad_z[2],
        grad_y[2] + grad_z[1],
        grad_x[2] + grad_z[0],
        grad_x[1] + grad_y[0],
    ]
    updated = []
    for row_index in range(6):
        change = ordered_sum(
            [
                stiffness[symmetric_index(row_index, col_index)] * strain[col_index]
                for col_index in range(6)
            ]
        )
        updated.append(stress[row_index] + time_step * change)
    return jnp.stack(updated)


def on_device_general(euler_table, crystal, orient, weight, cell_map, density, velocity, stress):
    part_x = lax.axis_size("gx")
    part_y = lax.axis_size("gy")
    layers = lax.axis_size("ga")
    brick_x, brick_y, brick_z = (stress.shape[1], stress.shape[2], stress.shape[3])
    sub_x = brick_x // part_x
    sub_y = brick_y // part_y
    depth = brick_z * layers
    grains = orient.shape[0]
    count_cells = orient.shape[3]
    table = rotated_table(euler_table, crystal)
    summed, total = accumulate(
        table, orient.reshape(grains, count_cells), weight.reshape(grains, count_cells)
    )
    slots = cell_map.reshape(count_cells)
    layer_pos = slots % depth
    remainder = slots // depth
    sub_y_pos = remainder % sub_y
    remainder = remainder // sub_y
    brick_y_pos = remainder % part_y
    remainder = remainder // part_y
    sub_x_pos = remainder % sub_x
    brick_x_pos = remainder // sub_x
    target = (
        ((brick_x_pos * part_y + brick_y_pos) * sub_x + sub_x_pos) * sub_y + sub_y_pos
    ) * depth + layer_pos
    placed = jnp.zeros((21, count_cells), jnp.float32).at[:, target].set(summed)
    counted = jnp.zeros((count_cells,), jnp.float32).at[target].set(total)
    placed = placed.reshape(21, part_x * part_y, sub_x, sub_y, depth)
    counted = counted.reshape(part_x * part_y, sub_x, sub_y, depth)
    placed, counted = (
        lax.psum_scatter(placed, "ga", scatter_dimension=4, tiled=True),
        lax.psum_scatter(counted, "ga", scatter_dimension=3, tiled=True),
    )
    averaged = placed / counted[None]
    moved = lax.all_to_all(averaged, ("gx", "gy"), split_axis=1, concat_axis=1, tiled=True)
    moved = moved.reshape(21, part_x, part_y, sub_x, sub_y, brick_z)
    stiffness = moved.transpose(0, 1, 3, 2, 4, 5).reshape(21, brick_x, brick_y, brick_z)
    for step_index in range(STEPS):
        padded_stress = with_halo(stress, (("gx", 1), ("gy", 2), ("ga", 3)), 4)
        velocity = advance_velocity(velocity, padded_stress, density)
        padded_velocity = with_halo(velocity, (("gx", 1), ("gy", 2), ("ga", 3)), 4)
        stress = advance_stress(stress, padded_velocity, stiffness)
    return (stiffness, velocity, stress)


SUB = 8
LANES = 128
SUM_ROWS = 11
EDGE_ROWS = 6
FIELD_AT = SUM_ROWS + EDGE_ROWS
BLOCK_ROWS = FIELD_AT + 10
EDGE_AT = 192
WIDE_AT = EDGE_AT + 128
WIDE_ROWS = 48
FIELDS = 10
HALF = FIELDS // 2
LOW_ROWS = tuple(range(8)) + (16, 17, 18)
HIGH_ROWS = tuple(range(8, 16)) + (19, 20, 21)


def fits_plane(part_x, part_y, layers, orient, stress, euler_table):
    brick_x, brick_y, brick_z = stress.shape[1:]
    return (
        part_x % 2 == 0
        and part_y == 2
        and layers == 2
        and brick_x == SUB
        and part_x == SUB
        and brick_y == 4
        and brick_z == 8
        and orient.shape[3] == part_x * 64
        and orient.shape[0] % 8 == 0
        and euler_table.shape[1] % LANES == 0
    )


def lanes_of(shape):
    return lax.broadcasted_iota(jnp.int32, shape, len(shape) - 1)


def rows_of(shape):
    return lax.broadcasted_iota(jnp.int32, shape, len(shape) - 2)


def opposite_class(value, lane):
    value = jnp.where(
        (lane // 8) % 2 == 0, pltpu.roll(value, LANES - 8, 1), pltpu.roll(value, 8, 1)
    )
    return pltpu.roll(value, LANES // 2, 1)


def near_lanes(lane, row_half, layer):
    return (lane // 64 == row_half) | ((lane // 8) % 2 == layer)


def bond_matrix(trig):
    cos_one, cos_mid, cos_two, sin_one, sin_mid, sin_two = trig
    cos_two_mid = cos_two * cos_mid
    sin_two_mid = sin_two * cos_mid
    bunge = [
        [
            cos_one * cos_two - sin_one * sin_two_mid,
            sin_one * cos_two + cos_one * sin_two_mid,
            sin_two * sin_mid,
        ],
        [
            -cos_one * sin_two - sin_one * cos_two_mid,
            -sin_one * sin_two + cos_one * cos_two_mid,
            cos_two * sin_mid,
        ],
        [sin_one * sin_mid, -cos_one * sin_mid, cos_mid],
    ]
    rotation = [[bunge[col][row] for col in range(3)] for row in range(3)]
    bond = []
    for first, second in voigt_pairs:
        row = []
        for in_index, (third, fourth) in enumerate(voigt_pairs):
            if in_index < 3:
                row.append(rotation[first][third] * rotation[second][third])
            else:
                row.append(
                    rotation[first][third] * rotation[second][fourth]
                    + rotation[first][fourth] * rotation[second][third]
                )
        bond.append(row)
    return bond


def grain_kernel(
    crystal_hbm,
    euler_hbm,
    orient_hbm,
    weight_hbm,
    map_hbm,
    density_hbm,
    velocity_hbm,
    stress_hbm,
    send_ref,
    crystal_ref,
    euler_ref,
    orient_ref,
    weight_ref,
    map_ref,
    density_ref,
    velocity_ref,
    stress_ref,
    trig_ref,
    sums_ref,
    place_ref,
    acc_ref,
    arrived,
):
    row_part = lax.axis_index("gy")
    layer = lax.axis_index("ga")
    grains = weight_ref.shape[0]
    cells = weight_ref.shape[1]
    tiles = cells // LANES
    octets = grains // SUB
    table_tiles = euler_ref.shape[1] // LANES
    destinations = send_ref.shape[0] // BLOCK_ROWS

    copies = [
        pltpu.make_async_copy(source, target, arrived.at[at])
        for at, (source, target) in enumerate(
            [
                (euler_hbm, euler_ref),
                (orient_hbm, orient_ref),
                (weight_hbm, weight_ref),
                (crystal_hbm, crystal_ref),
                (map_hbm, map_ref),
                (stress_hbm, stress_ref),
                (velocity_hbm, velocity_ref),
                (density_hbm, density_ref),
            ]
        )
    ]
    for copy in copies:
        copy.start()
    sums_ref[...] = jnp.zeros_like(sums_ref)
    place_ref[...] = jnp.zeros_like(place_ref)

    copies[0].wait()
    angles = euler_ref[...]
    trig_ref[0:3, :] = jnp.cos(angles)
    trig_ref[3:6, :] = jnp.sin(angles)

    for copy in copies[1:4]:
        copy.wait()
    entries = [
        [crystal_ref[symmetric_index(row, col)] for col in range(6)] for row in range(6)
    ]
    row_of = {}
    for k in range(len(LOW_ROWS)):
        row_of[LOW_ROWS[k]] = k
        row_of[HIGH_ROWS[k]] = 16 + k

    def pick(tile, octet):
        index = orient_ref[pl.ds(octet * SUB * tiles + tile, SUB, stride=tiles), :]
        low, high = index & (LANES - 1), index >> 7
        values = [None] * 6
        for table_tile in range(table_tiles):
            here = high == table_tile
            for which in range(6):
                source = jnp.broadcast_to(
                    trig_ref[
                        which : which + 1, table_tile * LANES : (table_tile + 1) * LANES
                    ],
                    (SUB, LANES),
                )
                found = jnp.take_along_axis(source, low, axis=1, mode="promise_in_bounds")
                values[which] = found if table_tile == 0 else jnp.where(here, found, values[which])
        return values

    def one_tile(tile, unused):
        for octet in range(octets):
            bond = bond_matrix(pick(tile, octet))
            mass = weight_ref[
                octet * SUB : (octet + 1) * SUB, pl.ds(pl.multiple_of(tile * LANES, LANES), LANES)
            ].astype(jnp.float32)
            pair = 0
            for row in range(6):
                product = [
                    ordered_sum([bond[row][inner] * entries[inner][col] for inner in range(6)])
                    * mass
                    for col in range(6)
                ]
                for col in range(row, 6):
                    value = ordered_sum([product[inner] * bond[col][inner] for inner in range(6)])
                    acc_ref[pair] = value if octet == 0 else acc_ref[pair] + value
                    pair += 1
            acc_ref[21] = mass if octet == 0 else acc_ref[21] + mass
        for pair in range(22):
            sums_ref[
                row_of[pair] : row_of[pair] + 1, pl.ds(pl.multiple_of(tile * LANES, LANES), LANES)
            ] = jnp.sum(acc_ref[pair], axis=0, keepdims=True)
        return unused

    lax.fori_loop(0, tiles, one_tile, 0)
    for copy in copies[4:]:
        copy.wait()

    slots = map_ref[...]
    half = cells // (cells // 32)
    for chunk in range(cells // half):
        wanted = rows_of((half, cells)) + chunk * half
        hit = jnp.where(jnp.broadcast_to(slots, (half, cells)) == wanted, 1.0, 0.0)
        start = pl.multiple_of(chunk * 2 * half + row_part * half, half)
        place_ref[pl.ds(start, half), :] = hit.astype(jnp.bfloat16)
    sums = sums_ref[...]
    part_one = sums.astype(jnp.bfloat16)
    rest = sums - part_one.astype(jnp.float32)
    part_two = rest.astype(jnp.bfloat16)
    part_three = (rest - part_two.astype(jnp.float32)).astype(jnp.bfloat16)
    parts = jnp.concatenate([part_one, part_two, part_three], axis=0)
    placed = lax.dot_general(
        parts, place_ref[...], (((1,), (1,)), ((), ())), preferred_element_type=jnp.float32
    )
    placed = placed[0:32] + placed[32:64] + placed[64:96]

    own = row_part * 2 + layer

    def field_rows(component, y):
        if component < 6:
            return stress_ref[pl.ds(component * 32 + y, SUB, stride=4), :]
        if component < 9:
            return velocity_ref[pl.ds((component - 6) * 32 + y, SUB, stride=4), :]
        return density_ref[pl.ds(y, SUB, stride=4), :]

    def spread(component, slot, into):
        goal = own ^ slot
        for y in range(4):
            start = (goal // 2) * 64 + y * 16 + (goal % 2) * 8
            narrow = jnp.concatenate(
                [field_rows(component, y), jnp.zeros((SUB, LANES - 8), jnp.float32)], axis=1
            )
            into = into + pltpu.roll(narrow, start, 1)
        return into

    nothing = jnp.zeros((SUB, LANES), jnp.float32)
    groups, tails = [], []
    for half in range(2):
        group, tail = nothing, nothing
        for slot in range(4):
            group = spread(half * HALF + slot, slot, group)
            piece = spread(half * HALF + 4, slot, nothing)
            tail = tail + (piece if slot == 0 else pltpu.roll(piece, SUB - 2 * slot, 0))
        groups.append(group)
        tails.append(tail[0:2])

    shift = 32 + row_part * 64
    bricks = destinations // 4
    lane = lanes_of((SUB, LANES))
    upper = lax.axis_index("gx") >= SUB // 2
    own_sums, edge_sums = [], []
    for brick in range(bricks):
        halves = [
            placed[at : at + 16, brick * LANES : (brick + 1) * LANES] for at in (0, 16)
        ]
        own_sums.append(halves[0] + pltpu.roll(halves[1], shift, 1))
        edge_sums.append(
            [
                half[0:8] + pltpu.roll(pltpu.roll(half, 16 - EDGE_ROWS, 0)[0:8], shift, 1)
                for half in halves
            ]
        )
    for brick in range(bricks):
        side = brick % 2
        before, after = brick - side - 1, brick - side + 2
        before = edge_sums[before][side] if before >= 0 else nothing
        after = edge_sums[after][side] if after < bricks else nothing
        near = jnp.where(upper, before, after)
        far = opposite_class(jnp.where(upper, after, before), lane)
        for inner in range(4):
            at = (brick * 4 + inner) * BLOCK_ROWS
            edge = jnp.where(near_lanes(lane, inner // 2, inner % 2), near, far)
            send_ref[at : at + SUM_ROWS, :] = own_sums[brick][0:SUM_ROWS]
            send_ref[at + SUM_ROWS : at + FIELD_AT, :] = edge[0:EDGE_ROWS]
            send_ref[at + FIELD_AT : at + FIELD_AT + SUB, :] = groups[side]
            send_ref[at + FIELD_AT + SUB : at + BLOCK_ROWS, :] = tails[side]


def plane_derivative(field, dim, lane):
    position = lane // 16 if dim == 1 else lane % 16
    extent = 8 if dim == 1 else 16
    unit = 16 if dim == 1 else 1
    total = None
    for order in range(1, 5):
        ahead = pltpu.roll(field, LANES - order * unit, 1)
        behind = pltpu.roll(field, order * unit, 1)
        term = stencil_weights[order - 1] * (
            jnp.where(position + order < extent, ahead, 0.0)
            - jnp.where(position - order >= 0, behind, 0.0)
        )
        total = term if total is None else total + term
    return total


def row_derivative(read, start, count):
    total = stencil_weights[0] * (read(start + 1, count) - read(start - 1, count))
    for order in range(2, 5):
        total = total + stencil_weights[order - 1] * (
            read(start + order, count) - read(start - order, count)
        )
    return total


def velocity_update(wide_stress, old_velocity, density, inside, count):
    lane = lanes_of((count, LANES))

    def along(component, dim):
        if dim == 0:
            return row_derivative(
                lambda at, size: wide_stress[component, at : at + size, :], 4, count
            )
        return plane_derivative(wide_stress[component, 4 : 4 + count, :], dim, lane)

    sums = [
        along(0, 0) + along(5, 1) + along(4, 2),
        along(5, 0) + along(1, 1) + along(3, 2),
        along(4, 0) + along(3, 1) + along(2, 2),
    ]
    return [
        jnp.where(inside, old_velocity[at] + time_step * sums[at] / density, 0.0)
        for at in range(3)
    ]


def stress_update(wide_velocity, start, old_stress, stiff):
    lane = lanes_of((SUB, LANES))

    def along(component, dim):
        if dim == 0:
            return row_derivative(
                lambda at, size: wide_velocity[component, pl.ds(at, size), :], start, SUB
            )
        return plane_derivative(wide_velocity[component, pl.ds(start, SUB), :], dim, lane)

    strain = [
        along(0, 0),
        along(1, 1),
        along(2, 2),
        along(2, 1) + along(1, 2),
        along(2, 0) + along(0, 2),
        along(1, 0) + along(0, 1),
    ]
    return [
        old_stress[row]
        + time_step
        * ordered_sum([stiff(symmetric_index(row, col)) * strain[col] for col in range(6)])
        for row in range(6)
    ]


def inside_rows(brick, bricks, margin, count):
    place = rows_of((count, LANES)) - margin + brick * SUB
    return (place >= 0) & (place < bricks * SUB)


def unpack_kernel(got_ref, out_ref):
    brick = lax.axis_index("gx")
    bricks = got_ref.shape[0] // BLOCK_ROWS // 4

    def by_slot(zero, one):
        first_slot = (lanes_of(zero.shape) // 32) % 2 == 0
        low = jnp.where(first_slot, zero, one)
        high = jnp.where(first_slot, one, zero)
        high = jnp.where(first_slot, pltpu.roll(high, LANES - 32, 1), pltpu.roll(high, 32, 1))
        return low, high

    for p in range(bricks):

        def both_layers(part, offset, count):
            at = (p * 4 + part * 2) * BLOCK_ROWS + offset
            return got_ref[at : at + count, :] + got_ref[at + BLOCK_ROWS : at + BLOCK_ROWS + count, :]

        low, high = by_slot(both_layers(0, 0, SUM_ROWS), both_layers(1, 0, SUM_ROWS))
        total = jnp.broadcast_to(high[10:11], (SUB, LANES))
        out_ref[p * 24 : p * 24 + 8, :] = low[0:8] / total
        out_ref[p * 24 + 8 : p * 24 + 16, :] = high[0:8] / total
        out_ref[p * 24 + 16 : p * 24 + 19, :] = low[8:11] / total[0:3]
        out_ref[p * 24 + 19 : p * 24 + 22, :] = high[8:11] / total[0:3]
        low, high = by_slot(
            both_layers(0, SUM_ROWS, EDGE_ROWS), both_layers(1, SUM_ROWS, EDGE_ROWS)
        )
        at = EDGE_AT + p * 16
        out_ref[at : at + EDGE_ROWS, :] = low
        out_ref[at + EDGE_ROWS : at + SUM_ROWS, :] = high[0 : SUM_ROWS - EDGE_ROWS]

    def collect(source, offset, count, slot):
        lane = lanes_of((count, LANES))
        kind = (lane // 64) * 2 + (lane // 8) % 2
        pieces = [
            got_ref[pl.ds((source * 4 + (q ^ slot)) * BLOCK_ROWS + offset, count), :]
            for q in range(4)
        ]
        value = jnp.where(
            kind < 2,
            jnp.where(kind == 0, pieces[0], pieces[1]),
            jnp.where(kind == 2, pieces[2], pieces[3]),
        )
        if slot & 1:
            value = jnp.where(
                (lane // 8) % 2 == 0,
                pltpu.roll(value, LANES - 8, 1),
                pltpu.roll(value, 8, 1),
            )
        if slot & 2:
            value = pltpu.roll(value, 64, 1)
        return value

    for side in range(WIDE_ROWS // SUB):
        wanted = (brick // 2) * 2 + side - 2
        source = jnp.clip(wanted, 0, bricks - 1)
        valid = source == wanted
        for slot in range(4):
            at = WIDE_AT + slot * WIDE_ROWS + side * SUB
            value = collect(source, FIELD_AT, SUB, slot)
            out_ref[at : at + SUB, :] = jnp.where(valid, value, 0.0)
            at = WIDE_AT + 4 * WIDE_ROWS + side * SUB + 2 * slot
            value = collect(source, FIELD_AT + SUB, 2, slot)
            out_ref[at : at + 2, :] = jnp.where(valid, value, 0.0)


def stiffness_kernel(stiff_ref, out_ref, turned_ref):
    own = lax.axis_index("gy") * 64 + lax.axis_index("ga") * 8
    for p in range(SUB):
        turned_ref[...] = jnp.transpose(stiff_ref[p * 24 : (p + 1) * 24, :])
        for y in range(4):
            rows = pl.ds(pl.multiple_of(own + y * 16, 8), 8)
            out_ref[p * 32 + y * 8 : p * 32 + y * 8 + 8, :] = turned_ref[rows, 0:21]


def steps_kernel(
    own_ref,
    other_ref,
    out_velocity_ref,
    out_stress_ref,
    wide_ref,
    edge_ref,
    first_velocity_ref,
    first_stress_ref,
    last_velocity_ref,
    *,
    bricks,
):
    brick = lax.axis_index("gx")
    row_part, layer = lax.axis_index("gy"), lax.axis_index("ga")
    odd = brick % 2
    lane = lanes_of((SUB, LANES))
    row = rows_of((SUB, LANES))

    for at in range(HALF):
        rows = pl.ds(pl.multiple_of(WIDE_AT + at * WIDE_ROWS + odd * SUB, SUB), 5 * SUB)
        wide_ref[odd * HALF + at] = own_ref[rows, :]
        wide_ref[(1 - odd) * HALF + at] = other_ref[rows, :]

    edge_valid = jnp.where(odd == 0, brick - 1, brick + 1)
    edge_valid = (edge_valid >= 0) & (edge_valid < bricks)
    near_row = jnp.where(odd == 0, row, SUB - 1 - row) >= SUB // 2
    own_lane = (lane // 64 == row_part) & ((lane // 8) % 2 == layer)
    usable = (own_lane | (near_row & near_lanes(lane, row_part, layer))) & edge_valid

    def edge(half, k):
        rows = pl.ds(EDGE_AT + k, SUB, stride=16)
        value = jnp.where(odd == half, own_ref[rows, :], other_ref[rows, :])
        return jnp.where(near_row, value, opposite_class(value, lane))

    total = jnp.where(usable, edge(1, 10), 1.0)
    for half, named in enumerate((LOW_ROWS, HIGH_ROWS)):
        for k, pair in enumerate(named):
            if pair < 21:
                edge_ref[pair] = edge(half, k) / total

    inside = inside_rows(brick, bricks, 12, 32)
    density = jnp.where(inside, wide_ref[9, 4:36, :], 1.0)
    fresh = velocity_update(
        wide_ref, [wide_ref[6 + at, 4:36, :] for at in range(3)], density, inside, 32
    )
    for at in range(3):
        first_velocity_ref[at] = fresh[at]
    own_stiff = lambda pair: own_ref[pl.ds(pair, SUB, stride=24), :]
    for group, stiff, valid in (
        (SUB, own_stiff, None),
        (2 * SUB - odd * 2 * SUB, lambda pair: other_ref[pl.ds(pair, SUB, stride=24), :], None),
        (odd * 2 * SUB, lambda pair: edge_ref[pair], edge_valid),
    ):
        fresh = stress_update(
            first_velocity_ref,
            group + 4,
            [wide_ref[at, pl.ds(group + SUB, SUB), :] for at in range(6)],
            stiff,
        )
        for at in range(6):
            value = fresh[at] if valid is None else jnp.where(valid, fresh[at], 0.0)
            first_stress_ref[at, pl.ds(group, SUB), :] = value

    velocity = velocity_update(
        first_stress_ref,
        [first_velocity_ref[at, 8:24, :] for at in range(3)],
        density[8:24],
        inside_rows(brick, bricks, 4, 16),
        16,
    )
    for at in range(3):
        last_velocity_ref[at] = velocity[at]
    stress = stress_update(
        last_velocity_ref, 4, [first_stress_ref[at, 8:16, :] for at in range(6)], own_stiff
    )
    own = row_part * 64 + layer * 8

    def put(out_ref, at, value):
        for y in range(4):
            turned = pltpu.roll(value, (LANES - own - y * 16) % LANES, 1)
            out_ref[pl.ds(at * 32 + y, SUB, stride=4), :] = turned[:, 0:8]

    for at in range(3):
        put(out_velocity_ref, at, last_velocity_ref[at, 4:12, :])
    for at in range(6):
        put(out_stress_ref, at, stress[at])


def on_plane(euler_table, crystal, orient, weight, cell_map, density, velocity, stress):
    part_x = lax.axis_size("gx")
    devices = part_x * lax.axis_size("gy") * lax.axis_size("ga")
    grains, cells = orient.shape[0], orient.shape[3]
    tiles = cells // LANES
    octets = grains // SUB
    vmem = pl.BlockSpec(memory_space=pltpu.VMEM)
    hbm = pl.BlockSpec(memory_space=pltpu.HBM)
    f32 = jnp.float32

    send = pl.pallas_call(
        grain_kernel,
        out_shape=jax.ShapeDtypeStruct((devices * BLOCK_ROWS, LANES), f32),
        in_specs=[hbm] * 8,
        out_specs=vmem,
        scratch_shapes=[
            pltpu.SMEM((21,), f32),
            pltpu.VMEM(euler_table.shape, f32),
            pltpu.VMEM((grains * tiles, LANES), jnp.int32),
            pltpu.VMEM((grains, cells), weight.dtype),
            pltpu.VMEM((1, cells), jnp.int32),
            pltpu.VMEM((SUB * 4, 8), f32),
            pltpu.VMEM((3 * SUB * 4, 8), f32),
            pltpu.VMEM((6 * SUB * 4, 8), f32),
            pltpu.VMEM((SUB, euler_table.shape[1]), f32),
            pltpu.VMEM((32, cells), f32),
            pltpu.VMEM((2 * cells, cells), jnp.bfloat16),
            pltpu.VMEM((22, SUB, LANES), f32),
            pltpu.SemaphoreType.DMA((8,)),
        ],
        compiler_params=pltpu.CompilerParams(vmem_limit_bytes=8 * 2**20),
    )(*[pltpu.with_memory_space_constraint(x, pltpu.HBM) for x in (
        crystal,
        euler_table,
        orient.reshape(grains * tiles, LANES),
        weight.reshape(grains, cells),
        cell_map.reshape(1, cells),
        density.reshape(SUB * 4, 8),
        velocity.reshape(3 * SUB * 4, 8),
        stress.reshape(6 * SUB * 4, 8),
    )])
    got = lax.all_to_all(
        send.reshape(devices, 1, BLOCK_ROWS * LANES),
        ("gx", "gy", "ga"),
        split_axis=0,
        concat_axis=0,
        tiled=True,
    ).reshape(devices * BLOCK_ROWS, LANES)
    small = pltpu.CompilerParams(vmem_limit_bytes=8 * 2**20)
    own_part = pl.pallas_call(
        unpack_kernel,
        out_shape=jax.ShapeDtypeStruct((WIDE_AT + HALF * WIDE_ROWS, LANES), f32),
        in_specs=[vmem],
        out_specs=vmem,
        compiler_params=small,
    )(got)
    other_part = lax.ppermute(own_part, "gx", [(i, i ^ 1) for i in range(part_x)])
    stiffness = pl.pallas_call(
        stiffness_kernel,
        out_shape=jax.ShapeDtypeStruct((SUB * 4 * 8, 21), f32),
        in_specs=[vmem],
        out_specs=vmem,
        scratch_shapes=[pltpu.VMEM((LANES, 24), f32)],
        cost_estimate=pl.CostEstimate(flops=100000, bytes_accessed=200000, transcendentals=0),
        compiler_params=small,
    )(own_part)
    new_velocity, new_stress = pl.pallas_call(
        functools.partial(steps_kernel, bricks=part_x),
        out_shape=(
            jax.ShapeDtypeStruct((3 * SUB * 4, 8), f32),
            jax.ShapeDtypeStruct((6 * SUB * 4, 8), f32),
        ),
        in_specs=[vmem] * 2,
        out_specs=(vmem,) * 2,
        scratch_shapes=[
            pltpu.VMEM((FIELDS, 5 * SUB, LANES), f32),
            pltpu.VMEM((21, SUB, LANES), f32),
            pltpu.VMEM((3, 4 * SUB, LANES), f32),
            pltpu.VMEM((6, 3 * SUB, LANES), f32),
            pltpu.VMEM((3, 2 * SUB, LANES), f32),
        ],
        compiler_params=small,
    )(own_part, other_part)
    return (
        stiffness.reshape(SUB, 4, 8, 21).transpose(3, 0, 1, 2),
        new_velocity.reshape(3, SUB, 4, 8),
        new_stress.reshape(6, SUB, 4, 8),
    )


def on_device(euler_table, crystal, orient, weight, cell_map, density, velocity, stress):
    sizes = (lax.axis_size("gx"), lax.axis_size("gy"), lax.axis_size("ga"))
    form = on_plane if fits_plane(*sizes, orient, stress, euler_table) else on_device_general
    return form(euler_table, crystal, orient, weight, cell_map, density, velocity, stress)


def solution(mesh):
    return jax.shard_map(
        on_device,
        mesh=mesh,
        in_specs=(
            P(),
            P(),
            P("ga", "gx", "gy", None),
            P("ga", "gx", "gy", None),
            P("gx", "gy", None),
            P("gx", "gy", "ga"),
            P(None, "gx", "gy", "ga"),
            P(None, "gx", "gy", "ga"),
        ),
        out_specs=(P(None, "gx", "gy", "ga"), P(None, "gx", "gy", "ga"), P(None, "gx", "gy", "ga")),
        check_vma=False,
    )
```

```python
import functools

import jax
import jax.numpy as jnp
from jax import lax
from jax.experimental import pallas as pl
from jax.experimental.pallas import tpu as pltpu
from jax.sharding import PartitionSpec as P

STEPS = 2


stencil_weights = (0.8, -0.2, 4.0 / 105.0, -1.0 / 280.0)
time_step = 0.2
grain_block = 4
voigt_pairs = ((0, 0), (1, 1), (2, 2), (1, 2), (0, 2), (0, 1))
upper_pairs = [
    (row_index, col_index) for row_index in range(6) for col_index in range(row_index, 6)
]


def with_halo(cells, sides, width):
    for axis, dim in sides:
        count = lax.axis_size(axis)
        ends = count - 1
        head = lax.slice_in_dim(cells, 0, width, axis=dim)
        tail = lax.slice_in_dim(cells, cells.shape[dim] - width, cells.shape[dim], axis=dim)
        cells = jnp.concatenate(
            [
                lax.ppermute(tail, axis, [(i, (i + 1) % count) for i in range(ends)]),
                cells,
                lax.ppermute(head, axis, [((i + 1) % count, i) for i in range(ends)]),
            ],
            axis=dim,
        )
    return cells


def symmetric_index(first_index, second_index):
    return upper_pairs.index((min(first_index, second_index), max(first_index, second_index)))


def ordered_sum(summands):
    running = summands[0]
    for summand in summands[1:]:
        running = running + summand
    return running


def rotated_table(euler_table, crystal):
    cos_one, sin_one = (jnp.cos(euler_table[0]), jnp.sin(euler_table[0]))
    cos_mid, sin_mid = (jnp.cos(euler_table[1]), jnp.sin(euler_table[1]))
    cos_two, sin_two = (jnp.cos(euler_table[2]), jnp.sin(euler_table[2]))
    bunge = [
        [
            cos_one * cos_two - sin_one * sin_two * cos_mid,
            sin_one * cos_two + cos_one * sin_two * cos_mid,
            sin_two * sin_mid,
        ],
        [
            -cos_one * sin_two - sin_one * cos_two * cos_mid,
            -sin_one * sin_two + cos_one * cos_two * cos_mid,
            cos_two * sin_mid,
        ],
        [sin_one * sin_mid, -cos_one * sin_mid, cos_mid],
    ]
    rotation = [[bunge[col_index][row_index] for col_index in range(3)] for row_index in range(3)]
    bond = []
    for out_index in range(6):
        first, second = voigt_pairs[out_index]
        bond_row = []
        for in_index in range(6):
            third, fourth = voigt_pairs[in_index]
            if in_index < 3:
                bond_row.append(rotation[first][third] * rotation[second][third])
            else:
                bond_row.append(
                    rotation[first][third] * rotation[second][fourth]
                    + rotation[first][fourth] * rotation[second][third]
                )
        bond.append(bond_row)
    entries = [
        [crystal[symmetric_index(row_index, col_index)] for col_index in range(6)]
        for row_index in range(6)
    ]
    product = [
        [
            ordered_sum([bond[row_index][inner] * entries[inner][col_index] for inner in range(6)])
            for col_index in range(6)
        ]
        for row_index in range(6)
    ]
    rotated = [
        ordered_sum([product[row_index][inner] * bond[col_index][inner] for inner in range(6)])
        for row_index, col_index in upper_pairs
    ]
    return jnp.stack(rotated)


def accumulate(table, orient_rows, weight_rows):
    blocks = orient_rows.shape[0] // grain_block
    count_cells = orient_rows.shape[1]

    def absorb(carry, inputs):
        chosen, masses = inputs
        picked = jnp.take(table, chosen, axis=1)
        masses_wide = masses.astype(jnp.float32)
        return (
            (
                carry[0] + jnp.sum(picked * masses_wide[None], axis=1),
                carry[1] + jnp.sum(masses_wide, axis=0),
            ),
            None,
        )

    initial = (jnp.zeros((21, count_cells), jnp.float32), jnp.zeros((count_cells,), jnp.float32))
    result, unused = lax.scan(
        absorb,
        initial,
        (
            orient_rows.reshape(blocks, grain_block, count_cells),
            weight_rows.reshape(blocks, grain_block, count_cells),
        ),
    )
    return result


def derivative(padded, direction):
    interior = [padded.shape[0]] + [extent - 8 for extent in padded.shape[1:]]

    def window(offset):
        starts = [0, 4, 4, 4]
        starts[direction] = 4 + offset
        return lax.slice(
            padded, starts, [begin + extent for begin, extent in zip(starts, interior)]
        )

    result = stencil_weights[0] * (window(1) - window(-1))
    for order_index in range(1, 4):
        result = result + stencil_weights[order_index] * (
            window(order_index + 1) - window(-order_index - 1)
        )
    return result


def advance_velocity(velocity, padded_stress, density):
    along_x = derivative(jnp.stack([padded_stress[0], padded_stress[5], padded_stress[4]]), 1)
    along_y = derivative(jnp.stack([padded_stress[5], padded_stress[1], padded_stress[3]]), 2)
    along_z = derivative(jnp.stack([padded_stress[4], padded_stress[3], padded_stress[2]]), 3)
    return velocity + time_step * (along_x + along_y + along_z) / density[None]


def advance_stress(stress, padded_velocity, stiffness):
    grad_x = derivative(padded_velocity, 1)
    grad_y = derivative(padded_velocity, 2)
    grad_z = derivative(padded_velocity, 3)
    strain = [
        grad_x[0],
        grad_y[1],
        grad_z[2],
        grad_y[2] + grad_z[1],
        grad_x[2] + grad_z[0],
        grad_x[1] + grad_y[0],
    ]
    updated = []
    for row_index in range(6):
        change = ordered_sum(
            [
                stiffness[symmetric_index(row_index, col_index)] * strain[col_index]
                for col_index in range(6)
            ]
        )
        updated.append(stress[row_index] + time_step * change)
    return jnp.stack(updated)


def on_device_general(euler_table, crystal, orient, weight, cell_map, density, velocity, stress):
    part_x = lax.axis_size("gx")
    part_y = lax.axis_size("gy")
    layers = lax.axis_size("ga")
    brick_x, brick_y, brick_z = (stress.shape[1], stress.shape[2], stress.shape[3])
    sub_x = brick_x // part_x
    sub_y = brick_y // part_y
    depth = brick_z * layers
    grains = orient.shape[0]
    count_cells = orient.shape[3]
    table = rotated_table(euler_table, crystal)
    summed, total = accumulate(
        table, orient.reshape(grains, count_cells), weight.reshape(grains, count_cells)
    )
    slots = cell_map.reshape(count_cells)
    layer_pos = slots % depth
    remainder = slots // depth
    sub_y_pos = remainder % sub_y
    remainder = remainder // sub_y
    brick_y_pos = remainder % part_y
    remainder = remainder // part_y
    sub_x_pos = remainder % sub_x
    brick_x_pos = remainder // sub_x
    target = (
        ((brick_x_pos * part_y + brick_y_pos) * sub_x + sub_x_pos) * sub_y + sub_y_pos
    ) * depth + layer_pos
    placed = jnp.zeros((21, count_cells), jnp.float32).at[:, target].set(summed)
    counted = jnp.zeros((count_cells,), jnp.float32).at[target].set(total)
    placed = placed.reshape(21, part_x * part_y, sub_x, sub_y, depth)
    counted = counted.reshape(part_x * part_y, sub_x, sub_y, depth)
    placed, counted = (
        lax.psum_scatter(placed, "ga", scatter_dimension=4, tiled=True),
        lax.psum_scatter(counted, "ga", scatter_dimension=3, tiled=True),
    )
    averaged = placed / counted[None]
    moved = lax.all_to_all(averaged, ("gx", "gy"), split_axis=1, concat_axis=1, tiled=True)
    moved = moved.reshape(21, part_x, part_y, sub_x, sub_y, brick_z)
    stiffness = moved.transpose(0, 1, 3, 2, 4, 5).reshape(21, brick_x, brick_y, brick_z)
    for step_index in range(STEPS):
        padded_stress = with_halo(stress, (("gx", 1), ("gy", 2), ("ga", 3)), 4)
        velocity = advance_velocity(velocity, padded_stress, density)
        padded_velocity = with_halo(velocity, (("gx", 1), ("gy", 2), ("ga", 3)), 4)
        stress = advance_stress(stress, padded_velocity, stiffness)
    return (stiffness, velocity, stress)


SUB = 8
LANES = 128
SUM_ROWS = 11
EDGE_ROWS = 6
FIELD_AT = SUM_ROWS + EDGE_ROWS
BLOCK_ROWS = FIELD_AT + 10
EDGE_AT = 192
WIDE_AT = EDGE_AT + 128
WIDE_ROWS = 48
FIELDS = 10
HALF = FIELDS // 2
LOW_ROWS = tuple(range(8)) + (16, 17, 18)
HIGH_ROWS = tuple(range(8, 16)) + (19, 20, 21)


def fits_plane(part_x, part_y, layers, orient, stress, euler_table):
    brick_x, brick_y, brick_z = stress.shape[1:]
    return (
        part_x % 2 == 0
        and part_y == 2
        and layers == 2
        and brick_x == SUB
        and part_x == SUB
        and brick_y == 4
        and brick_z == 8
        and orient.shape[3] == part_x * 64
        and orient.shape[0] % 8 == 0
        and euler_table.shape[1] in [LANES << level for level in range(8)]
        and STEPS == 2
    )


def lanes_of(shape):
    return lax.broadcasted_iota(jnp.int32, shape, len(shape) - 1)


def rows_of(shape):
    return lax.broadcasted_iota(jnp.int32, shape, len(shape) - 2)


def opposite_class(value, lane):
    value = jnp.where(
        (lane // 8) % 2 == 0, pltpu.roll(value, LANES - 8, 1), pltpu.roll(value, 8, 1)
    )
    return pltpu.roll(value, LANES // 2, 1)


def near_lanes(lane, row_half, layer):
    return (lane // 64 == row_half) | ((lane // 8) % 2 == layer)


def cos_and_sin(angle):
    turns = jnp.floor(angle * 0.6366197723675814 + 0.5)
    rest = angle - turns * 1.5703125
    rest = rest - turns * 4.837512969970703e-4
    rest = rest - turns * 7.549789948768648e-8
    square = rest * rest
    sin_poly = (-1.9515295891e-4 * square + 8.3321608736e-3) * square - 1.6666654611e-1
    sin = rest + rest * square * sin_poly
    cos_poly = (2.443315711809948e-5 * square - 1.388731625493765e-3) * square
    cos = 1.0 - 0.5 * square + square * square * (cos_poly + 4.166664568298827e-2)
    quarter = turns.astype(jnp.int32)
    odd = (quarter & 1) == 1
    turned_cos, turned_sin = jnp.where(odd, sin, cos), jnp.where(odd, cos, sin)
    return (
        jnp.where(((quarter + 1) & 2) == 2, -turned_cos, turned_cos),
        jnp.where((quarter & 2) == 2, -turned_sin, turned_sin),
    )


def multiples(c, s):
    c2 = 2.0 * (c * c) - 1.0
    s2 = 2.0 * (c * s)
    return (
        (c, s),
        (c2, s2),
        (c2 * c - s2 * s, s2 * c + c2 * s),
        (2.0 * (c2 * c2) - 1.0, 2.0 * (c2 * s2)),
    )


def adapted(entries, axes):
    one, two, three, shear, first, second = axes
    at = lambda row, col: entries[(min(row, col), max(row, col))]
    mean = at(one, one) + at(two, two)
    cross = 2.0 * at(one, two)
    spread = mean - cross
    half_shear = 0.5 * at(shear, shear)
    half_spread = 0.5 * spread
    half_first = 0.5 * at(first, first)
    half_second = 0.5 * at(second, second)
    lone = lambda with_: (at(one, with_) + at(two, with_), at(one, with_) - at(two, with_))
    sum_three, diff_three = lone(three)
    sum_shear, diff_shear = lone(shear)
    sum_first, diff_first = lone(first)
    sum_second, diff_second = lone(second)
    fixed = (
        mean + cross,
        sum_three,
        at(three, three),
        half_spread + half_shear,
        half_first + half_second,
    )
    pairs = [
        (2, at(one, one) - at(two, two), sum_shear),
        (2, diff_three, at(three, shear)),
        (1, sum_first, sum_second),
        (1, at(three, first), at(three, second)),
        (4, half_spread - half_shear, diff_shear),
        (2, half_first - half_second, at(first, second)),
        (1, diff_first + at(shear, second), at(shear, first) - diff_second),
        (3, diff_first - at(shear, second), at(shear, first) + diff_second),
    ]
    return fixed, pairs


def turned(adapted_set, angles):
    fixed, pairs = adapted_set
    fresh = []
    for order, x, y in pairs:
        c, s = angles[order - 1]
        fresh.append((order, c * x - s * y, s * x + c * y))
    return fixed, fresh


def natural(adapted_set, axes):
    one, two, three, shear, first, second = axes
    (whole, sum_three, three_three, shear_mean, side_mean), pairs = adapted_set
    (
        (_, lean, sum_shear),
        (_, diff_three, three_shear),
        (_, sum_first, sum_second),
        (_, three_first, three_second),
        (_, shear_half, diff_shear),
        (_, side_half, first_second),
        (_, real_one, imag_one),
        (_, real_three, imag_three),
    ) = pairs
    spread = shear_mean + shear_half
    diff_first = 0.5 * (real_one + real_three)
    diff_second = 0.5 * (imag_three - imag_one)
    quarter = 0.25 * (whole + spread)
    half_lean = 0.5 * lean
    out = {}

    def put(row, col, value):
        out[(min(row, col), max(row, col))] = value

    put(one, one, quarter + half_lean)
    put(two, two, quarter - half_lean)
    put(one, two, 0.25 * (whole - spread))
    for with_, total, gap in (
        (three, sum_three, diff_three),
        (shear, sum_shear, diff_shear),
        (first, sum_first, diff_first),
        (second, sum_second, diff_second),
    ):
        put(one, with_, 0.5 * (total + gap))
        put(two, with_, 0.5 * (total - gap))
    put(three, three, three_three)
    put(three, shear, three_shear)
    put(three, first, three_first)
    put(three, second, three_second)
    put(shear, shear, shear_mean - shear_half)
    put(shear, first, 0.5 * (imag_one + imag_three))
    put(shear, second, 0.5 * (real_one - real_three))
    put(first, first, side_mean + side_half)
    put(second, second, side_mean - side_half)
    put(first, second, first_second)
    return out


about_z = (0, 1, 2, 5, 4, 3)
about_x = (1, 2, 0, 3, 5, 4)


def rotated_stiffness(entries, trig):
    cos_one, cos_mid, cos_two, sin_one, sin_mid, sin_two = trig
    first = turned(adapted(entries, about_z), multiples(cos_two, sin_two))
    middle = turned(adapted(natural(first, about_z), about_x), multiples(cos_mid, sin_mid))
    last = turned(adapted(natural(middle, about_x), about_z), multiples(cos_one, sin_one))
    return natural(last, about_z)


def grain_kernel(
    crystal_hbm,
    euler_hbm,
    orient_hbm,
    weight_hbm,
    map_hbm,
    density_hbm,
    velocity_hbm,
    stress_hbm,
    send_ref,
    crystal_ref,
    euler_ref,
    orient_ref,
    weight_ref,
    map_ref,
    density_ref,
    velocity_ref,
    stress_ref,
    trig_ref,
    sums_ref,
    place_ref,
    acc_ref,
    fields_ref,
    arrived,
):
    row_part = lax.axis_index("gy")
    layer = lax.axis_index("ga")
    grains = weight_ref.shape[0]
    cells = weight_ref.shape[1]
    tiles = cells // LANES
    octets = grains // SUB
    table_tiles = euler_ref.shape[1] // LANES
    destinations = send_ref.shape[0] // BLOCK_ROWS

    copies = [
        pltpu.make_async_copy(source, target, arrived.at[at])
        for at, (source, target) in enumerate(
            [
                (euler_hbm, euler_ref),
                (orient_hbm, orient_ref),
                (weight_hbm, weight_ref),
                (crystal_hbm, crystal_ref),
                (map_hbm, map_ref),
                (stress_hbm, stress_ref),
                (velocity_hbm, velocity_ref),
                (density_hbm, density_ref),
            ]
        )
    ]
    for copy in copies:
        copy.start()
    sums_ref[...] = jnp.zeros_like(sums_ref)
    place_ref[...] = jnp.zeros_like(place_ref)

    copies[0].wait()
    trig_ref[0:3, :], trig_ref[3:6, :] = cos_and_sin(euler_ref[...])

    for copy in copies[1:]:
        copy.wait()
    scale = (1.0, 1.0, 1.0, 2.0, 2.0, 2.0)
    entries = {
        (row, col): (scale[row] * scale[col]) * crystal_ref[pair]
        for pair, (row, col) in enumerate(upper_pairs)
    }
    row_of = {}
    for k in range(len(LOW_ROWS)):
        row_of[LOW_ROWS[k]] = k
        row_of[HIGH_ROWS[k]] = 16 + k

    def pick(tile, octet):
        index = orient_ref[pl.ds(octet * SUB * tiles + tile, SUB, stride=tiles), :]
        low = index & (LANES - 1)
        bits = [(index & (LANES << level)) != 0 for level in range(table_tiles.bit_length() - 1)]

        def find(which, first, level):
            if level == 0:
                source = jnp.broadcast_to(
                    trig_ref[which : which + 1, first * LANES : (first + 1) * LANES], (SUB, LANES)
                )
                return jnp.take_along_axis(source, low, axis=1, mode="promise_in_bounds")
            lower = find(which, first, level - 1)
            upper = find(which, first + (1 << (level - 1)), level - 1)
            return jnp.where(bits[level - 1], upper, lower)

        values = [find(which, 0, len(bits)) for which in range(6)]
        return values

    held = [pick(0, octet) for octet in range(octets)]

    slots = map_ref[...]
    half = 32
    for chunk in range(cells // half):
        wanted = rows_of((half, cells)) + chunk * half
        hit = jnp.where(jnp.broadcast_to(slots, (half, cells)) == wanted, 1.0, 0.0)
        start = pl.multiple_of(chunk * 2 * half + row_part * half, half)
        place_ref[pl.ds(start, half), :] = hit.astype(jnp.bfloat16)

    own = row_part * 2 + layer

    def field_rows(component, y):
        if component < 6:
            return stress_ref[pl.ds(component * 32 + y, SUB, stride=4), :]
        if component < 9:
            return velocity_ref[pl.ds((component - 6) * 32 + y, SUB, stride=4), :]
        return density_ref[pl.ds(y, SUB, stride=4), :]

    def spread(component, slot, into):
        goal = own ^ slot
        for y in range(4):
            start = (goal // 2) * 64 + y * 16 + (goal % 2) * 8
            narrow = jnp.concatenate(
                [field_rows(component, y), jnp.zeros((SUB, LANES - 8), jnp.float32)], axis=1
            )
            into = into + pltpu.roll(narrow, start, 1)
        return into

    nothing = jnp.zeros((SUB, LANES), jnp.float32)
    for half in range(2):
        group, tail = nothing, nothing
        for slot in range(4):
            group = spread(half * HALF + slot, slot, group)
            piece = spread(half * HALF + 4, slot, nothing)
            tail = tail + (piece if slot == 0 else pltpu.roll(piece, SUB - 2 * slot, 0))
        fields_ref[half, 0:SUB, :] = group
        fields_ref[half, SUB : SUB + 2, :] = tail[0:2]

    def add_tile(tile, held):
        lanes = slice(tile * LANES, (tile + 1) * LANES)
        for octet in range(octets):
            rotated = rotated_stiffness(entries, held[octet])
            mass = weight_ref[octet * SUB : (octet + 1) * SUB, lanes].astype(jnp.float32)
            masses = {1.0: mass, 0.5: 0.5 * mass, 0.25: 0.25 * mass}
            for pair, (row, col) in enumerate(upper_pairs):
                value = rotated[row, col] * masses[1.0 / (scale[row] * scale[col])]
                acc_ref[pair] = value if octet == 0 else acc_ref[pair] + value
            acc_ref[21] = mass if octet == 0 else acc_ref[21] + mass
        for pair in range(22):
            at = row_of[pair]
            sums_ref[at : at + 1, lanes] = jnp.sum(acc_ref[pair], axis=0, keepdims=True)

    def one_tile(tile, held):
        fresh = [pick(tile + 1, octet) for octet in range(octets)]
        add_tile(tile, held)
        return fresh

    for tile in range(tiles - 1):
        held = one_tile(tile, held)
    add_tile(tiles - 1, held)

    sums = sums_ref[...]
    part_one = sums.astype(jnp.bfloat16)
    rest = sums - part_one.astype(jnp.float32)
    part_two = rest.astype(jnp.bfloat16)
    part_three = (rest - part_two.astype(jnp.float32)).astype(jnp.bfloat16)
    parts = jnp.concatenate([part_one, part_two, part_three], axis=0)
    placed = lax.dot_general(
        parts, place_ref[...], (((1,), (1,)), ((), ())), preferred_element_type=jnp.float32
    )
    placed = placed[0:32] + placed[32:64] + placed[64:96]

    shift = 32 + row_part * 64
    bricks = destinations // 4
    lane = lanes_of((SUB, LANES))
    upper = lax.axis_index("gx") >= SUB // 2
    own_sums, edge_sums = [], []
    for brick in range(bricks):
        halves = [
            placed[at : at + 16, brick * LANES : (brick + 1) * LANES] for at in (0, 16)
        ]
        own_sums.append(halves[0] + pltpu.roll(halves[1], shift, 1))
        edge_sums.append(
            [
                half[0:8] + pltpu.roll(pltpu.roll(half, 16 - EDGE_ROWS, 0)[0:8], shift, 1)
                for half in halves
            ]
        )
    for brick in range(bricks):
        side = brick % 2
        before, after = brick - side - 1, brick - side + 2
        before = edge_sums[before][side] if before >= 0 else nothing
        after = edge_sums[after][side] if after < bricks else nothing
        near = jnp.where(upper, before, after)
        far = opposite_class(jnp.where(upper, after, before), lane)
        for inner in range(4):
            at = (brick * 4 + inner) * BLOCK_ROWS
            edge = jnp.where(near_lanes(lane, inner // 2, inner % 2), near, far)
            send_ref[at : at + SUM_ROWS, :] = own_sums[brick][0:SUM_ROWS]
            send_ref[at + SUM_ROWS : at + FIELD_AT, :] = edge[0:EDGE_ROWS]
            send_ref[at + FIELD_AT : at + FIELD_AT + SUB, :] = fields_ref[side, 0:SUB, :]
            send_ref[at + FIELD_AT + SUB : at + BLOCK_ROWS, :] = fields_ref[side, SUB : SUB + 2, :]


def plane_shifts(dim, count):
    lane = lanes_of((count, LANES))
    position, extent, unit = (lane // 16, 8, 16) if dim == 1 else (lane % 16, 16, 1)
    terms = {}
    for order in range(1, 5):
        weight = stencil_weights[order - 1]
        behind = jnp.where(position >= order, -weight, 0.0)
        ahead = jnp.where(position < extent - order, weight, 0.0)
        for shift, own in ((order * unit, behind), (LANES - order * unit, ahead)):
            terms[shift] = terms[shift] + own if shift in terms else own
    return list(terms.items())


def plane_derivative(field, shifts):
    return ordered_sum([weights * pltpu.roll(field, shift, 1) for shift, weights in shifts])


def row_derivative(read, start, count):
    total = stencil_weights[0] * (read(start + 1, count) - read(start - 1, count))
    for order in range(2, 5):
        total = total + stencil_weights[order - 1] * (
            read(start + order, count) - read(start - order, count)
        )
    return total


def velocity_update(wide_stress, old_velocity, density, inside, count):
    shifts = {dim: plane_shifts(dim, count) for dim in (1, 2)}

    def along(component, dim):
        if dim == 0:
            return row_derivative(
                lambda at, size: wide_stress[component, at : at + size, :], 4, count
            )
        return plane_derivative(wide_stress[component, 4 : 4 + count, :], shifts[dim])

    sums = [
        along(0, 0) + along(5, 1) + along(4, 2),
        along(5, 0) + along(1, 1) + along(3, 2),
        along(4, 0) + along(3, 1) + along(2, 2),
    ]
    return [
        jnp.where(inside, old_velocity[at] + time_step * sums[at] / density, 0.0)
        for at in range(3)
    ]


def stress_update(wide_velocity, start, old_stress, stiff):
    shifts = {dim: plane_shifts(dim, SUB) for dim in (1, 2)}

    def along(component, dim):
        if dim == 0:
            return row_derivative(
                lambda at, size: wide_velocity[component, pl.ds(at, size), :], start, SUB
            )
        return plane_derivative(wide_velocity[component, pl.ds(start, SUB), :], shifts[dim])

    strain = [
        along(0, 0),
        along(1, 1),
        along(2, 2),
        along(2, 1) + along(1, 2),
        along(2, 0) + along(0, 2),
        along(1, 0) + along(0, 1),
    ]
    return [
        old_stress[row]
        + time_step
        * ordered_sum([stiff(symmetric_index(row, col)) * strain[col] for col in range(6)])
        for row in range(6)
    ]


def inside_rows(brick, bricks, margin, count):
    place = rows_of((count, LANES)) - margin + brick * SUB
    return (place >= 0) & (place < bricks * SUB)


def unpack_kernel(got_ref, out_ref):
    brick = lax.axis_index("gx")
    bricks = got_ref.shape[0] // BLOCK_ROWS // 4

    def by_slot(zero, one):
        first_slot = (lanes_of(zero.shape) // 32) % 2 == 0
        low = jnp.where(first_slot, zero, one)
        high = jnp.where(first_slot, one, zero)
        high = jnp.where(first_slot, pltpu.roll(high, LANES - 32, 1), pltpu.roll(high, 32, 1))
        return low, high

    for p in range(bricks):

        def both_layers(part, offset, count):
            at = (p * 4 + part * 2) * BLOCK_ROWS + offset
            return got_ref[at : at + count, :] + got_ref[at + BLOCK_ROWS : at + BLOCK_ROWS + count, :]

        low, high = by_slot(both_layers(0, 0, SUM_ROWS), both_layers(1, 0, SUM_ROWS))
        total = jnp.broadcast_to(high[10:11], (SUB, LANES))
        out_ref[p * 24 : p * 24 + 8, :] = low[0:8] / total
        out_ref[p * 24 + 8 : p * 24 + 16, :] = high[0:8] / total
        out_ref[p * 24 + 16 : p * 24 + 19, :] = low[8:11] / total[0:3]
        out_ref[p * 24 + 19 : p * 24 + 22, :] = high[8:11] / total[0:3]
        low, high = by_slot(
            both_layers(0, SUM_ROWS, EDGE_ROWS), both_layers(1, SUM_ROWS, EDGE_ROWS)
        )
        at = EDGE_AT + p * 16
        out_ref[at : at + EDGE_ROWS, :] = low
        out_ref[at + EDGE_ROWS : at + SUM_ROWS, :] = high[0 : SUM_ROWS - EDGE_ROWS]

    def collect(source, offset, count, slot):
        lane = lanes_of((count, LANES))
        kind = (lane // 64) * 2 + (lane // 8) % 2
        pieces = [
            got_ref[pl.ds((source * 4 + (q ^ slot)) * BLOCK_ROWS + offset, count), :]
            for q in range(4)
        ]
        value = jnp.where(
            kind < 2,
            jnp.where(kind == 0, pieces[0], pieces[1]),
            jnp.where(kind == 2, pieces[2], pieces[3]),
        )
        if slot & 1:
            value = jnp.where(
                (lane // 8) % 2 == 0,
                pltpu.roll(value, LANES - 8, 1),
                pltpu.roll(value, 8, 1),
            )
        if slot & 2:
            value = pltpu.roll(value, 64, 1)
        return value

    for side in range(WIDE_ROWS // SUB):
        wanted = (brick // 2) * 2 + side - 2
        source = jnp.clip(wanted, 0, bricks - 1)
        valid = source == wanted
        for slot in range(4):
            at = WIDE_AT + slot * WIDE_ROWS + side * SUB
            value = collect(source, FIELD_AT, SUB, slot)
            out_ref[at : at + SUB, :] = jnp.where(valid, value, 0.0)
            at = WIDE_AT + 4 * WIDE_ROWS + side * SUB + 2 * slot
            value = collect(source, FIELD_AT + SUB, 2, slot)
            out_ref[at : at + 2, :] = jnp.where(valid, value, 0.0)


def stiffness_kernel(stiff_ref, out_ref, turned_ref):
    own = lax.axis_index("gy") * 64 + lax.axis_index("ga") * 8
    for p in range(SUB):
        turned_ref[...] = jnp.transpose(stiff_ref[p * 24 : (p + 1) * 24, :])
        for y in range(4):
            rows = pl.ds(pl.multiple_of(own + y * 16, 8), 8)
            out_ref[p * 32 + y * 8 : p * 32 + y * 8 + 8, :] = turned_ref[rows, 0:21]


def steps_kernel(
    own_ref,
    other_ref,
    out_velocity_ref,
    out_stress_ref,
    wide_ref,
    edge_ref,
    first_velocity_ref,
    first_stress_ref,
    last_velocity_ref,
    *,
    bricks,
):
    brick = lax.axis_index("gx")
    row_part, layer = lax.axis_index("gy"), lax.axis_index("ga")
    odd = brick % 2
    lane = lanes_of((SUB, LANES))
    row = rows_of((SUB, LANES))

    for at in range(HALF):
        rows = pl.ds(pl.multiple_of(WIDE_AT + at * WIDE_ROWS + odd * SUB, SUB), 5 * SUB)
        wide_ref[odd * HALF + at] = own_ref[rows, :]
        wide_ref[(1 - odd) * HALF + at] = other_ref[rows, :]

    edge_valid = jnp.where(odd == 0, brick - 1, brick + 1)
    edge_valid = (edge_valid >= 0) & (edge_valid < bricks)
    near_row = jnp.where(odd == 0, row, SUB - 1 - row) >= SUB // 2
    own_lane = (lane // 64 == row_part) & ((lane // 8) % 2 == layer)
    usable = (own_lane | (near_row & near_lanes(lane, row_part, layer))) & edge_valid

    def edge(half, k):
        rows = pl.ds(EDGE_AT + k, SUB, stride=16)
        value = jnp.where(odd == half, own_ref[rows, :], other_ref[rows, :])
        return jnp.where(near_row, value, opposite_class(value, lane))

    total = jnp.where(usable, edge(1, 10), 1.0)
    for half, named in enumerate((LOW_ROWS, HIGH_ROWS)):
        for k, pair in enumerate(named):
            if pair < 21:
                edge_ref[pair] = edge(half, k) / total

    inside = inside_rows(brick, bricks, 12, 32)
    density = jnp.where(inside, wide_ref[9, 4:36, :], 1.0)
    fresh = velocity_update(
        wide_ref, [wide_ref[6 + at, 4:36, :] for at in range(3)], density, inside, 32
    )
    for at in range(3):
        first_velocity_ref[at] = fresh[at]
    own_stiff = lambda pair: own_ref[pl.ds(pair, SUB, stride=24), :]
    for group, stiff, valid in (
        (SUB, own_stiff, None),
        (2 * SUB - odd * 2 * SUB, lambda pair: other_ref[pl.ds(pair, SUB, stride=24), :], None),
        (odd * 2 * SUB, lambda pair: edge_ref[pair], edge_valid),
    ):
        fresh = stress_update(
            first_velocity_ref,
            group + 4,
            [wide_ref[at, pl.ds(group + SUB, SUB), :] for at in range(6)],
            stiff,
        )
        for at in range(6):
            value = fresh[at] if valid is None else jnp.where(valid, fresh[at], 0.0)
            first_stress_ref[at, pl.ds(group, SUB), :] = value

    velocity = velocity_update(
        first_stress_ref,
        [first_velocity_ref[at, 8:24, :] for at in range(3)],
        density[8:24],
        inside_rows(brick, bricks, 4, 16),
        16,
    )
    for at in range(3):
        last_velocity_ref[at] = velocity[at]
    stress = stress_update(
        last_velocity_ref, 4, [first_stress_ref[at, 8:16, :] for at in range(6)], own_stiff
    )
    own = row_part * 64 + layer * 8

    def put(out_ref, at, value):
        for y in range(4):
            turned = pltpu.roll(value, (LANES - own - y * 16) % LANES, 1)
            out_ref[pl.ds(at * 32 + y, SUB, stride=4), :] = turned[:, 0:8]

    for at in range(3):
        put(out_velocity_ref, at, last_velocity_ref[at, 4:12, :])
    for at in range(6):
        put(out_stress_ref, at, stress[at])


def on_plane(euler_table, crystal, orient, weight, cell_map, density, velocity, stress):
    part_x = lax.axis_size("gx")
    devices = part_x * lax.axis_size("gy") * lax.axis_size("ga")
    grains, cells = orient.shape[0], orient.shape[3]
    tiles = cells // LANES
    octets = grains // SUB
    vmem = pl.BlockSpec(memory_space=pltpu.VMEM)
    hbm = pl.BlockSpec(memory_space=pltpu.HBM)
    f32 = jnp.float32

    send = pl.pallas_call(
        grain_kernel,
        out_shape=jax.ShapeDtypeStruct((devices * BLOCK_ROWS, LANES), f32),
        in_specs=[hbm] * 8,
        out_specs=vmem,
        scratch_shapes=[
            pltpu.SMEM((21,), f32),
            pltpu.VMEM(euler_table.shape, f32),
            pltpu.VMEM((grains * tiles, LANES), jnp.int32),
            pltpu.VMEM((grains, cells), weight.dtype),
            pltpu.VMEM((1, cells), jnp.int32),
            pltpu.VMEM((SUB * 4, 8), f32),
            pltpu.VMEM((3 * SUB * 4, 8), f32),
            pltpu.VMEM((6 * SUB * 4, 8), f32),
            pltpu.VMEM((SUB, euler_table.shape[1]), f32),
            pltpu.VMEM((32, cells), f32),
            pltpu.VMEM((2 * cells, cells), jnp.bfloat16),
            pltpu.VMEM((22, SUB, LANES), f32),
            pltpu.VMEM((2, 2 * SUB, LANES), f32),
            pltpu.SemaphoreType.DMA((8,)),
        ],
        compiler_params=pltpu.CompilerParams(vmem_limit_bytes=8 * 2**20),
    )(*[pltpu.with_memory_space_constraint(x, pltpu.HBM) for x in (
        crystal,
        euler_table,
        orient.reshape(grains * tiles, LANES),
        weight.reshape(grains, cells),
        cell_map.reshape(1, cells),
        density.reshape(SUB * 4, 8),
        velocity.reshape(3 * SUB * 4, 8),
        stress.reshape(6 * SUB * 4, 8),
    )])
    got = lax.all_to_all(
        send.reshape(devices, 1, BLOCK_ROWS * LANES),
        ("gx", "gy", "ga"),
        split_axis=0,
        concat_axis=0,
        tiled=True,
    ).reshape(devices * BLOCK_ROWS, LANES)
    small = pltpu.CompilerParams(vmem_limit_bytes=8 * 2**20)
    own_part = pl.pallas_call(
        unpack_kernel,
        out_shape=jax.ShapeDtypeStruct((WIDE_AT + HALF * WIDE_ROWS, LANES), f32),
        in_specs=[vmem],
        out_specs=vmem,
        compiler_params=small,
    )(got)
    other_part = lax.ppermute(own_part, "gx", [(i, i ^ 1) for i in range(part_x)])
    stiffness = pl.pallas_call(
        stiffness_kernel,
        out_shape=jax.ShapeDtypeStruct((SUB * 4 * 8, 21), f32),
        in_specs=[vmem],
        out_specs=vmem,
        scratch_shapes=[pltpu.VMEM((LANES, 24), f32)],
        cost_estimate=pl.CostEstimate(flops=100000, bytes_accessed=200000, transcendentals=0),
        compiler_params=small,
    )(own_part)
    new_velocity, new_stress = pl.pallas_call(
        functools.partial(steps_kernel, bricks=part_x),
        out_shape=(
            jax.ShapeDtypeStruct((3 * SUB * 4, 8), f32),
            jax.ShapeDtypeStruct((6 * SUB * 4, 8), f32),
        ),
        in_specs=[vmem] * 2,
        out_specs=(vmem,) * 2,
        scratch_shapes=[
            pltpu.VMEM((FIELDS, 5 * SUB, LANES), f32),
            pltpu.VMEM((21, SUB, LANES), f32),
            pltpu.VMEM((3, 4 * SUB, LANES), f32),
            pltpu.VMEM((6, 3 * SUB, LANES), f32),
            pltpu.VMEM((3, 2 * SUB, LANES), f32),
        ],
        compiler_params=small,
    )(own_part, other_part)
    return (
        stiffness.reshape(SUB, 4, 8, 21).transpose(3, 0, 1, 2),
        new_velocity.reshape(3, SUB, 4, 8),
        new_stress.reshape(6, SUB, 4, 8),
    )


def on_device(euler_table, crystal, orient, weight, cell_map, density, velocity, stress):
    sizes = (lax.axis_size("gx"), lax.axis_size("gy"), lax.axis_size("ga"))
    form = on_plane if fits_plane(*sizes, orient, stress, euler_table) else on_device_general
    return form(euler_table, crystal, orient, weight, cell_map, density, velocity, stress)


def solution(mesh):
    return jax.shard_map(
        on_device,
        mesh=mesh,
        in_specs=(
            P(),
            P(),
            P("ga", "gx", "gy", None),
            P("ga", "gx", "gy", None),
            P("gx", "gy", None),
            P("gx", "gy", "ga"),
            P(None, "gx", "gy", "ga"),
            P(None, "gx", "gy", "ga"),
        ),
        out_specs=(P(None, "gx", "gy", "ga"), P(None, "gx", "gy", "ga"), P(None, "gx", "gy", "ga")),
        check_vma=False,
    )
```

```python
import functools

import jax
import jax.numpy as jnp
from jax import lax
from jax.experimental import pallas as pl
from jax.experimental.pallas import tpu as pltpu
from jax.sharding import PartitionSpec as P

STEPS = 2


stencil_weights = (0.8, -0.2, 4.0 / 105.0, -1.0 / 280.0)
time_step = 0.2
grain_block = 4
voigt_pairs = ((0, 0), (1, 1), (2, 2), (1, 2), (0, 2), (0, 1))
upper_pairs = [
    (row_index, col_index) for row_index in range(6) for col_index in range(row_index, 6)
]


def with_halo(cells, sides, width):
    for axis, dim in sides:
        count = lax.axis_size(axis)
        ends = count - 1
        head = lax.slice_in_dim(cells, 0, width, axis=dim)
        tail = lax.slice_in_dim(cells, cells.shape[dim] - width, cells.shape[dim], axis=dim)
        cells = jnp.concatenate(
            [
                lax.ppermute(tail, axis, [(i, (i + 1) % count) for i in range(ends)]),
                cells,
                lax.ppermute(head, axis, [((i + 1) % count, i) for i in range(ends)]),
            ],
            axis=dim,
        )
    return cells


def symmetric_index(first_index, second_index):
    return upper_pairs.index((min(first_index, second_index), max(first_index, second_index)))


def ordered_sum(summands):
    running = summands[0]
    for summand in summands[1:]:
        running = running + summand
    return running


def rotated_table(euler_table, crystal):
    cos_one, sin_one = (jnp.cos(euler_table[0]), jnp.sin(euler_table[0]))
    cos_mid, sin_mid = (jnp.cos(euler_table[1]), jnp.sin(euler_table[1]))
    cos_two, sin_two = (jnp.cos(euler_table[2]), jnp.sin(euler_table[2]))
    bunge = [
        [
            cos_one * cos_two - sin_one * sin_two * cos_mid,
            sin_one * cos_two + cos_one * sin_two * cos_mid,
            sin_two * sin_mid,
        ],
        [
            -cos_one * sin_two - sin_one * cos_two * cos_mid,
            -sin_one * sin_two + cos_one * cos_two * cos_mid,
            cos_two * sin_mid,
        ],
        [sin_one * sin_mid, -cos_one * sin_mid, cos_mid],
    ]
    rotation = [[bunge[col_index][row_index] for col_index in range(3)] for row_index in range(3)]
    bond = []
    for out_index in range(6):
        first, second = voigt_pairs[out_index]
        bond_row = []
        for in_index in range(6):
            third, fourth = voigt_pairs[in_index]
            if in_index < 3:
                bond_row.append(rotation[first][third] * rotation[second][third])
            else:
                bond_row.append(
                    rotation[first][third] * rotation[second][fourth]
                    + rotation[first][fourth] * rotation[second][third]
                )
        bond.append(bond_row)
    entries = [
        [crystal[symmetric_index(row_index, col_index)] for col_index in range(6)]
        for row_index in range(6)
    ]
    product = [
        [
            ordered_sum([bond[row_index][inner] * entries[inner][col_index] for inner in range(6)])
            for col_index in range(6)
        ]
        for row_index in range(6)
    ]
    rotated = [
        ordered_sum([product[row_index][inner] * bond[col_index][inner] for inner in range(6)])
        for row_index, col_index in upper_pairs
    ]
    return jnp.stack(rotated)


def accumulate(table, orient_rows, weight_rows):
    blocks = orient_rows.shape[0] // grain_block
    count_cells = orient_rows.shape[1]

    def absorb(carry, inputs):
        chosen, masses = inputs
        picked = jnp.take(table, chosen, axis=1)
        masses_wide = masses.astype(jnp.float32)
        return (
            (
                carry[0] + jnp.sum(picked * masses_wide[None], axis=1),
                carry[1] + jnp.sum(masses_wide, axis=0),
            ),
            None,
        )

    initial = (jnp.zeros((21, count_cells), jnp.float32), jnp.zeros((count_cells,), jnp.float32))
    result, unused = lax.scan(
        absorb,
        initial,
        (
            orient_rows.reshape(blocks, grain_block, count_cells),
            weight_rows.reshape(blocks, grain_block, count_cells),
        ),
    )
    return result


def derivative(padded, direction):
    interior = [padded.shape[0]] + [extent - 8 for extent in padded.shape[1:]]

    def window(offset):
        starts = [0, 4, 4, 4]
        starts[direction] = 4 + offset
        return lax.slice(
            padded, starts, [begin + extent for begin, extent in zip(starts, interior)]
        )

    result = stencil_weights[0] * (window(1) - window(-1))
    for order_index in range(1, 4):
        result = result + stencil_weights[order_index] * (
            window(order_index + 1) - window(-order_index - 1)
        )
    return result


def advance_velocity(velocity, padded_stress, density):
    along_x = derivative(jnp.stack([padded_stress[0], padded_stress[5], padded_stress[4]]), 1)
    along_y = derivative(jnp.stack([padded_stress[5], padded_stress[1], padded_stress[3]]), 2)
    along_z = derivative(jnp.stack([padded_stress[4], padded_stress[3], padded_stress[2]]), 3)
    return velocity + time_step * (along_x + along_y + along_z) / density[None]


def advance_stress(stress, padded_velocity, stiffness):
    grad_x = derivative(padded_velocity, 1)
    grad_y = derivative(padded_velocity, 2)
    grad_z = derivative(padded_velocity, 3)
    strain = [
        grad_x[0],
        grad_y[1],
        grad_z[2],
        grad_y[2] + grad_z[1],
        grad_x[2] + grad_z[0],
        grad_x[1] + grad_y[0],
    ]
    updated = []
    for row_index in range(6):
        change = ordered_sum(
            [
                stiffness[symmetric_index(row_index, col_index)] * strain[col_index]
                for col_index in range(6)
            ]
        )
        updated.append(stress[row_index] + time_step * change)
    return jnp.stack(updated)


def on_device_general(euler_table, crystal, orient, weight, cell_map, density, velocity, stress):
    part_x = lax.axis_size("gx")
    part_y = lax.axis_size("gy")
    layers = lax.axis_size("ga")
    brick_x, brick_y, brick_z = (stress.shape[1], stress.shape[2], stress.shape[3])
    sub_x = brick_x // part_x
    sub_y = brick_y // part_y
    depth = brick_z * layers
    grains = orient.shape[0]
    count_cells = orient.shape[3]
    table = rotated_table(euler_table, crystal)
    summed, total = accumulate(
        table, orient.reshape(grains, count_cells), weight.reshape(grains, count_cells)
    )
    slots = cell_map.reshape(count_cells)
    layer_pos = slots % depth
    remainder = slots // depth
    sub_y_pos = remainder % sub_y
    remainder = remainder // sub_y
    brick_y_pos = remainder % part_y
    remainder = remainder // part_y
    sub_x_pos = remainder % sub_x
    brick_x_pos = remainder // sub_x
    target = (
        ((brick_x_pos * part_y + brick_y_pos) * sub_x + sub_x_pos) * sub_y + sub_y_pos
    ) * depth + layer_pos
    placed = jnp.zeros((21, count_cells), jnp.float32).at[:, target].set(summed)
    counted = jnp.zeros((count_cells,), jnp.float32).at[target].set(total)
    placed = placed.reshape(21, part_x * part_y, sub_x, sub_y, depth)
    counted = counted.reshape(part_x * part_y, sub_x, sub_y, depth)
    placed, counted = (
        lax.psum_scatter(placed, "ga", scatter_dimension=4, tiled=True),
        lax.psum_scatter(counted, "ga", scatter_dimension=3, tiled=True),
    )
    averaged = placed / counted[None]
    moved = lax.all_to_all(averaged, ("gx", "gy"), split_axis=1, concat_axis=1, tiled=True)
    moved = moved.reshape(21, part_x, part_y, sub_x, sub_y, brick_z)
    stiffness = moved.transpose(0, 1, 3, 2, 4, 5).reshape(21, brick_x, brick_y, brick_z)
    for step_index in range(STEPS):
        padded_stress = with_halo(stress, (("gx", 1), ("gy", 2), ("ga", 3)), 4)
        velocity = advance_velocity(velocity, padded_stress, density)
        padded_velocity = with_halo(velocity, (("gx", 1), ("gy", 2), ("ga", 3)), 4)
        stress = advance_stress(stress, padded_velocity, stiffness)
    return (stiffness, velocity, stress)


SUB = 8
LANES = 128
SUM_ROWS = 11
EDGE_ROWS = 6
FIELD_AT = SUM_ROWS + EDGE_ROWS
BLOCK_ROWS = FIELD_AT + 10
EDGE_AT = 192
WIDE_AT = EDGE_AT + 128
WIDE_ROWS = 48
FIELDS = 10
HALF = FIELDS // 2
LOW_ROWS = tuple(range(8)) + (16, 17, 18)
HIGH_ROWS = tuple(range(8, 16)) + (19, 20, 21)


def fits_plane(part_x, part_y, layers, orient, stress, euler_table):
    brick_x, brick_y, brick_z = stress.shape[1:]
    return (
        part_x % 2 == 0
        and part_y == 2
        and layers == 2
        and brick_x == SUB
        and part_x == SUB
        and brick_y == 4
        and brick_z == 8
        and orient.shape[3] == part_x * 64
        and orient.shape[0] % 8 == 0
        and euler_table.shape[1] in [LANES << level for level in range(8)]
        and STEPS == 2
    )


def lanes_of(shape):
    return lax.broadcasted_iota(jnp.int32, shape, len(shape) - 1)


def rows_of(shape):
    return lax.broadcasted_iota(jnp.int32, shape, len(shape) - 2)


def other_layer(value, lane):
    return jnp.where(
        (lane // 8) % 2 == 0, pltpu.roll(value, LANES - 8, 1), pltpu.roll(value, 8, 1)
    )


def opposite_class(value, lane):
    return pltpu.roll(other_layer(value, lane), LANES // 2, 1)


def sublane_sums(values):
    row = rows_of((SUB, LANES))
    values = values + [None] * (SUB - len(values))
    for step in (1, 2, 4):
        keep = (row // step) % 2 == 0
        merged = []
        for one, two in zip(values[0::2], values[1::2]):
            if one is None:
                merged.append(None)
                continue
            two = jnp.zeros_like(one) if two is None else two
            merged.append(
                jnp.where(keep, one, two) + pltpu.roll(jnp.where(keep, two, one), step, 0)
            )
        values = merged
    return values[0]


def near_lanes(lane, row_half, layer):
    return (lane // 64 == row_half) | ((lane // 8) % 2 == layer)


def cos_and_sin(angle):
    turns = jnp.floor(angle * 0.6366197723675814 + 0.5)
    rest = angle - turns * 1.5703125
    rest = rest - turns * 4.837512969970703e-4
    rest = rest - turns * 7.549789948768648e-8
    square = rest * rest
    sin_poly = (-1.9515295891e-4 * square + 8.3321608736e-3) * square - 1.6666654611e-1
    sin = rest + rest * square * sin_poly
    cos_poly = (2.443315711809948e-5 * square - 1.388731625493765e-3) * square
    cos = 1.0 - 0.5 * square + square * square * (cos_poly + 4.166664568298827e-2)
    quarter = turns.astype(jnp.int32)
    odd = (quarter & 1) == 1
    turned_cos, turned_sin = jnp.where(odd, sin, cos), jnp.where(odd, cos, sin)
    return (
        jnp.where(((quarter + 1) & 2) == 2, -turned_cos, turned_cos),
        jnp.where((quarter & 2) == 2, -turned_sin, turned_sin),
    )


def multiples(c, s):
    c2 = 2.0 * (c * c) - 1.0
    s2 = 2.0 * (c * s)
    return (
        (c, s),
        (c2, s2),
        (c2 * c - s2 * s, s2 * c + c2 * s),
        (2.0 * (c2 * c2) - 1.0, 2.0 * (c2 * s2)),
    )


def adapted(entries, axes):
    one, two, three, shear, first, second = axes
    at = lambda row, col: entries[(min(row, col), max(row, col))]
    mean = at(one, one) + at(two, two)
    cross = 2.0 * at(one, two)
    spread = mean - cross
    half_shear = 0.5 * at(shear, shear)
    half_spread = 0.5 * spread
    half_first = 0.5 * at(first, first)
    half_second = 0.5 * at(second, second)
    lone = lambda with_: (at(one, with_) + at(two, with_), at(one, with_) - at(two, with_))
    sum_three, diff_three = lone(three)
    sum_shear, diff_shear = lone(shear)
    sum_first, diff_first = lone(first)
    sum_second, diff_second = lone(second)
    fixed = (
        mean + cross,
        sum_three,
        at(three, three),
        half_spread + half_shear,
        half_first + half_second,
    )
    pairs = [
        (2, at(one, one) - at(two, two), sum_shear),
        (2, diff_three, at(three, shear)),
        (1, sum_first, sum_second),
        (1, at(three, first), at(three, second)),
        (4, half_spread - half_shear, diff_shear),
        (2, half_first - half_second, at(first, second)),
        (1, diff_first + at(shear, second), at(shear, first) - diff_second),
        (3, diff_first - at(shear, second), at(shear, first) + diff_second),
    ]
    return fixed, pairs


def turned(adapted_set, angles):
    fixed, pairs = adapted_set
    fresh = []
    for order, x, y in pairs:
        c, s = angles[order - 1]
        fresh.append((order, c * x - s * y, s * x + c * y))
    return fixed, fresh


def natural(adapted_set, axes):
    one, two, three, shear, first, second = axes
    (whole, sum_three, three_three, shear_mean, side_mean), pairs = adapted_set
    (
        (_, lean, sum_shear),
        (_, diff_three, three_shear),
        (_, sum_first, sum_second),
        (_, three_first, three_second),
        (_, shear_half, diff_shear),
        (_, side_half, first_second),
        (_, real_one, imag_one),
        (_, real_three, imag_three),
    ) = pairs
    spread = shear_mean + shear_half
    diff_first = 0.5 * (real_one + real_three)
    diff_second = 0.5 * (imag_three - imag_one)
    quarter = 0.25 * (whole + spread)
    half_lean = 0.5 * lean
    out = {}

    def put(row, col, value):
        out[(min(row, col), max(row, col))] = value

    put(one, one, quarter + half_lean)
    put(two, two, quarter - half_lean)
    put(one, two, 0.25 * (whole - spread))
    for with_, total, gap in (
        (three, sum_three, diff_three),
        (shear, sum_shear, diff_shear),
        (first, sum_first, diff_first),
        (second, sum_second, diff_second),
    ):
        put(one, with_, 0.5 * (total + gap))
        put(two, with_, 0.5 * (total - gap))
    put(three, three, three_three)
    put(three, shear, three_shear)
    put(three, first, three_first)
    put(three, second, three_second)
    put(shear, shear, shear_mean - shear_half)
    put(shear, first, 0.5 * (imag_one + imag_three))
    put(shear, second, 0.5 * (real_one - real_three))
    put(first, first, side_mean + side_half)
    put(second, second, side_mean - side_half)
    put(first, second, first_second)
    return out


about_z = (0, 1, 2, 5, 4, 3)
about_x = (1, 2, 0, 3, 5, 4)


def rotated_stiffness(entries, trig):
    cos_one, cos_mid, cos_two, sin_one, sin_mid, sin_two = trig
    first = turned(adapted(entries, about_z), multiples(cos_two, sin_two))
    middle = turned(adapted(natural(first, about_z), about_x), multiples(cos_mid, sin_mid))
    last = turned(adapted(natural(middle, about_x), about_z), multiples(cos_one, sin_one))
    return natural(last, about_z)


def grain_kernel(
    crystal_hbm,
    euler_hbm,
    orient_hbm,
    weight_hbm,
    map_hbm,
    density_hbm,
    velocity_hbm,
    stress_hbm,
    send_ref,
    crystal_ref,
    euler_ref,
    orient_ref,
    weight_ref,
    map_ref,
    density_ref,
    velocity_ref,
    stress_ref,
    sums_ref,
    place_ref,
    acc_ref,
    fields_ref,
    arrived,
):
    row_part = lax.axis_index("gy")
    layer = lax.axis_index("ga")
    grains = weight_ref.shape[0]
    cells = weight_ref.shape[1]
    tiles = cells // LANES
    octets = grains // SUB
    table_tiles = euler_ref.shape[1] // LANES
    destinations = send_ref.shape[0] // BLOCK_ROWS

    copies = [
        pltpu.make_async_copy(source, target, arrived.at[at])
        for at, (source, target) in enumerate(
            [
                (orient_hbm, orient_ref),
                (euler_hbm, euler_ref),
                (map_hbm, map_ref),
                (crystal_hbm, crystal_ref),
                (weight_hbm, weight_ref),
                (stress_hbm, stress_ref),
                (velocity_hbm, velocity_ref),
                (density_hbm, density_ref),
            ]
        )
    ]
    for copy in copies:
        copy.start()
    sums_ref[...] = jnp.zeros_like(sums_ref)
    place_ref[...] = jnp.zeros_like(place_ref)

    for copy in copies[:5]:
        copy.wait()
    scale = (1.0, 1.0, 1.0, 2.0, 2.0, 2.0)
    entries = {
        (row, col): (scale[row] * scale[col]) * crystal_ref[pair]
        for pair, (row, col) in enumerate(upper_pairs)
    }
    def pick(tile, octet):
        index = orient_ref[pl.ds(octet * SUB * tiles + tile, SUB, stride=tiles), :]
        low = index & (LANES - 1)
        bits = [(index & (LANES << level)) != 0 for level in range(table_tiles.bit_length() - 1)]

        def find(which, first, level):
            if level == 0:
                source = jnp.broadcast_to(
                    euler_ref[which : which + 1, first * LANES : (first + 1) * LANES], (SUB, LANES)
                )
                return jnp.take_along_axis(source, low, axis=1, mode="promise_in_bounds")
            lower = find(which, first, level - 1)
            upper = find(which, first + (1 << (level - 1)), level - 1)
            return jnp.where(bits[level - 1], upper, lower)

        values = [find(which, 0, len(bits)) for which in range(3)]
        return values

    held = [pick(0, octet) for octet in range(octets)]

    slots = map_ref[...]
    half = 32
    for chunk in range(cells // half):
        wanted = rows_of((half, cells)) + chunk * half
        hit = jnp.where(jnp.broadcast_to(slots, (half, cells)) == wanted, 1.0, 0.0)
        start = pl.multiple_of(chunk * 2 * half + row_part * half, half)
        place_ref[pl.ds(start, half), :] = hit.astype(jnp.bfloat16)

    def add_tile(tile, held):
        lanes = slice(tile * LANES, (tile + 1) * LANES)
        for octet in range(octets):
            turns = [cos_and_sin(angle) for angle in held[octet]]
            rotated = rotated_stiffness(entries, [turn[at] for at in range(2) for turn in turns])
            mass = weight_ref[octet * SUB : (octet + 1) * SUB, lanes].astype(jnp.float32)
            masses = {1.0: mass, 0.5: 0.5 * mass, 0.25: 0.25 * mass}
            for pair, (row, col) in enumerate(upper_pairs):
                value = rotated[row, col] * masses[1.0 / (scale[row] * scale[col])]
                acc_ref[pair] = value if octet == 0 else acc_ref[pair] + value
            acc_ref[21] = mass if octet == 0 else acc_ref[21] + mass
        for at, named in enumerate((LOW_ROWS, HIGH_ROWS)):
            for first in (0, SUB):
                summed = sublane_sums([acc_ref[pair] for pair in named[first : first + SUB]])
                sums_ref[at * 16 + first : at * 16 + first + SUB, lanes] = summed

    def one_tile(tile, held):
        fresh = [pick(tile + 1, octet) for octet in range(octets)]
        add_tile(tile, held)
        return fresh

    for tile in range(tiles // 2):
        held = one_tile(tile, held)

    for copy in copies[5:]:
        copy.wait()
    own = row_part * 2 + layer

    def field_rows(component, y):
        if component < 6:
            return stress_ref[pl.ds(component * 32 + y, SUB, stride=4), :]
        if component < 9:
            return velocity_ref[pl.ds((component - 6) * 32 + y, SUB, stride=4), :]
        return density_ref[pl.ds(y, SUB, stride=4), :]

    def spread(component, slot, into):
        goal = own ^ slot
        for y in range(4):
            start = (goal // 2) * 64 + y * 16 + (goal % 2) * 8
            narrow = jnp.concatenate(
                [field_rows(component, y), jnp.zeros((SUB, LANES - 8), jnp.float32)], axis=1
            )
            into = into + pltpu.roll(narrow, start, 1)
        return into

    nothing = jnp.zeros((SUB, LANES), jnp.float32)
    for half in range(2):
        group, tail = nothing, nothing
        for slot in (0, 1, 3, 2):
            group = spread(half * HALF + slot, slot, group)
            if slot == 0:
                piece = spread(half * HALF + 4, slot, nothing)
            elif slot == 3:
                piece = pltpu.roll(piece, LANES // 2, 1)
            else:
                piece = other_layer(piece, lanes_of((SUB, LANES)))
            tail = tail + (piece if slot == 0 else pltpu.roll(piece, SUB - 2 * slot, 0))
        fields_ref[half, 0:SUB, :] = group
        fields_ref[half, SUB : SUB + 2, :] = tail[0:2]

    for tile in range(tiles // 2, tiles - 1):
        held = one_tile(tile, held)
    add_tile(tiles - 1, held)

    sums = sums_ref[...]
    part_one = sums.astype(jnp.bfloat16)
    rest = sums - part_one.astype(jnp.float32)
    part_two = rest.astype(jnp.bfloat16)
    part_three = (rest - part_two.astype(jnp.float32)).astype(jnp.bfloat16)
    parts = jnp.concatenate([part_one, part_two, part_three], axis=0)
    placed = lax.dot_general(
        parts, place_ref[...], (((1,), (1,)), ((), ())), preferred_element_type=jnp.float32
    )
    placed = placed[0:32] + placed[32:64] + placed[64:96]

    shift = 32 + row_part * 64
    bricks = destinations // 4
    lane = lanes_of((SUB, LANES))
    upper = lax.axis_index("gx") >= SUB // 2
    own_sums, edge_sums = [], []
    for brick in range(bricks):
        halves = [
            placed[at : at + 16, brick * LANES : (brick + 1) * LANES] for at in (0, 16)
        ]
        own_sums.append(halves[0] + pltpu.roll(halves[1], shift, 1))
        edge_sums.append(
            [
                half[0:8] + pltpu.roll(pltpu.roll(half, 16 - EDGE_ROWS, 0)[0:8], shift, 1)
                for half in halves
            ]
        )
    for brick in range(bricks):
        side = brick % 2
        before, after = brick - side - 1, brick - side + 2
        before = edge_sums[before][side] if before >= 0 else nothing
        after = edge_sums[after][side] if after < bricks else nothing
        near = jnp.where(upper, before, after)
        far = opposite_class(jnp.where(upper, after, before), lane)
        for inner in range(4):
            at = (brick * 4 + inner) * BLOCK_ROWS
            edge = jnp.where(near_lanes(lane, inner // 2, inner % 2), near, far)
            send_ref[at : at + SUM_ROWS, :] = own_sums[brick][0:SUM_ROWS]
            send_ref[at + SUM_ROWS : at + FIELD_AT, :] = edge[0:EDGE_ROWS]
            send_ref[at + FIELD_AT : at + FIELD_AT + SUB, :] = fields_ref[side, 0:SUB, :]
            send_ref[at + FIELD_AT + SUB : at + BLOCK_ROWS, :] = fields_ref[side, SUB : SUB + 2, :]


def plane_shifts(dim, count):
    lane = lanes_of((count, LANES))
    position, extent, unit = (lane // 16, 8, 16) if dim == 1 else (lane % 16, 16, 1)
    terms = {}
    for order in range(1, 5):
        weight = stencil_weights[order - 1]
        behind = jnp.where(position >= order, -weight, 0.0)
        ahead = jnp.where(position < extent - order, weight, 0.0)
        for shift, own in ((order * unit, behind), (LANES - order * unit, ahead)):
            terms[shift] = terms[shift] + own if shift in terms else own
    return list(terms.items())


def plane_derivative(field, shifts):
    return ordered_sum([weights * pltpu.roll(field, shift, 1) for shift, weights in shifts])


def row_derivative(read, start, count):
    total = stencil_weights[0] * (read(start + 1, count) - read(start - 1, count))
    for order in range(2, 5):
        total = total + stencil_weights[order - 1] * (
            read(start + order, count) - read(start - order, count)
        )
    return total


def velocity_update(wide_stress, old_velocity, density, inside, count):
    shifts = {dim: plane_shifts(dim, count) for dim in (1, 2)}

    def along(component, dim):
        if dim == 0:
            return row_derivative(
                lambda at, size: wide_stress[component, at : at + size, :], 4, count
            )
        return plane_derivative(wide_stress[component, 4 : 4 + count, :], shifts[dim])

    sums = [
        along(0, 0) + along(5, 1) + along(4, 2),
        along(5, 0) + along(1, 1) + along(3, 2),
        along(4, 0) + along(3, 1) + along(2, 2),
    ]
    return [
        jnp.where(inside, old_velocity[at] + time_step * sums[at] / density, 0.0)
        for at in range(3)
    ]


def stress_update(wide_velocity, start, old_stress, stiff):
    shifts = {dim: plane_shifts(dim, SUB) for dim in (1, 2)}

    def along(component, dim):
        if dim == 0:
            return row_derivative(
                lambda at, size: wide_velocity[component, pl.ds(at, size), :], start, SUB
            )
        return plane_derivative(wide_velocity[component, pl.ds(start, SUB), :], shifts[dim])

    strain = [
        along(0, 0),
        along(1, 1),
        along(2, 2),
        along(2, 1) + along(1, 2),
        along(2, 0) + along(0, 2),
        along(1, 0) + along(0, 1),
    ]
    return [
        old_stress[row]
        + time_step
        * ordered_sum([stiff(symmetric_index(row, col)) * strain[col] for col in range(6)])
        for row in range(6)
    ]


def inside_rows(brick, bricks, margin, count):
    place = rows_of((count, LANES)) - margin + brick * SUB
    return (place >= 0) & (place < bricks * SUB)


def unpack_kernel(got_ref, out_ref):
    brick = lax.axis_index("gx")
    bricks = got_ref.shape[0] // BLOCK_ROWS // 4

    def by_slot(zero, one):
        first_slot = (lanes_of(zero.shape) // 32) % 2 == 0
        low = jnp.where(first_slot, zero, one)
        high = jnp.where(first_slot, one, zero)
        high = jnp.where(first_slot, pltpu.roll(high, LANES - 32, 1), pltpu.roll(high, 32, 1))
        return low, high

    for p in range(bricks):

        def both_layers(part, offset, count):
            at = (p * 4 + part * 2) * BLOCK_ROWS + offset
            return got_ref[at : at + count, :] + got_ref[at + BLOCK_ROWS : at + BLOCK_ROWS + count, :]

        low, high = by_slot(both_layers(0, 0, SUM_ROWS), both_layers(1, 0, SUM_ROWS))
        total = jnp.broadcast_to(high[10:11], (SUB, LANES))
        out_ref[p * 24 : p * 24 + 8, :] = low[0:8] / total
        out_ref[p * 24 + 8 : p * 24 + 16, :] = high[0:8] / total
        out_ref[p * 24 + 16 : p * 24 + 19, :] = low[8:11] / total[0:3]
        out_ref[p * 24 + 19 : p * 24 + 22, :] = high[8:11] / total[0:3]
        low, high = by_slot(
            both_layers(0, SUM_ROWS, EDGE_ROWS), both_layers(1, SUM_ROWS, EDGE_ROWS)
        )
        at = EDGE_AT + p * 16
        out_ref[at : at + EDGE_ROWS, :] = low
        out_ref[at + EDGE_ROWS : at + SUM_ROWS, :] = high[0 : SUM_ROWS - EDGE_ROWS]

    def collect(source, offset, count, slot):
        lane = lanes_of((count, LANES))
        kind = (lane // 64) * 2 + (lane // 8) % 2
        pieces = [
            got_ref[pl.ds((source * 4 + (q ^ slot)) * BLOCK_ROWS + offset, count), :]
            for q in range(4)
        ]
        value = jnp.where(
            kind < 2,
            jnp.where(kind == 0, pieces[0], pieces[1]),
            jnp.where(kind == 2, pieces[2], pieces[3]),
        )
        if slot & 1:
            value = jnp.where(
                (lane // 8) % 2 == 0,
                pltpu.roll(value, LANES - 8, 1),
                pltpu.roll(value, 8, 1),
            )
        if slot & 2:
            value = pltpu.roll(value, 64, 1)
        return value

    for side in range(WIDE_ROWS // SUB):
        wanted = (brick // 2) * 2 + side - 2
        source = jnp.clip(wanted, 0, bricks - 1)
        valid = source == wanted
        for slot in range(4):
            at = WIDE_AT + slot * WIDE_ROWS + side * SUB
            value = collect(source, FIELD_AT, SUB, slot)
            out_ref[at : at + SUB, :] = jnp.where(valid, value, 0.0)
            at = WIDE_AT + 4 * WIDE_ROWS + side * SUB + 2 * slot
            value = collect(source, FIELD_AT + SUB, 2, slot)
            out_ref[at : at + 2, :] = jnp.where(valid, value, 0.0)


def stiffness_kernel(stiff_ref, out_ref, turned_ref):
    own = lax.axis_index("gy") * 64 + lax.axis_index("ga") * 8
    for p in range(SUB):
        turned_ref[...] = jnp.transpose(stiff_ref[p * 24 : (p + 1) * 24, :])
        for y in range(4):
            rows = pl.ds(pl.multiple_of(own + y * 16, 8), 8)
            out_ref[p * 32 + y * 8 : p * 32 + y * 8 + 8, :] = turned_ref[rows, 0:21]


def steps_kernel(
    own_ref,
    other_ref,
    out_velocity_ref,
    out_stress_ref,
    wide_ref,
    edge_ref,
    first_velocity_ref,
    first_stress_ref,
    last_velocity_ref,
    *,
    bricks,
):
    brick = lax.axis_index("gx")
    row_part, layer = lax.axis_index("gy"), lax.axis_index("ga")
    odd = brick % 2
    lane = lanes_of((SUB, LANES))
    row = rows_of((SUB, LANES))

    for at in range(HALF):
        rows = pl.ds(pl.multiple_of(WIDE_AT + at * WIDE_ROWS + odd * SUB, SUB), 5 * SUB)
        wide_ref[odd * HALF + at] = own_ref[rows, :]
        wide_ref[(1 - odd) * HALF + at] = other_ref[rows, :]

    edge_valid = jnp.where(odd == 0, brick - 1, brick + 1)
    edge_valid = (edge_valid >= 0) & (edge_valid < bricks)
    near_row = jnp.where(odd == 0, row, SUB - 1 - row) >= SUB // 2
    own_lane = (lane // 64 == row_part) & ((lane // 8) % 2 == layer)
    usable = (own_lane | (near_row & near_lanes(lane, row_part, layer))) & edge_valid

    def edge(half, k):
        rows = pl.ds(EDGE_AT + k, SUB, stride=16)
        value = jnp.where(odd == half, own_ref[rows, :], other_ref[rows, :])
        return jnp.where(near_row, value, opposite_class(value, lane))

    total = jnp.where(usable, edge(1, 10), 1.0)
    for half, named in enumerate((LOW_ROWS, HIGH_ROWS)):
        for k, pair in enumerate(named):
            if pair < 21:
                edge_ref[pair] = edge(half, k) / total

    inside = inside_rows(brick, bricks, 12, 32)
    density = jnp.where(inside, wide_ref[9, 4:36, :], 1.0)
    fresh = velocity_update(
        wide_ref, [wide_ref[6 + at, 4:36, :] for at in range(3)], density, inside, 32
    )
    for at in range(3):
        first_velocity_ref[at] = fresh[at]
    own_stiff = lambda pair: own_ref[pl.ds(pair, SUB, stride=24), :]
    for group, stiff, valid in (
        (SUB, own_stiff, None),
        (2 * SUB - odd * 2 * SUB, lambda pair: other_ref[pl.ds(pair, SUB, stride=24), :], None),
        (odd * 2 * SUB, lambda pair: edge_ref[pair], edge_valid),
    ):
        fresh = stress_update(
            first_velocity_ref,
            group + 4,
            [wide_ref[at, pl.ds(group + SUB, SUB), :] for at in range(6)],
            stiff,
        )
        for at in range(6):
            value = fresh[at] if valid is None else jnp.where(valid, fresh[at], 0.0)
            first_stress_ref[at, pl.ds(group, SUB), :] = value

    velocity = velocity_update(
        first_stress_ref,
        [first_velocity_ref[at, 8:24, :] for at in range(3)],
        density[8:24],
        inside_rows(brick, bricks, 4, 16),
        16,
    )
    for at in range(3):
        last_velocity_ref[at] = velocity[at]
    stress = stress_update(
        last_velocity_ref, 4, [first_stress_ref[at, 8:16, :] for at in range(6)], own_stiff
    )
    own = row_part * 64 + layer * 8

    def put(out_ref, at, value):
        for y in range(4):
            turned = pltpu.roll(value, (LANES - own - y * 16) % LANES, 1)
            out_ref[pl.ds(at * 32 + y, SUB, stride=4), :] = turned[:, 0:8]

    for at in range(3):
        put(out_velocity_ref, at, last_velocity_ref[at, 4:12, :])
    for at in range(6):
        put(out_stress_ref, at, stress[at])


def on_plane(euler_table, crystal, orient, weight, cell_map, density, velocity, stress):
    part_x = lax.axis_size("gx")
    devices = part_x * lax.axis_size("gy") * lax.axis_size("ga")
    grains, cells = orient.shape[0], orient.shape[3]
    tiles = cells // LANES
    octets = grains // SUB
    vmem = pl.BlockSpec(memory_space=pltpu.VMEM)
    hbm = pl.BlockSpec(memory_space=pltpu.HBM)
    f32 = jnp.float32

    send = pl.pallas_call(
        grain_kernel,
        out_shape=jax.ShapeDtypeStruct((devices * BLOCK_ROWS, LANES), f32),
        in_specs=[hbm] * 8,
        out_specs=vmem,
        scratch_shapes=[
            pltpu.SMEM((21,), f32),
            pltpu.VMEM(euler_table.shape, f32),
            pltpu.VMEM((grains * tiles, LANES), jnp.int32),
            pltpu.VMEM((grains, cells), weight.dtype),
            pltpu.VMEM((1, cells), jnp.int32),
            pltpu.VMEM((SUB * 4, 8), f32),
            pltpu.VMEM((3 * SUB * 4, 8), f32),
            pltpu.VMEM((6 * SUB * 4, 8), f32),
            pltpu.VMEM((32, cells), f32),
            pltpu.VMEM((2 * cells, cells), jnp.bfloat16),
            pltpu.VMEM((22, SUB, LANES), f32),
            pltpu.VMEM((2, 2 * SUB, LANES), f32),
            pltpu.SemaphoreType.DMA((8,)),
        ],
        compiler_params=pltpu.CompilerParams(vmem_limit_bytes=8 * 2**20),
    )(*[pltpu.with_memory_space_constraint(x, pltpu.HBM) for x in (
        crystal,
        euler_table,
        orient.reshape(grains * tiles, LANES),
        weight.reshape(grains, cells),
        cell_map.reshape(1, cells),
        density.reshape(SUB * 4, 8),
        velocity.reshape(3 * SUB * 4, 8),
        stress.reshape(6 * SUB * 4, 8),
    )])
    got = lax.all_to_all(
        send.reshape(devices, 1, BLOCK_ROWS * LANES),
        ("gx", "gy", "ga"),
        split_axis=0,
        concat_axis=0,
        tiled=True,
    ).reshape(devices * BLOCK_ROWS, LANES)
    small = pltpu.CompilerParams(vmem_limit_bytes=8 * 2**20)
    own_part = pl.pallas_call(
        unpack_kernel,
        out_shape=jax.ShapeDtypeStruct((WIDE_AT + HALF * WIDE_ROWS, LANES), f32),
        in_specs=[vmem],
        out_specs=vmem,
        compiler_params=small,
    )(got)
    other_part = lax.ppermute(own_part, "gx", [(i, i ^ 1) for i in range(part_x)])
    stiffness = pl.pallas_call(
        stiffness_kernel,
        out_shape=jax.ShapeDtypeStruct((SUB * 4 * 8, 21), f32),
        in_specs=[vmem],
        out_specs=vmem,
        scratch_shapes=[pltpu.VMEM((LANES, 24), f32)],
        cost_estimate=pl.CostEstimate(flops=100000, bytes_accessed=200000, transcendentals=0),
        compiler_params=small,
    )(own_part)
    new_velocity, new_stress = pl.pallas_call(
        functools.partial(steps_kernel, bricks=part_x),
        out_shape=(
            jax.ShapeDtypeStruct((3 * SUB * 4, 8), f32),
            jax.ShapeDtypeStruct((6 * SUB * 4, 8), f32),
        ),
        in_specs=[vmem] * 2,
        out_specs=(vmem,) * 2,
        scratch_shapes=[
            pltpu.VMEM((FIELDS, 5 * SUB, LANES), f32),
            pltpu.VMEM((21, SUB, LANES), f32),
            pltpu.VMEM((3, 4 * SUB, LANES), f32),
            pltpu.VMEM((6, 3 * SUB, LANES), f32),
            pltpu.VMEM((3, 2 * SUB, LANES), f32),
        ],
        compiler_params=small,
    )(own_part, other_part)
    return (
        stiffness.reshape(SUB, 4, 8, 21).transpose(3, 0, 1, 2),
        new_velocity.reshape(3, SUB, 4, 8),
        new_stress.reshape(6, SUB, 4, 8),
    )


def on_device(euler_table, crystal, orient, weight, cell_map, density, velocity, stress):
    sizes = (lax.axis_size("gx"), lax.axis_size("gy"), lax.axis_size("ga"))
    form = on_plane if fits_plane(*sizes, orient, stress, euler_table) else on_device_general
    return form(euler_table, crystal, orient, weight, cell_map, density, velocity, stress)


def solution(mesh):
    return jax.shard_map(
        on_device,
        mesh=mesh,
        in_specs=(
            P(),
            P(),
            P("ga", "gx", "gy", None),
            P("ga", "gx", "gy", None),
            P("gx", "gy", None),
            P("gx", "gy", "ga"),
            P(None, "gx", "gy", "ga"),
            P(None, "gx", "gy", "ga"),
        ),
        out_specs=(P(None, "gx", "gy", "ga"), P(None, "gx", "gy", "ga"), P(None, "gx", "gy", "ga")),
        check_vma=False,
    )
```

```python
import functools

import jax
import jax.numpy as jnp
from jax import lax
from jax.experimental import pallas as pl
from jax.experimental.pallas import tpu as pltpu
from jax.sharding import PartitionSpec as P

STEPS = 2


stencil_weights = (0.8, -0.2, 4.0 / 105.0, -1.0 / 280.0)
time_step = 0.2
grain_block = 4
voigt_pairs = ((0, 0), (1, 1), (2, 2), (1, 2), (0, 2), (0, 1))
upper_pairs = [
    (row_index, col_index) for row_index in range(6) for col_index in range(row_index, 6)
]


def with_halo(cells, sides, width):
    for axis, dim in sides:
        count = lax.axis_size(axis)
        ends = count - 1
        head = lax.slice_in_dim(cells, 0, width, axis=dim)
        tail = lax.slice_in_dim(cells, cells.shape[dim] - width, cells.shape[dim], axis=dim)
        cells = jnp.concatenate(
            [
                lax.ppermute(tail, axis, [(i, (i + 1) % count) for i in range(ends)]),
                cells,
                lax.ppermute(head, axis, [((i + 1) % count, i) for i in range(ends)]),
            ],
            axis=dim,
        )
    return cells


def symmetric_index(first_index, second_index):
    return upper_pairs.index((min(first_index, second_index), max(first_index, second_index)))


def ordered_sum(summands):
    running = summands[0]
    for summand in summands[1:]:
        running = running + summand
    return running


def rotated_table(euler_table, crystal):
    cos_one, sin_one = (jnp.cos(euler_table[0]), jnp.sin(euler_table[0]))
    cos_mid, sin_mid = (jnp.cos(euler_table[1]), jnp.sin(euler_table[1]))
    cos_two, sin_two = (jnp.cos(euler_table[2]), jnp.sin(euler_table[2]))
    bunge = [
        [
            cos_one * cos_two - sin_one * sin_two * cos_mid,
            sin_one * cos_two + cos_one * sin_two * cos_mid,
            sin_two * sin_mid,
        ],
        [
            -cos_one * sin_two - sin_one * cos_two * cos_mid,
            -sin_one * sin_two + cos_one * cos_two * cos_mid,
            cos_two * sin_mid,
        ],
        [sin_one * sin_mid, -cos_one * sin_mid, cos_mid],
    ]
    rotation = [[bunge[col_index][row_index] for col_index in range(3)] for row_index in range(3)]
    bond = []
    for out_index in range(6):
        first, second = voigt_pairs[out_index]
        bond_row = []
        for in_index in range(6):
            third, fourth = voigt_pairs[in_index]
            if in_index < 3:
                bond_row.append(rotation[first][third] * rotation[second][third])
            else:
                bond_row.append(
                    rotation[first][third] * rotation[second][fourth]
                    + rotation[first][fourth] * rotation[second][third]
                )
        bond.append(bond_row)
    entries = [
        [crystal[symmetric_index(row_index, col_index)] for col_index in range(6)]
        for row_index in range(6)
    ]
    product = [
        [
            ordered_sum([bond[row_index][inner] * entries[inner][col_index] for inner in range(6)])
            for col_index in range(6)
        ]
        for row_index in range(6)
    ]
    rotated = [
        ordered_sum([product[row_index][inner] * bond[col_index][inner] for inner in range(6)])
        for row_index, col_index in upper_pairs
    ]
    return jnp.stack(rotated)


def accumulate(table, orient_rows, weight_rows):
    blocks = orient_rows.shape[0] // grain_block
    count_cells = orient_rows.shape[1]

    def absorb(carry, inputs):
        chosen, masses = inputs
        picked = jnp.take(table, chosen, axis=1)
        masses_wide = masses.astype(jnp.float32)
        return (
            (
                carry[0] + jnp.sum(picked * masses_wide[None], axis=1),
                carry[1] + jnp.sum(masses_wide, axis=0),
            ),
            None,
        )

    initial = (jnp.zeros((21, count_cells), jnp.float32), jnp.zeros((count_cells,), jnp.float32))
    result, unused = lax.scan(
        absorb,
        initial,
        (
            orient_rows.reshape(blocks, grain_block, count_cells),
            weight_rows.reshape(blocks, grain_block, count_cells),
        ),
    )
    return result


def derivative(padded, direction):
    interior = [padded.shape[0]] + [extent - 8 for extent in padded.shape[1:]]

    def window(offset):
        starts = [0, 4, 4, 4]
        starts[direction] = 4 + offset
        return lax.slice(
            padded, starts, [begin + extent for begin, extent in zip(starts, interior)]
        )

    result = stencil_weights[0] * (window(1) - window(-1))
    for order_index in range(1, 4):
        result = result + stencil_weights[order_index] * (
            window(order_index + 1) - window(-order_index - 1)
        )
    return result


def advance_velocity(velocity, padded_stress, density):
    along_x = derivative(jnp.stack([padded_stress[0], padded_stress[5], padded_stress[4]]), 1)
    along_y = derivative(jnp.stack([padded_stress[5], padded_stress[1], padded_stress[3]]), 2)
    along_z = derivative(jnp.stack([padded_stress[4], padded_stress[3], padded_stress[2]]), 3)
    return velocity + time_step * (along_x + along_y + along_z) / density[None]


def advance_stress(stress, padded_velocity, stiffness):
    grad_x = derivative(padded_velocity, 1)
    grad_y = derivative(padded_velocity, 2)
    grad_z = derivative(padded_velocity, 3)
    strain = [
        grad_x[0],
        grad_y[1],
        grad_z[2],
        grad_y[2] + grad_z[1],
        grad_x[2] + grad_z[0],
        grad_x[1] + grad_y[0],
    ]
    updated = []
    for row_index in range(6):
        change = ordered_sum(
            [
                stiffness[symmetric_index(row_index, col_index)] * strain[col_index]
                for col_index in range(6)
            ]
        )
        updated.append(stress[row_index] + time_step * change)
    return jnp.stack(updated)


def on_device_general(euler_table, crystal, orient, weight, cell_map, density, velocity, stress):
    part_x = lax.axis_size("gx")
    part_y = lax.axis_size("gy")
    layers = lax.axis_size("ga")
    brick_x, brick_y, brick_z = (stress.shape[1], stress.shape[2], stress.shape[3])
    sub_x = brick_x // part_x
    sub_y = brick_y // part_y
    depth = brick_z * layers
    grains = orient.shape[0]
    count_cells = orient.shape[3]
    table = rotated_table(euler_table, crystal)
    summed, total = accumulate(
        table, orient.reshape(grains, count_cells), weight.reshape(grains, count_cells)
    )
    slots = cell_map.reshape(count_cells)
    layer_pos = slots % depth
    remainder = slots // depth
    sub_y_pos = remainder % sub_y
    remainder = remainder // sub_y
    brick_y_pos = remainder % part_y
    remainder = remainder // part_y
    sub_x_pos = remainder % sub_x
    brick_x_pos = remainder // sub_x
    target = (
        ((brick_x_pos * part_y + brick_y_pos) * sub_x + sub_x_pos) * sub_y + sub_y_pos
    ) * depth + layer_pos
    placed = jnp.zeros((21, count_cells), jnp.float32).at[:, target].set(summed)
    counted = jnp.zeros((count_cells,), jnp.float32).at[target].set(total)
    placed = placed.reshape(21, part_x * part_y, sub_x, sub_y, depth)
    counted = counted.reshape(part_x * part_y, sub_x, sub_y, depth)
    placed, counted = (
        lax.psum_scatter(placed, "ga", scatter_dimension=4, tiled=True),
        lax.psum_scatter(counted, "ga", scatter_dimension=3, tiled=True),
    )
    averaged = placed / counted[None]
    moved = lax.all_to_all(averaged, ("gx", "gy"), split_axis=1, concat_axis=1, tiled=True)
    moved = moved.reshape(21, part_x, part_y, sub_x, sub_y, brick_z)
    stiffness = moved.transpose(0, 1, 3, 2, 4, 5).reshape(21, brick_x, brick_y, brick_z)
    for step_index in range(STEPS):
        padded_stress = with_halo(stress, (("gx", 1), ("gy", 2), ("ga", 3)), 4)
        velocity = advance_velocity(velocity, padded_stress, density)
        padded_velocity = with_halo(velocity, (("gx", 1), ("gy", 2), ("ga", 3)), 4)
        stress = advance_stress(stress, padded_velocity, stiffness)
    return (stiffness, velocity, stress)


SUB = 8
LANES = 128
SUM_ROWS = 11
EDGE_ROWS = 6
FIELD_AT = SUM_ROWS + EDGE_ROWS
BLOCK_ROWS = FIELD_AT + 10
EDGE_AT = 192
WIDE_AT = EDGE_AT + 128
WIDE_ROWS = 48
FIELDS = 10
HALF = FIELDS // 2
LOW_ROWS = tuple(range(8)) + (16, 17, 18)
HIGH_ROWS = tuple(range(8, 16)) + (19, 20, 21)


def fits_plane(part_x, part_y, layers, orient, stress, euler_table):
    brick_x, brick_y, brick_z = stress.shape[1:]
    return (
        part_x % 2 == 0
        and part_y == 2
        and layers == 2
        and brick_x == SUB
        and part_x == SUB
        and brick_y == 4
        and brick_z == 8
        and orient.shape[3] == part_x * 64
        and orient.shape[0] % 8 == 0
        and euler_table.shape[1] in [LANES << level for level in range(8)]
        and STEPS == 2
    )


def lanes_of(shape):
    return lax.broadcasted_iota(jnp.int32, shape, len(shape) - 1)


def rows_of(shape):
    return lax.broadcasted_iota(jnp.int32, shape, len(shape) - 2)


def other_layer(value, lane):
    return jnp.where(
        (lane // 8) % 2 == 0, pltpu.roll(value, LANES - 8, 1), pltpu.roll(value, 8, 1)
    )


def opposite_class(value, lane):
    return pltpu.roll(other_layer(value, lane), LANES // 2, 1)


def sublane_sums(values):
    row = rows_of((SUB, LANES))
    values = values + [None] * (SUB - len(values))
    for step in (1, 2, 4):
        keep = (row // step) % 2 == 0
        merged = []
        for one, two in zip(values[0::2], values[1::2]):
            if one is None:
                merged.append(None)
                continue
            two = jnp.zeros_like(one) if two is None else two
            merged.append(
                jnp.where(keep, one, two) + pltpu.roll(jnp.where(keep, two, one), step, 0)
            )
        values = merged
    return values[0]


def block_of(brick, inner, bricks):
    return (inner % 2) * bricks * 2 + brick * 2 + inner // 2


def near_lanes(lane, row_half, layer):
    return (lane // 64 == row_half) | ((lane // 8) % 2 == layer)


def cos_and_sin(angle):
    turns = jnp.floor(angle * 0.6366197723675814 + 0.5)
    rest = angle - turns * 1.5703125
    rest = rest - turns * 4.837512969970703e-4
    rest = rest - turns * 7.549789948768648e-8
    square = rest * rest
    sin_poly = (-1.9515295891e-4 * square + 8.3321608736e-3) * square - 1.6666654611e-1
    sin = rest + rest * square * sin_poly
    cos_poly = (2.443315711809948e-5 * square - 1.388731625493765e-3) * square
    cos = 1.0 - 0.5 * square + square * square * (cos_poly + 4.166664568298827e-2)
    quarter = turns.astype(jnp.int32)
    odd = (quarter & 1) == 1
    turned_cos, turned_sin = jnp.where(odd, sin, cos), jnp.where(odd, cos, sin)
    return (
        jnp.where(((quarter + 1) & 2) == 2, -turned_cos, turned_cos),
        jnp.where((quarter & 2) == 2, -turned_sin, turned_sin),
    )


def multiples(c, s):
    c2 = 2.0 * (c * c) - 1.0
    s2 = 2.0 * (c * s)
    return (
        (c, s),
        (c2, s2),
        (c2 * c - s2 * s, s2 * c + c2 * s),
        (2.0 * (c2 * c2) - 1.0, 2.0 * (c2 * s2)),
    )


def adapted(entries, axes):
    one, two, three, shear, first, second = axes
    at = lambda row, col: entries[(min(row, col), max(row, col))]
    mean = at(one, one) + at(two, two)
    cross = 2.0 * at(one, two)
    spread = mean - cross
    half_shear = 0.5 * at(shear, shear)
    half_spread = 0.5 * spread
    half_first = 0.5 * at(first, first)
    half_second = 0.5 * at(second, second)
    lone = lambda with_: (at(one, with_) + at(two, with_), at(one, with_) - at(two, with_))
    sum_three, diff_three = lone(three)
    sum_shear, diff_shear = lone(shear)
    sum_first, diff_first = lone(first)
    sum_second, diff_second = lone(second)
    fixed = (
        mean + cross,
        sum_three,
        at(three, three),
        half_spread + half_shear,
        half_first + half_second,
    )
    pairs = [
        (2, at(one, one) - at(two, two), sum_shear),
        (2, diff_three, at(three, shear)),
        (1, sum_first, sum_second),
        (1, at(three, first), at(three, second)),
        (4, half_spread - half_shear, diff_shear),
        (2, half_first - half_second, at(first, second)),
        (1, diff_first + at(shear, second), at(shear, first) - diff_second),
        (3, diff_first - at(shear, second), at(shear, first) + diff_second),
    ]
    return fixed, pairs


def turned(adapted_set, angles):
    fixed, pairs = adapted_set
    fresh = []
    for order, x, y in pairs:
        c, s = angles[order - 1]
        fresh.append((order, c * x - s * y, s * x + c * y))
    return fixed, fresh


def natural(adapted_set, axes):
    one, two, three, shear, first, second = axes
    (whole, sum_three, three_three, shear_mean, side_mean), pairs = adapted_set
    (
        (_, lean, sum_shear),
        (_, diff_three, three_shear),
        (_, sum_first, sum_second),
        (_, three_first, three_second),
        (_, shear_half, diff_shear),
        (_, side_half, first_second),
        (_, real_one, imag_one),
        (_, real_three, imag_three),
    ) = pairs
    spread = shear_mean + shear_half
    diff_first = 0.5 * (real_one + real_three)
    diff_second = 0.5 * (imag_three - imag_one)
    quarter = 0.25 * (whole + spread)
    half_lean = 0.5 * lean
    out = {}

    def put(row, col, value):
        out[(min(row, col), max(row, col))] = value

    put(one, one, quarter + half_lean)
    put(two, two, quarter - half_lean)
    put(one, two, 0.25 * (whole - spread))
    for with_, total, gap in (
        (three, sum_three, diff_three),
        (shear, sum_shear, diff_shear),
        (first, sum_first, diff_first),
        (second, sum_second, diff_second),
    ):
        put(one, with_, 0.5 * (total + gap))
        put(two, with_, 0.5 * (total - gap))
    put(three, three, three_three)
    put(three, shear, three_shear)
    put(three, first, three_first)
    put(three, second, three_second)
    put(shear, shear, shear_mean - shear_half)
    put(shear, first, 0.5 * (imag_one + imag_three))
    put(shear, second, 0.5 * (real_one - real_three))
    put(first, first, side_mean + side_half)
    put(second, second, side_mean - side_half)
    put(first, second, first_second)
    return out


about_z = (0, 1, 2, 5, 4, 3)
about_x = (1, 2, 0, 3, 5, 4)


def rotated_stiffness(entries, trig):
    cos_one, cos_mid, cos_two, sin_one, sin_mid, sin_two = trig
    first = turned(adapted(entries, about_z), multiples(cos_two, sin_two))
    middle = turned(adapted(natural(first, about_z), about_x), multiples(cos_mid, sin_mid))
    last = turned(adapted(natural(middle, about_x), about_z), multiples(cos_one, sin_one))
    return natural(last, about_z)


def grain_kernel(
    crystal_hbm,
    euler_hbm,
    orient_hbm,
    weight_hbm,
    map_hbm,
    density_hbm,
    velocity_hbm,
    stress_hbm,
    send_ref,
    crystal_ref,
    euler_ref,
    orient_ref,
    weight_ref,
    map_ref,
    density_ref,
    velocity_ref,
    stress_ref,
    sums_ref,
    place_ref,
    acc_ref,
    fields_ref,
    arrived,
):
    row_part = lax.axis_index("gy")
    layer = lax.axis_index("ga")
    grains = weight_ref.shape[0]
    cells = weight_ref.shape[1]
    tiles = cells // LANES
    octets = grains // SUB
    table_tiles = euler_ref.shape[1] // LANES
    destinations = send_ref.shape[0] // BLOCK_ROWS

    copies = [
        pltpu.make_async_copy(source, target, arrived.at[at])
        for at, (source, target) in enumerate(
            [
                (orient_hbm, orient_ref),
                (euler_hbm, euler_ref),
                (map_hbm, map_ref),
                (crystal_hbm, crystal_ref),
                (weight_hbm, weight_ref),
                (stress_hbm, stress_ref),
                (velocity_hbm, velocity_ref),
                (density_hbm, density_ref),
            ]
        )
    ]
    for copy in copies:
        copy.start()
    sums_ref[...] = jnp.zeros_like(sums_ref)
    place_ref[...] = jnp.zeros_like(place_ref)

    for copy in copies[:5]:
        copy.wait()
    scale = (1.0, 1.0, 1.0, 2.0, 2.0, 2.0)
    entries = {
        (row, col): (scale[row] * scale[col]) * crystal_ref[pair]
        for pair, (row, col) in enumerate(upper_pairs)
    }
    def pick(tile, octet):
        index = orient_ref[pl.ds(octet * SUB * tiles + tile, SUB, stride=tiles), :]
        low = index & (LANES - 1)
        bits = [(index & (LANES << level)) != 0 for level in range(table_tiles.bit_length() - 1)]

        def find(which, first, level):
            if level == 0:
                source = jnp.broadcast_to(
                    euler_ref[which : which + 1, first * LANES : (first + 1) * LANES], (SUB, LANES)
                )
                return jnp.take_along_axis(source, low, axis=1, mode="promise_in_bounds")
            lower = find(which, first, level - 1)
            upper = find(which, first + (1 << (level - 1)), level - 1)
            return jnp.where(bits[level - 1], upper, lower)

        values = [find(which, 0, len(bits)) for which in range(3)]
        return values

    held = [pick(0, octet) for octet in range(octets)]

    slots = map_ref[...]
    half = 32
    inner = jnp.where(
        jnp.broadcast_to(slots & (half - 1), (half, cells)) == rows_of((half, cells)), 1.0, 0.0
    ).astype(jnp.bfloat16)
    outer = jnp.broadcast_to(slots // half, (half, cells)).astype(jnp.bfloat16)
    for chunk in range(cells // half):
        start = pl.multiple_of(chunk * 2 * half + row_part * half, half)
        place_ref[pl.ds(start, half), :] = jnp.where(
            outer == jnp.bfloat16(chunk), inner, jnp.bfloat16(0.0)
        )

    def add_tile(tile, held):
        lanes = slice(tile * LANES, (tile + 1) * LANES)
        for octet in range(octets):
            turns = [cos_and_sin(angle) for angle in held[octet]]
            rotated = rotated_stiffness(entries, [turn[at] for at in range(2) for turn in turns])
            mass = weight_ref[octet * SUB : (octet + 1) * SUB, lanes].astype(jnp.float32)
            masses = {1.0: mass, 0.5: 0.5 * mass, 0.25: 0.25 * mass}
            for pair, (row, col) in enumerate(upper_pairs):
                value = rotated[row, col] * masses[1.0 / (scale[row] * scale[col])]
                acc_ref[pair] = value if octet == 0 else acc_ref[pair] + value
            acc_ref[21] = mass if octet == 0 else acc_ref[21] + mass
        for at, named in enumerate((LOW_ROWS, HIGH_ROWS)):
            for first in (0, SUB):
                summed = sublane_sums([acc_ref[pair] for pair in named[first : first + SUB]])
                sums_ref[at * 16 + first : at * 16 + first + SUB, lanes] = summed

    def one_tile(tile, held):
        fresh = [pick(tile + 1, octet) for octet in range(octets)]
        add_tile(tile, held)
        return fresh

    for tile in range(tiles // 2):
        held = one_tile(tile, held)

    for copy in copies[5:]:
        copy.wait()
    own = row_part * 2 + layer

    def field_rows(component, y):
        if component < 6:
            return stress_ref[pl.ds(component * 32 + y, SUB, stride=4), :]
        if component < 9:
            return velocity_ref[pl.ds((component - 6) * 32 + y, SUB, stride=4), :]
        return density_ref[pl.ds(y, SUB, stride=4), :]

    def spread(component, slot, into):
        goal = own ^ slot
        for y in range(4):
            start = (goal // 2) * 64 + y * 16 + (goal % 2) * 8
            narrow = jnp.concatenate(
                [field_rows(component, y), jnp.zeros((SUB, LANES - 8), jnp.float32)], axis=1
            )
            into = into + pltpu.roll(narrow, start, 1)
        return into

    nothing = jnp.zeros((SUB, LANES), jnp.float32)
    for half in range(2):
        group, tail = nothing, nothing
        for slot in (0, 1, 3, 2):
            group = spread(half * HALF + slot, slot, group)
            if slot == 0:
                piece = spread(half * HALF + 4, slot, nothing)
            elif slot == 3:
                piece = pltpu.roll(piece, LANES // 2, 1)
            else:
                piece = other_layer(piece, lanes_of((SUB, LANES)))
            tail = tail + (piece if slot == 0 else pltpu.roll(piece, SUB - 2 * slot, 0))
        fields_ref[half, 0:SUB, :] = group
        fields_ref[half, SUB : SUB + 2, :] = tail[0:2]

    for tile in range(tiles // 2, tiles - 1):
        held = one_tile(tile, held)
    add_tile(tiles - 1, held)

    sums = sums_ref[...]
    part_one = sums.astype(jnp.bfloat16)
    rest = sums - part_one.astype(jnp.float32)
    part_two = rest.astype(jnp.bfloat16)
    part_three = (rest - part_two.astype(jnp.float32)).astype(jnp.bfloat16)
    parts = jnp.concatenate([part_one, part_two, part_three], axis=0)
    placed = lax.dot_general(
        parts, place_ref[...], (((1,), (1,)), ((), ())), preferred_element_type=jnp.float32
    )
    placed = placed[0:32] + placed[32:64] + placed[64:96]

    shift = 32 + row_part * 64
    bricks = destinations // 4
    lane = lanes_of((SUB, LANES))
    upper = lax.axis_index("gx") >= SUB // 2
    own_sums, edge_sums = [], []
    for brick in range(bricks):
        halves = [
            placed[at : at + 16, brick * LANES : (brick + 1) * LANES] for at in (0, 16)
        ]
        own_sums.append(halves[0] + pltpu.roll(halves[1], shift, 1))
        edge_sums.append(
            [
                half[0:8] + pltpu.roll(pltpu.roll(half, 16 - EDGE_ROWS, 0)[0:8], shift, 1)
                for half in halves
            ]
        )
    for brick in range(bricks):
        side = brick % 2
        before, after = brick - side - 1, brick - side + 2
        before = edge_sums[before][side] if before >= 0 else nothing
        after = edge_sums[after][side] if after < bricks else nothing
        near = jnp.where(upper, before, after)
        far = opposite_class(jnp.where(upper, after, before), lane)
        for inner in range(4):
            at = block_of(brick, inner, bricks) * BLOCK_ROWS
            edge = jnp.where(near_lanes(lane, inner // 2, inner % 2), near, far)
            send_ref[at : at + SUM_ROWS, :] = own_sums[brick][0:SUM_ROWS]
            send_ref[at + SUM_ROWS : at + FIELD_AT, :] = edge[0:EDGE_ROWS]
            send_ref[at + FIELD_AT : at + FIELD_AT + SUB, :] = fields_ref[side, 0:SUB, :]
            send_ref[at + FIELD_AT + SUB : at + BLOCK_ROWS, :] = fields_ref[side, SUB : SUB + 2, :]


def plane_shifts(dim, count):
    lane = lanes_of((count, LANES))
    position, extent, unit = (lane // 16, 8, 16) if dim == 1 else (lane % 16, 16, 1)
    terms = {}
    for order in range(1, 5):
        weight = stencil_weights[order - 1]
        behind = jnp.where(position >= order, -weight, 0.0)
        ahead = jnp.where(position < extent - order, weight, 0.0)
        for shift, own in ((order * unit, behind), (LANES - order * unit, ahead)):
            terms[shift] = terms[shift] + own if shift in terms else own
    return list(terms.items())


def tree_sum(terms):
    while len(terms) > 1:
        paired = [one + two for one, two in zip(terms[0::2], terms[1::2])]
        terms = paired + terms[2 * len(paired) :]
    return terms[0]


def plane_derivative(field, shifts):
    return tree_sum([weights * pltpu.roll(field, shift, 1) for shift, weights in shifts])


def row_derivative(read, start, count):
    return tree_sum(
        [
            stencil_weights[order - 1] * (read(start + order, count) - read(start - order, count))
            for order in range(1, 5)
        ]
    )


def velocity_update(wide_stress, old_velocity, density, inside, count):
    shifts = {dim: plane_shifts(dim, count) for dim in (1, 2)}

    def along(component, dim):
        if dim == 0:
            return row_derivative(
                lambda at, size: wide_stress[component, at : at + size, :], 4, count
            )
        return plane_derivative(wide_stress[component, 4 : 4 + count, :], shifts[dim])

    sums = [
        along(0, 0) + along(5, 1) + along(4, 2),
        along(5, 0) + along(1, 1) + along(3, 2),
        along(4, 0) + along(3, 1) + along(2, 2),
    ]
    return [
        jnp.where(inside, old_velocity[at] + time_step * sums[at] / density, 0.0)
        for at in range(3)
    ]


def stress_update(wide_velocity, start, old_stress, stiff):
    shifts = {dim: plane_shifts(dim, SUB) for dim in (1, 2)}

    def along(component, dim):
        if dim == 0:
            return row_derivative(
                lambda at, size: wide_velocity[component, pl.ds(at, size), :], start, SUB
            )
        return plane_derivative(wide_velocity[component, pl.ds(start, SUB), :], shifts[dim])

    strain = [
        along(0, 0),
        along(1, 1),
        along(2, 2),
        along(2, 1) + along(1, 2),
        along(2, 0) + along(0, 2),
        along(1, 0) + along(0, 1),
    ]
    return [
        old_stress[row]
        + time_step
        * tree_sum([stiff(symmetric_index(row, col)) * strain[col] for col in range(6)])
        for row in range(6)
    ]


def inside_rows(brick, bricks, margin, count):
    place = rows_of((count, LANES)) - margin + brick * SUB
    return (place >= 0) & (place < bricks * SUB)


def unpack_kernel(got_ref, out_ref):
    brick = lax.axis_index("gx")
    bricks = got_ref.shape[0] // BLOCK_ROWS // 4

    def by_slot(zero, one):
        first_slot = (lanes_of(zero.shape) // 32) % 2 == 0
        low = jnp.where(first_slot, zero, one)
        high = jnp.where(first_slot, one, zero)
        high = jnp.where(first_slot, pltpu.roll(high, LANES - 32, 1), pltpu.roll(high, 32, 1))
        return low, high

    for p in range(bricks):

        def both_layers(part, offset, count):
            first, second = [
                block_of(p, part * 2 + layer, bricks) * BLOCK_ROWS + offset for layer in range(2)
            ]
            return got_ref[first : first + count, :] + got_ref[second : second + count, :]

        low, high = by_slot(both_layers(0, 0, SUM_ROWS), both_layers(1, 0, SUM_ROWS))
        total = jnp.broadcast_to(high[10:11], (SUB, LANES))
        out_ref[p * 24 : p * 24 + 8, :] = low[0:8] / total
        out_ref[p * 24 + 8 : p * 24 + 16, :] = high[0:8] / total
        out_ref[p * 24 + 16 : p * 24 + 19, :] = low[8:11] / total[0:3]
        out_ref[p * 24 + 19 : p * 24 + 22, :] = high[8:11] / total[0:3]
        low, high = by_slot(
            both_layers(0, SUM_ROWS, EDGE_ROWS), both_layers(1, SUM_ROWS, EDGE_ROWS)
        )
        at = EDGE_AT + p * 16
        out_ref[at : at + EDGE_ROWS, :] = low
        out_ref[at + EDGE_ROWS : at + SUM_ROWS, :] = high[0 : SUM_ROWS - EDGE_ROWS]

    def collect(source, offset, count, slot):
        lane = lanes_of((count, LANES))
        kind = (lane // 64) * 2 + (lane // 8) % 2
        pieces = [
            got_ref[pl.ds(block_of(source, q ^ slot, bricks) * BLOCK_ROWS + offset, count), :]
            for q in range(4)
        ]
        value = jnp.where(
            kind < 2,
            jnp.where(kind == 0, pieces[0], pieces[1]),
            jnp.where(kind == 2, pieces[2], pieces[3]),
        )
        if slot & 1:
            value = jnp.where(
                (lane // 8) % 2 == 0,
                pltpu.roll(value, LANES - 8, 1),
                pltpu.roll(value, 8, 1),
            )
        if slot & 2:
            value = pltpu.roll(value, 64, 1)
        return value

    for side in range(WIDE_ROWS // SUB):
        wanted = (brick // 2) * 2 + side - 2
        source = jnp.clip(wanted, 0, bricks - 1)
        valid = source == wanted
        for slot in range(4):
            at = WIDE_AT + slot * WIDE_ROWS + side * SUB
            value = collect(source, FIELD_AT, SUB, slot)
            out_ref[at : at + SUB, :] = jnp.where(valid, value, 0.0)
            at = WIDE_AT + 4 * WIDE_ROWS + side * SUB + 2 * slot
            value = collect(source, FIELD_AT + SUB, 2, slot)
            out_ref[at : at + 2, :] = jnp.where(valid, value, 0.0)


def stiffness_kernel(stiff_ref, out_ref, turned_ref):
    own = lax.axis_index("gy") * 64 + lax.axis_index("ga") * 8
    for p in range(SUB):
        turned_ref[...] = jnp.transpose(stiff_ref[p * 24 : (p + 1) * 24, :])
        for y in range(4):
            rows = pl.ds(pl.multiple_of(own + y * 16, 8), 8)
            out_ref[p * 32 + y * 8 : p * 32 + y * 8 + 8, :] = turned_ref[rows, 0:21]


def steps_kernel(
    own_ref,
    other_ref,
    out_velocity_ref,
    out_stress_ref,
    wide_ref,
    edge_ref,
    first_velocity_ref,
    first_stress_ref,
    last_velocity_ref,
    *,
    bricks,
):
    brick = lax.axis_index("gx")
    row_part, layer = lax.axis_index("gy"), lax.axis_index("ga")
    odd = brick % 2
    lane = lanes_of((SUB, LANES))
    row = rows_of((SUB, LANES))

    for at in range(HALF):
        rows = pl.ds(pl.multiple_of(WIDE_AT + at * WIDE_ROWS + odd * SUB, SUB), 5 * SUB)
        wide_ref[odd * HALF + at] = own_ref[rows, :]
        wide_ref[(1 - odd) * HALF + at] = other_ref[rows, :]

    edge_valid = jnp.where(odd == 0, brick - 1, brick + 1)
    edge_valid = (edge_valid >= 0) & (edge_valid < bricks)
    near_row = jnp.where(odd == 0, row, SUB - 1 - row) >= SUB // 2
    own_lane = (lane // 64 == row_part) & ((lane // 8) % 2 == layer)
    usable = (own_lane | (near_row & near_lanes(lane, row_part, layer))) & edge_valid

    def edge(half, k):
        rows = pl.ds(EDGE_AT + k, SUB, stride=16)
        value = jnp.where(odd == half, own_ref[rows, :], other_ref[rows, :])
        return jnp.where(near_row, value, opposite_class(value, lane))

    total = jnp.where(usable, edge(1, 10), 1.0)
    for half, named in enumerate((LOW_ROWS, HIGH_ROWS)):
        for k, pair in enumerate(named):
            if pair < 21:
                edge_ref[pair] = edge(half, k) / total

    inside = inside_rows(brick, bricks, 12, 32)
    density = jnp.where(inside, wide_ref[9, 4:36, :], 1.0)
    fresh = velocity_update(
        wide_ref, [wide_ref[6 + at, 4:36, :] for at in range(3)], density, inside, 32
    )
    for at in range(3):
        first_velocity_ref[at] = fresh[at]
    own_stiff = lambda pair: own_ref[pl.ds(pair, SUB, stride=24), :]
    for group, stiff, valid in (
        (SUB, own_stiff, None),
        (2 * SUB - odd * 2 * SUB, lambda pair: other_ref[pl.ds(pair, SUB, stride=24), :], None),
        (odd * 2 * SUB, lambda pair: edge_ref[pair], edge_valid),
    ):
        fresh = stress_update(
            first_velocity_ref,
            group + 4,
            [wide_ref[at, pl.ds(group + SUB, SUB), :] for at in range(6)],
            stiff,
        )
        for at in range(6):
            value = fresh[at] if valid is None else jnp.where(valid, fresh[at], 0.0)
            first_stress_ref[at, pl.ds(group, SUB), :] = value

    velocity = velocity_update(
        first_stress_ref,
        [first_velocity_ref[at, 8:24, :] for at in range(3)],
        density[8:24],
        inside_rows(brick, bricks, 4, 16),
        16,
    )
    for at in range(3):
        last_velocity_ref[at] = velocity[at]
    stress = stress_update(
        last_velocity_ref, 4, [first_stress_ref[at, 8:16, :] for at in range(6)], own_stiff
    )
    own = row_part * 64 + layer * 8

    def put(out_ref, at, value):
        for y in range(4):
            turned = pltpu.roll(value, (LANES - own - y * 16) % LANES, 1)
            out_ref[pl.ds(at * 32 + y, SUB, stride=4), :] = turned[:, 0:8]

    for at in range(3):
        put(out_velocity_ref, at, last_velocity_ref[at, 4:12, :])
    for at in range(6):
        put(out_stress_ref, at, stress[at])


def on_plane(euler_table, crystal, orient, weight, cell_map, density, velocity, stress):
    part_x = lax.axis_size("gx")
    devices = part_x * lax.axis_size("gy") * lax.axis_size("ga")
    grains, cells = orient.shape[0], orient.shape[3]
    tiles = cells // LANES
    octets = grains // SUB
    vmem = pl.BlockSpec(memory_space=pltpu.VMEM)
    hbm = pl.BlockSpec(memory_space=pltpu.HBM)
    f32 = jnp.float32

    send = pl.pallas_call(
        grain_kernel,
        out_shape=jax.ShapeDtypeStruct((devices * BLOCK_ROWS, LANES), f32),
        in_specs=[hbm] * 8,
        out_specs=vmem,
        scratch_shapes=[
            pltpu.SMEM((21,), f32),
            pltpu.VMEM(euler_table.shape, f32),
            pltpu.VMEM((grains * tiles, LANES), jnp.int32),
            pltpu.VMEM((grains, cells), weight.dtype),
            pltpu.VMEM((1, cells), jnp.int32),
            pltpu.VMEM((SUB * 4, 8), f32),
            pltpu.VMEM((3 * SUB * 4, 8), f32),
            pltpu.VMEM((6 * SUB * 4, 8), f32),
            pltpu.VMEM((32, cells), f32),
            pltpu.VMEM((2 * cells, cells), jnp.bfloat16),
            pltpu.VMEM((22, SUB, LANES), f32),
            pltpu.VMEM((2, 2 * SUB, LANES), f32),
            pltpu.SemaphoreType.DMA((8,)),
        ],
        compiler_params=pltpu.CompilerParams(vmem_limit_bytes=8 * 2**20),
    )(*[pltpu.with_memory_space_constraint(x, pltpu.HBM) for x in (
        crystal,
        euler_table,
        orient.reshape(grains * tiles, LANES),
        weight.reshape(grains, cells),
        cell_map.reshape(1, cells),
        density.reshape(SUB * 4, 8),
        velocity.reshape(3 * SUB * 4, 8),
        stress.reshape(6 * SUB * 4, 8),
    )])
    got = lax.all_to_all(
        send.reshape(devices, 1, BLOCK_ROWS * LANES),
        ("ga", "gx", "gy"),
        split_axis=0,
        concat_axis=0,
        tiled=True,
    ).reshape(devices * BLOCK_ROWS, LANES)
    small = pltpu.CompilerParams(vmem_limit_bytes=8 * 2**20)
    own_part = pl.pallas_call(
        unpack_kernel,
        out_shape=jax.ShapeDtypeStruct((WIDE_AT + HALF * WIDE_ROWS, LANES), f32),
        in_specs=[vmem],
        out_specs=vmem,
        compiler_params=small,
    )(got)
    other_part = lax.ppermute(own_part, "gx", [(i, i ^ 1) for i in range(part_x)])
    stiffness = pl.pallas_call(
        stiffness_kernel,
        out_shape=jax.ShapeDtypeStruct((SUB * 4 * 8, 21), f32),
        in_specs=[vmem],
        out_specs=vmem,
        scratch_shapes=[pltpu.VMEM((LANES, 24), f32)],
        cost_estimate=pl.CostEstimate(flops=100000, bytes_accessed=200000, transcendentals=0),
        compiler_params=small,
    )(own_part)
    new_velocity, new_stress = pl.pallas_call(
        functools.partial(steps_kernel, bricks=part_x),
        out_shape=(
            jax.ShapeDtypeStruct((3 * SUB * 4, 8), f32),
            jax.ShapeDtypeStruct((6 * SUB * 4, 8), f32),
        ),
        in_specs=[vmem] * 2,
        out_specs=(vmem,) * 2,
        scratch_shapes=[
            pltpu.VMEM((FIELDS, 5 * SUB, LANES), f32),
            pltpu.VMEM((21, SUB, LANES), f32),
            pltpu.VMEM((3, 4 * SUB, LANES), f32),
            pltpu.VMEM((6, 3 * SUB, LANES), f32),
            pltpu.VMEM((3, 2 * SUB, LANES), f32),
        ],
        compiler_params=small,
    )(own_part, other_part)
    return (
        stiffness.reshape(SUB, 4, 8, 21).transpose(3, 0, 1, 2),
        new_velocity.reshape(3, SUB, 4, 8),
        new_stress.reshape(6, SUB, 4, 8),
    )


def on_device(euler_table, crystal, orient, weight, cell_map, density, velocity, stress):
    sizes = (lax.axis_size("gx"), lax.axis_size("gy"), lax.axis_size("ga"))
    form = on_plane if fits_plane(*sizes, orient, stress, euler_table) else on_device_general
    return form(euler_table, crystal, orient, weight, cell_map, density, velocity, stress)


def solution(mesh):
    return jax.shard_map(
        on_device,
        mesh=mesh,
        in_specs=(
            P(),
            P(),
            P("ga", "gx", "gy", None),
            P("ga", "gx", "gy", None),
            P("gx", "gy", None),
            P("gx", "gy", "ga"),
            P(None, "gx", "gy", "ga"),
            P(None, "gx", "gy", "ga"),
        ),
        out_specs=(P(None, "gx", "gy", "ga"), P(None, "gx", "gy", "ga"), P(None, "gx", "gy", "ga")),
        check_vma=False,
    )
```

```python
import functools

import jax
import jax.numpy as jnp
from jax import lax
from jax.experimental import pallas as pl
from jax.experimental.pallas import tpu as pltpu
from jax.sharding import PartitionSpec as P

STEPS = 2


stencil_weights = (0.8, -0.2, 4.0 / 105.0, -1.0 / 280.0)
time_step = 0.2
grain_block = 4
voigt_pairs = ((0, 0), (1, 1), (2, 2), (1, 2), (0, 2), (0, 1))
upper_pairs = [
    (row_index, col_index) for row_index in range(6) for col_index in range(row_index, 6)
]


def with_halo(cells, sides, width):
    for axis, dim in sides:
        count = lax.axis_size(axis)
        ends = count - 1
        head = lax.slice_in_dim(cells, 0, width, axis=dim)
        tail = lax.slice_in_dim(cells, cells.shape[dim] - width, cells.shape[dim], axis=dim)
        cells = jnp.concatenate(
            [
                lax.ppermute(tail, axis, [(i, (i + 1) % count) for i in range(ends)]),
                cells,
                lax.ppermute(head, axis, [((i + 1) % count, i) for i in range(ends)]),
            ],
            axis=dim,
        )
    return cells


def symmetric_index(first_index, second_index):
    return upper_pairs.index((min(first_index, second_index), max(first_index, second_index)))


def ordered_sum(summands):
    running = summands[0]
    for summand in summands[1:]:
        running = running + summand
    return running


def rotated_table(euler_table, crystal):
    cos_one, sin_one = (jnp.cos(euler_table[0]), jnp.sin(euler_table[0]))
    cos_mid, sin_mid = (jnp.cos(euler_table[1]), jnp.sin(euler_table[1]))
    cos_two, sin_two = (jnp.cos(euler_table[2]), jnp.sin(euler_table[2]))
    bunge = [
        [
            cos_one * cos_two - sin_one * sin_two * cos_mid,
            sin_one * cos_two + cos_one * sin_two * cos_mid,
            sin_two * sin_mid,
        ],
        [
            -cos_one * sin_two - sin_one * cos_two * cos_mid,
            -sin_one * sin_two + cos_one * cos_two * cos_mid,
            cos_two * sin_mid,
        ],
        [sin_one * sin_mid, -cos_one * sin_mid, cos_mid],
    ]
    rotation = [[bunge[col_index][row_index] for col_index in range(3)] for row_index in range(3)]
    bond = []
    for out_index in range(6):
        first, second = voigt_pairs[out_index]
        bond_row = []
        for in_index in range(6):
            third, fourth = voigt_pairs[in_index]
            if in_index < 3:
                bond_row.append(rotation[first][third] * rotation[second][third])
            else:
                bond_row.append(
                    rotation[first][third] * rotation[second][fourth]
                    + rotation[first][fourth] * rotation[second][third]
                )
        bond.append(bond_row)
    entries = [
        [crystal[symmetric_index(row_index, col_index)] for col_index in range(6)]
        for row_index in range(6)
    ]
    product = [
        [
            ordered_sum([bond[row_index][inner] * entries[inner][col_index] for inner in range(6)])
            for col_index in range(6)
        ]
        for row_index in range(6)
    ]
    rotated = [
        ordered_sum([product[row_index][inner] * bond[col_index][inner] for inner in range(6)])
        for row_index, col_index in upper_pairs
    ]
    return jnp.stack(rotated)


def accumulate(table, orient_rows, weight_rows):
    blocks = orient_rows.shape[0] // grain_block
    count_cells = orient_rows.shape[1]

    def absorb(carry, inputs):
        chosen, masses = inputs
        picked = jnp.take(table, chosen, axis=1)
        masses_wide = masses.astype(jnp.float32)
        return (
            (
                carry[0] + jnp.sum(picked * masses_wide[None], axis=1),
                carry[1] + jnp.sum(masses_wide, axis=0),
            ),
            None,
        )

    initial = (jnp.zeros((21, count_cells), jnp.float32), jnp.zeros((count_cells,), jnp.float32))
    result, unused = lax.scan(
        absorb,
        initial,
        (
            orient_rows.reshape(blocks, grain_block, count_cells),
            weight_rows.reshape(blocks, grain_block, count_cells),
        ),
    )
    return result


def derivative(padded, direction):
    interior = [padded.shape[0]] + [extent - 8 for extent in padded.shape[1:]]

    def window(offset):
        starts = [0, 4, 4, 4]
        starts[direction] = 4 + offset
        return lax.slice(
            padded, starts, [begin + extent for begin, extent in zip(starts, interior)]
        )

    result = stencil_weights[0] * (window(1) - window(-1))
    for order_index in range(1, 4):
        result = result + stencil_weights[order_index] * (
            window(order_index + 1) - window(-order_index - 1)
        )
    return result


def advance_velocity(velocity, padded_stress, density):
    along_x = derivative(jnp.stack([padded_stress[0], padded_stress[5], padded_stress[4]]), 1)
    along_y = derivative(jnp.stack([padded_stress[5], padded_stress[1], padded_stress[3]]), 2)
    along_z = derivative(jnp.stack([padded_stress[4], padded_stress[3], padded_stress[2]]), 3)
    return velocity + time_step * (along_x + along_y + along_z) / density[None]


def advance_stress(stress, padded_velocity, stiffness):
    grad_x = derivative(padded_velocity, 1)
    grad_y = derivative(padded_velocity, 2)
    grad_z = derivative(padded_velocity, 3)
    strain = [
        grad_x[0],
        grad_y[1],
        grad_z[2],
        grad_y[2] + grad_z[1],
        grad_x[2] + grad_z[0],
        grad_x[1] + grad_y[0],
    ]
    updated = []
    for row_index in range(6):
        change = ordered_sum(
            [
                stiffness[symmetric_index(row_index, col_index)] * strain[col_index]
                for col_index in range(6)
            ]
        )
        updated.append(stress[row_index] + time_step * change)
    return jnp.stack(updated)


def on_device_general(euler_table, crystal, orient, weight, cell_map, density, velocity, stress):
    part_x = lax.axis_size("gx")
    part_y = lax.axis_size("gy")
    layers = lax.axis_size("ga")
    brick_x, brick_y, brick_z = (stress.shape[1], stress.shape[2], stress.shape[3])
    sub_x = brick_x // part_x
    sub_y = brick_y // part_y
    depth = brick_z * layers
    grains = orient.shape[0]
    count_cells = orient.shape[3]
    table = rotated_table(euler_table, crystal)
    summed, total = accumulate(
        table, orient.reshape(grains, count_cells), weight.reshape(grains, count_cells)
    )
    slots = cell_map.reshape(count_cells)
    layer_pos = slots % depth
    remainder = slots // depth
    sub_y_pos = remainder % sub_y
    remainder = remainder // sub_y
    brick_y_pos = remainder % part_y
    remainder = remainder // part_y
    sub_x_pos = remainder % sub_x
    brick_x_pos = remainder // sub_x
    target = (
        ((brick_x_pos * part_y + brick_y_pos) * sub_x + sub_x_pos) * sub_y + sub_y_pos
    ) * depth + layer_pos
    placed = jnp.zeros((21, count_cells), jnp.float32).at[:, target].set(summed)
    counted = jnp.zeros((count_cells,), jnp.float32).at[target].set(total)
    placed = placed.reshape(21, part_x * part_y, sub_x, sub_y, depth)
    counted = counted.reshape(part_x * part_y, sub_x, sub_y, depth)
    placed, counted = (
        lax.psum_scatter(placed, "ga", scatter_dimension=4, tiled=True),
        lax.psum_scatter(counted, "ga", scatter_dimension=3, tiled=True),
    )
    averaged = placed / counted[None]
    moved = lax.all_to_all(averaged, ("gx", "gy"), split_axis=1, concat_axis=1, tiled=True)
    moved = moved.reshape(21, part_x, part_y, sub_x, sub_y, brick_z)
    stiffness = moved.transpose(0, 1, 3, 2, 4, 5).reshape(21, brick_x, brick_y, brick_z)
    for step_index in range(STEPS):
        padded_stress = with_halo(stress, (("gx", 1), ("gy", 2), ("ga", 3)), 4)
        velocity = advance_velocity(velocity, padded_stress, density)
        padded_velocity = with_halo(velocity, (("gx", 1), ("gy", 2), ("ga", 3)), 4)
        stress = advance_stress(stress, padded_velocity, stiffness)
    return (stiffness, velocity, stress)


SUB = 8
LANES = 128
SUM_ROWS = 11
EDGE_ROWS = 6
FIELD_AT = SUM_ROWS + EDGE_ROWS
BLOCK_ROWS = FIELD_AT + 10
STIFF_ROWS = 22
EDGE_AT = STIFF_ROWS * SUB
WIDE_AT = EDGE_AT + SUM_ROWS * SUB
WIDE_ROWS = 48
FIELDS = 10
HALF = FIELDS // 2
LOW_ROWS = tuple(range(8)) + (16, 17, 18)
HIGH_ROWS = tuple(range(8, 16)) + (19, 20, 21)


def fits_plane(part_x, part_y, layers, orient, stress, euler_table):
    brick_x, brick_y, brick_z = stress.shape[1:]
    return (
        part_x % 2 == 0
        and part_y == 2
        and layers == 2
        and brick_x == SUB
        and part_x == SUB
        and brick_y == 4
        and brick_z == 8
        and orient.shape[3] == part_x * 64
        and orient.shape[0] % 8 == 0
        and euler_table.shape[1] in [LANES << level for level in range(8)]
        and STEPS == 2
    )


def lanes_of(shape):
    return lax.broadcasted_iota(jnp.int32, shape, len(shape) - 1)


def rows_of(shape):
    return lax.broadcasted_iota(jnp.int32, shape, len(shape) - 2)


def other_layer(value, lane):
    return jnp.where(
        (lane // 8) % 2 == 0, pltpu.roll(value, LANES - 8, 1), pltpu.roll(value, 8, 1)
    )


def opposite_class(value, lane):
    return pltpu.roll(other_layer(value, lane), LANES // 2, 1)


def sublane_sums(values):
    row = rows_of((SUB, LANES))
    values = values + [None] * (SUB - len(values))
    for step in (1, 2, 4):
        keep = (row // step) % 2 == 0
        merged = []
        for one, two in zip(values[0::2], values[1::2]):
            if one is None:
                merged.append(None)
                continue
            two = jnp.zeros_like(one) if two is None else two
            merged.append(
                jnp.where(keep, one, two) + pltpu.roll(jnp.where(keep, two, one), step, 0)
            )
        values = merged
    return values[0]


def block_of(brick, inner, bricks):
    return (inner % 2) * bricks * 2 + brick * 2 + inner // 2


def near_lanes(lane, row_half, layer):
    return (lane // 64 == row_half) | ((lane // 8) % 2 == layer)


def cos_and_sin(angle):
    turns = jnp.floor(angle * 0.6366197723675814 + 0.5)
    rest = angle - turns * 1.5703125
    rest = rest - turns * 4.837512969970703e-4
    rest = rest - turns * 7.549789948768648e-8
    square = rest * rest
    sin_poly = (-1.9515295891e-4 * square + 8.3321608736e-3) * square - 1.6666654611e-1
    sin = rest + rest * square * sin_poly
    cos_poly = (2.443315711809948e-5 * square - 1.388731625493765e-3) * square
    cos = 1.0 - 0.5 * square + square * square * (cos_poly + 4.166664568298827e-2)
    quarter = turns.astype(jnp.int32)
    odd = (quarter & 1) == 1
    turned_cos, turned_sin = jnp.where(odd, sin, cos), jnp.where(odd, cos, sin)
    return (
        jnp.where(((quarter + 1) & 2) == 2, -turned_cos, turned_cos),
        jnp.where((quarter & 2) == 2, -turned_sin, turned_sin),
    )


def multiples(c, s):
    c2 = 2.0 * (c * c) - 1.0
    s2 = 2.0 * (c * s)
    return (
        (c, s),
        (c2, s2),
        (c2 * c - s2 * s, s2 * c + c2 * s),
        (2.0 * (c2 * c2) - 1.0, 2.0 * (c2 * s2)),
    )


def adapted(entries, axes):
    one, two, three, shear, first, second = axes
    at = lambda row, col: entries[(min(row, col), max(row, col))]
    mean = at(one, one) + at(two, two)
    cross = 2.0 * at(one, two)
    spread = mean - cross
    half_shear = 0.5 * at(shear, shear)
    half_spread = 0.5 * spread
    half_first = 0.5 * at(first, first)
    half_second = 0.5 * at(second, second)
    lone = lambda with_: (at(one, with_) + at(two, with_), at(one, with_) - at(two, with_))
    sum_three, diff_three = lone(three)
    sum_shear, diff_shear = lone(shear)
    sum_first, diff_first = lone(first)
    sum_second, diff_second = lone(second)
    fixed = (
        mean + cross,
        sum_three,
        at(three, three),
        half_spread + half_shear,
        half_first + half_second,
    )
    pairs = [
        (2, at(one, one) - at(two, two), sum_shear),
        (2, diff_three, at(three, shear)),
        (1, sum_first, sum_second),
        (1, at(three, first), at(three, second)),
        (4, half_spread - half_shear, diff_shear),
        (2, half_first - half_second, at(first, second)),
        (1, diff_first + at(shear, second), at(shear, first) - diff_second),
        (3, diff_first - at(shear, second), at(shear, first) + diff_second),
    ]
    return fixed, pairs


def turned(adapted_set, angles):
    fixed, pairs = adapted_set
    fresh = []
    for order, x, y in pairs:
        c, s = angles[order - 1]
        fresh.append((order, c * x - s * y, s * x + c * y))
    return fixed, fresh


def natural(adapted_set, axes):
    one, two, three, shear, first, second = axes
    (whole, sum_three, three_three, shear_mean, side_mean), pairs = adapted_set
    (
        (_, lean, sum_shear),
        (_, diff_three, three_shear),
        (_, sum_first, sum_second),
        (_, three_first, three_second),
        (_, shear_half, diff_shear),
        (_, side_half, first_second),
        (_, real_one, imag_one),
        (_, real_three, imag_three),
    ) = pairs
    spread = shear_mean + shear_half
    diff_first = 0.5 * (real_one + real_three)
    diff_second = 0.5 * (imag_three - imag_one)
    quarter = 0.25 * (whole + spread)
    half_lean = 0.5 * lean
    out = {}

    def put(row, col, value):
        out[(min(row, col), max(row, col))] = value

    put(one, one, quarter + half_lean)
    put(two, two, quarter - half_lean)
    put(one, two, 0.25 * (whole - spread))
    for with_, total, gap in (
        (three, sum_three, diff_three),
        (shear, sum_shear, diff_shear),
        (first, sum_first, diff_first),
        (second, sum_second, diff_second),
    ):
        put(one, with_, 0.5 * (total + gap))
        put(two, with_, 0.5 * (total - gap))
    put(three, three, three_three)
    put(three, shear, three_shear)
    put(three, first, three_first)
    put(three, second, three_second)
    put(shear, shear, shear_mean - shear_half)
    put(shear, first, 0.5 * (imag_one + imag_three))
    put(shear, second, 0.5 * (real_one - real_three))
    put(first, first, side_mean + side_half)
    put(second, second, side_mean - side_half)
    put(first, second, first_second)
    return out


about_z = (0, 1, 2, 5, 4, 3)
about_x = (1, 2, 0, 3, 5, 4)


def rotated_stiffness(entries, trig):
    cos_one, cos_mid, cos_two, sin_one, sin_mid, sin_two = trig
    first = turned(adapted(entries, about_z), multiples(cos_two, sin_two))
    middle = turned(adapted(natural(first, about_z), about_x), multiples(cos_mid, sin_mid))
    last = turned(adapted(natural(middle, about_x), about_z), multiples(cos_one, sin_one))
    return natural(last, about_z)


def grain_kernel(
    crystal_hbm,
    euler_hbm,
    orient_hbm,
    weight_hbm,
    map_hbm,
    density_hbm,
    velocity_hbm,
    stress_hbm,
    send_ref,
    crystal_ref,
    euler_ref,
    orient_ref,
    weight_ref,
    map_ref,
    density_ref,
    velocity_ref,
    stress_ref,
    sums_ref,
    place_ref,
    acc_ref,
    fields_ref,
    arrived,
):
    row_part = lax.axis_index("gy")
    layer = lax.axis_index("ga")
    grains = weight_ref.shape[0]
    cells = weight_ref.shape[1]
    tiles = cells // LANES
    octets = grains // SUB
    table_tiles = euler_ref.shape[1] // LANES
    destinations = send_ref.shape[0] // BLOCK_ROWS

    copies = [
        pltpu.make_async_copy(source, target, arrived.at[at])
        for at, (source, target) in enumerate(
            [
                (map_hbm, map_ref),
                (crystal_hbm, crystal_ref),
                (orient_hbm, orient_ref),
                (euler_hbm, euler_ref),
                (weight_hbm, weight_ref),
                (stress_hbm, stress_ref),
                (velocity_hbm, velocity_ref),
                (density_hbm, density_ref),
            ]
        )
    ]
    for copy in copies:
        copy.start()
    sums_ref[...] = jnp.zeros_like(sums_ref)
    place_ref[...] = jnp.zeros_like(place_ref)

    for copy in copies[:5]:
        copy.wait()
    scale = (1.0, 1.0, 1.0, 2.0, 2.0, 2.0)
    entries = {
        (row, col): (scale[row] * scale[col]) * crystal_ref[pair]
        for pair, (row, col) in enumerate(upper_pairs)
    }
    def pick(tile, octet):
        index = orient_ref[pl.ds(octet * SUB * tiles + tile, SUB, stride=tiles), :]
        low = index & (LANES - 1)
        bits = [(index & (LANES << level)) != 0 for level in range(table_tiles.bit_length() - 1)]

        def find(which, first, level):
            if level == 0:
                source = jnp.broadcast_to(
                    euler_ref[which : which + 1, first * LANES : (first + 1) * LANES], (SUB, LANES)
                )
                return jnp.take_along_axis(source, low, axis=1, mode="promise_in_bounds")
            lower = find(which, first, level - 1)
            upper = find(which, first + (1 << (level - 1)), level - 1)
            return jnp.where(bits[level - 1], upper, lower)

        values = [find(which, 0, len(bits)) for which in range(3)]
        return values

    held = [pick(0, octet) for octet in range(octets)]

    slots = map_ref[...]
    half = 32
    inner = jnp.where(
        jnp.broadcast_to(slots & (half - 1), (half, cells)) == rows_of((half, cells)), 1.0, 0.0
    ).astype(jnp.bfloat16)
    outer = jnp.broadcast_to(slots // half, (half, cells)).astype(jnp.bfloat16)
    for chunk in range(cells // half):
        start = pl.multiple_of(chunk * 2 * half + row_part * half, half)
        place_ref[pl.ds(start, half), :] = jnp.where(
            outer == jnp.bfloat16(chunk), inner, jnp.bfloat16(0.0)
        )

    def add_tile(tile, held):
        lanes = slice(tile * LANES, (tile + 1) * LANES)
        for octet in range(octets):
            turns = [cos_and_sin(angle) for angle in held[octet]]
            rotated = rotated_stiffness(entries, [turn[at] for at in range(2) for turn in turns])
            mass = weight_ref[octet * SUB : (octet + 1) * SUB, lanes].astype(jnp.float32)
            masses = {1.0: mass, 0.5: 0.5 * mass, 0.25: 0.25 * mass}
            for pair, (row, col) in enumerate(upper_pairs):
                value = rotated[row, col] * masses[1.0 / (scale[row] * scale[col])]
                acc_ref[pair] = value if octet == 0 else acc_ref[pair] + value
            acc_ref[21] = mass if octet == 0 else acc_ref[21] + mass
        for at, named in enumerate((LOW_ROWS, HIGH_ROWS)):
            for first in (0, SUB):
                summed = sublane_sums([acc_ref[pair] for pair in named[first : first + SUB]])
                sums_ref[at * 16 + first : at * 16 + first + SUB, lanes] = summed

    def one_tile(tile, held):
        fresh = [pick(tile + 1, octet) for octet in range(octets)]
        add_tile(tile, held)
        return fresh

    for tile in range(tiles // 2):
        held = one_tile(tile, held)

    for copy in copies[5:]:
        copy.wait()
    own = row_part * 2 + layer

    def field_rows(component, y):
        if component < 6:
            return stress_ref[pl.ds(component * 32 + y, SUB, stride=4), :]
        if component < 9:
            return velocity_ref[pl.ds((component - 6) * 32 + y, SUB, stride=4), :]
        return density_ref[pl.ds(y, SUB, stride=4), :]

    def spread(component, slot, into):
        goal = own ^ slot
        for y in range(4):
            start = (goal // 2) * 64 + y * 16 + (goal % 2) * 8
            narrow = jnp.concatenate(
                [field_rows(component, y), jnp.zeros((SUB, LANES - 8), jnp.float32)], axis=1
            )
            into = into + pltpu.roll(narrow, start, 1)
        return into

    nothing = jnp.zeros((SUB, LANES), jnp.float32)
    for half in range(2):
        group, tail = nothing, nothing
        for slot in (0, 1, 3, 2):
            group = spread(half * HALF + slot, slot, group)
            if slot == 0:
                piece = spread(half * HALF + 4, slot, nothing)
            elif slot == 3:
                piece = pltpu.roll(piece, LANES // 2, 1)
            else:
                piece = other_layer(piece, lanes_of((SUB, LANES)))
            tail = tail + (piece if slot == 0 else pltpu.roll(piece, SUB - 2 * slot, 0))
        fields_ref[half, 0:SUB, :] = group
        fields_ref[half, SUB : SUB + 2, :] = tail[0:2]

    for tile in range(tiles // 2, tiles - 1):
        held = one_tile(tile, held)
    add_tile(tiles - 1, held)

    sums = sums_ref[...]
    part_one = sums.astype(jnp.bfloat16)
    rest = sums - part_one.astype(jnp.float32)
    part_two = rest.astype(jnp.bfloat16)
    part_three = (rest - part_two.astype(jnp.float32)).astype(jnp.bfloat16)
    parts = jnp.concatenate([part_one, part_two, part_three], axis=0)
    placed = lax.dot_general(
        parts, place_ref[...], (((1,), (1,)), ((), ())), preferred_element_type=jnp.float32
    )
    placed = placed[0:32] + placed[32:64] + placed[64:96]

    shift = 32 + row_part * 64
    bricks = destinations // 4
    lane = lanes_of((SUB, LANES))
    upper = lax.axis_index("gx") >= SUB // 2
    own_sums, edge_sums = [], []
    for brick in range(bricks):
        halves = [
            placed[at : at + 16, brick * LANES : (brick + 1) * LANES] for at in (0, 16)
        ]
        own_sums.append(halves[0] + pltpu.roll(halves[1], shift, 1))
        edge_sums.append(
            [
                half[0:8] + pltpu.roll(pltpu.roll(half, 16 - EDGE_ROWS, 0)[0:8], shift, 1)
                for half in halves
            ]
        )
    for brick in range(bricks):
        side = brick % 2
        before, after = brick - side - 1, brick - side + 2
        before = edge_sums[before][side] if before >= 0 else nothing
        after = edge_sums[after][side] if after < bricks else nothing
        near = jnp.where(upper, before, after)
        far = opposite_class(jnp.where(upper, after, before), lane)
        for inner in range(4):
            at = block_of(brick, inner, bricks) * BLOCK_ROWS
            edge = jnp.where(near_lanes(lane, inner // 2, inner % 2), near, far)
            send_ref[at : at + SUM_ROWS, :] = own_sums[brick][0:SUM_ROWS]
            send_ref[at + SUM_ROWS : at + FIELD_AT, :] = edge[0:EDGE_ROWS]
            send_ref[at + FIELD_AT : at + FIELD_AT + SUB, :] = fields_ref[side, 0:SUB, :]
            send_ref[at + FIELD_AT + SUB : at + BLOCK_ROWS, :] = fields_ref[side, SUB : SUB + 2, :]


def plane_shifts(dim, count):
    lane = lanes_of((count, LANES))
    position, extent, unit = (lane // 16, 8, 16) if dim == 1 else (lane % 16, 16, 1)
    terms = {}
    for order in range(1, 5):
        weight = stencil_weights[order - 1]
        behind = jnp.where(position >= order, -weight, 0.0)
        ahead = jnp.where(position < extent - order, weight, 0.0)
        for shift, own in ((order * unit, behind), (LANES - order * unit, ahead)):
            terms[shift] = terms[shift] + own if shift in terms else own
    return list(terms.items())


def tree_sum(terms):
    while len(terms) > 1:
        paired = [one + two for one, two in zip(terms[0::2], terms[1::2])]
        terms = paired + terms[2 * len(paired) :]
    return terms[0]


def plane_derivative(field, shifts):
    return tree_sum([weights * pltpu.roll(field, shift, 1) for shift, weights in shifts])


def row_derivative(read, start, count):
    return tree_sum(
        [
            stencil_weights[order - 1] * (read(start + order, count) - read(start - order, count))
            for order in range(1, 5)
        ]
    )


def velocity_update(wide_stress, old_velocity, density, inside, count):
    shifts = {dim: plane_shifts(dim, count) for dim in (1, 2)}

    def along(component, dim):
        if dim == 0:
            return row_derivative(
                lambda at, size: wide_stress[component, at : at + size, :], 4, count
            )
        return plane_derivative(wide_stress[component, 4 : 4 + count, :], shifts[dim])

    sums = [
        along(0, 0) + along(5, 1) + along(4, 2),
        along(5, 0) + along(1, 1) + along(3, 2),
        along(4, 0) + along(3, 1) + along(2, 2),
    ]
    return [
        jnp.where(inside, old_velocity[at] + time_step * sums[at] / density, 0.0)
        for at in range(3)
    ]


def stress_update(wide_velocity, start, old_stress, stiff):
    shifts = {dim: plane_shifts(dim, SUB) for dim in (1, 2)}

    def along(component, dim):
        if dim == 0:
            return row_derivative(
                lambda at, size: wide_velocity[component, pl.ds(at, size), :], start, SUB
            )
        return plane_derivative(wide_velocity[component, pl.ds(start, SUB), :], shifts[dim])

    strain = [
        along(0, 0),
        along(1, 1),
        along(2, 2),
        along(2, 1) + along(1, 2),
        along(2, 0) + along(0, 2),
        along(1, 0) + along(0, 1),
    ]
    return [
        old_stress[row]
        + time_step
        * tree_sum([stiff(symmetric_index(row, col)) * strain[col] for col in range(6)])
        for row in range(6)
    ]


def inside_rows(brick, bricks, margin, count):
    place = rows_of((count, LANES)) - margin + brick * SUB
    return (place >= 0) & (place < bricks * SUB)


def unpack_kernel(got_ref, out_ref):
    brick = lax.axis_index("gx")
    bricks = got_ref.shape[0] // BLOCK_ROWS // 4

    def by_slot(zero, one):
        first_slot = (lanes_of(zero.shape) // 32) % 2 == 0
        low = jnp.where(first_slot, zero, one)
        high = jnp.where(first_slot, one, zero)
        high = jnp.where(first_slot, pltpu.roll(high, LANES - 32, 1), pltpu.roll(high, 32, 1))
        return low, high

    for p in range(bricks):

        def both_layers(part, offset, count):
            first, second = [
                block_of(p, part * 2 + layer, bricks) * BLOCK_ROWS + offset for layer in range(2)
            ]
            return got_ref[first : first + count, :] + got_ref[second : second + count, :]

        low, high = by_slot(both_layers(0, 0, SUM_ROWS), both_layers(1, 0, SUM_ROWS))
        total = jnp.broadcast_to(high[10:11], (SUB, LANES))
        at = p * STIFF_ROWS
        out_ref[at : at + 8, :] = low[0:8] / total
        out_ref[at + 8 : at + 16, :] = high[0:8] / total
        out_ref[at + 16 : at + 19, :] = low[8:11] / total[0:3]
        out_ref[at + 19 : at + 22, :] = high[8:11] / total[0:3]
        low, high = by_slot(
            both_layers(0, SUM_ROWS, EDGE_ROWS), both_layers(1, SUM_ROWS, EDGE_ROWS)
        )
        at = EDGE_AT + p * SUM_ROWS
        out_ref[at : at + EDGE_ROWS, :] = low
        out_ref[at + EDGE_ROWS : at + SUM_ROWS, :] = high[0 : SUM_ROWS - EDGE_ROWS]

    def collect(source, offset, count, slot):
        lane = lanes_of((count, LANES))
        kind = (lane // 64) * 2 + (lane // 8) % 2
        pieces = [
            got_ref[pl.ds(block_of(source, q ^ slot, bricks) * BLOCK_ROWS + offset, count), :]
            for q in range(4)
        ]
        value = jnp.where(
            kind < 2,
            jnp.where(kind == 0, pieces[0], pieces[1]),
            jnp.where(kind == 2, pieces[2], pieces[3]),
        )
        if slot & 1:
            value = jnp.where(
                (lane // 8) % 2 == 0,
                pltpu.roll(value, LANES - 8, 1),
                pltpu.roll(value, 8, 1),
            )
        if slot & 2:
            value = pltpu.roll(value, 64, 1)
        return value

    for side in range(WIDE_ROWS // SUB):
        wanted = (brick // 2) * 2 + side - 2
        source = jnp.clip(wanted, 0, bricks - 1)
        valid = source == wanted
        for slot in range(4):
            at = WIDE_AT + slot * WIDE_ROWS + side * SUB
            value = collect(source, FIELD_AT, SUB, slot)
            out_ref[at : at + SUB, :] = jnp.where(valid, value, 0.0)
            at = WIDE_AT + 4 * WIDE_ROWS + side * SUB + 2 * slot
            value = collect(source, FIELD_AT + SUB, 2, slot)
            out_ref[at : at + 2, :] = jnp.where(valid, value, 0.0)


def stiffness_kernel(stiff_ref, out_ref, turned_ref):
    own = lax.axis_index("gy") * 64 + lax.axis_index("ga") * 8
    for p in range(SUB):
        turned_ref[...] = jnp.transpose(stiff_ref[p * STIFF_ROWS : p * STIFF_ROWS + 24, :])
        for y in range(4):
            rows = pl.ds(pl.multiple_of(own + y * 16, 8), 8)
            out_ref[p * 32 + y * 8 : p * 32 + y * 8 + 8, :] = turned_ref[rows, 0:21]


def steps_kernel(
    own_ref,
    other_ref,
    out_velocity_ref,
    out_stress_ref,
    wide_ref,
    edge_ref,
    first_velocity_ref,
    first_stress_ref,
    last_velocity_ref,
    *,
    bricks,
):
    brick = lax.axis_index("gx")
    row_part, layer = lax.axis_index("gy"), lax.axis_index("ga")
    odd = brick % 2
    lane = lanes_of((SUB, LANES))
    row = rows_of((SUB, LANES))

    for at in range(HALF):
        rows = pl.ds(pl.multiple_of(WIDE_AT + at * WIDE_ROWS + odd * SUB, SUB), 5 * SUB)
        wide_ref[odd * HALF + at] = own_ref[rows, :]
        wide_ref[(1 - odd) * HALF + at] = other_ref[rows, :]

    edge_valid = jnp.where(odd == 0, brick - 1, brick + 1)
    edge_valid = (edge_valid >= 0) & (edge_valid < bricks)
    near_row = jnp.where(odd == 0, row, SUB - 1 - row) >= SUB // 2
    own_lane = (lane // 64 == row_part) & ((lane // 8) % 2 == layer)
    usable = (own_lane | (near_row & near_lanes(lane, row_part, layer))) & edge_valid

    def edge(half, k):
        rows = pl.ds(EDGE_AT + k, SUB, stride=SUM_ROWS)
        value = jnp.where(odd == half, own_ref[rows, :], other_ref[rows, :])
        return jnp.where(near_row, value, opposite_class(value, lane))

    total = jnp.where(usable, edge(1, 10), 1.0)
    for half, named in enumerate((LOW_ROWS, HIGH_ROWS)):
        for k, pair in enumerate(named):
            if pair < 21:
                edge_ref[pair] = edge(half, k) / total

    inside = inside_rows(brick, bricks, 12, 32)
    density = jnp.where(inside, wide_ref[9, 4:36, :], 1.0)
    fresh = velocity_update(
        wide_ref, [wide_ref[6 + at, 4:36, :] for at in range(3)], density, inside, 32
    )
    for at in range(3):
        first_velocity_ref[at] = fresh[at]
    own_stiff = lambda pair: own_ref[pl.ds(pair, SUB, stride=STIFF_ROWS), :]
    for group, stiff, valid in (
        (SUB, own_stiff, None),
        (2 * SUB - odd * 2 * SUB, lambda pair: other_ref[pl.ds(pair, SUB, stride=STIFF_ROWS), :], None),
        (odd * 2 * SUB, lambda pair: edge_ref[pair], edge_valid),
    ):
        fresh = stress_update(
            first_velocity_ref,
            group + 4,
            [wide_ref[at, pl.ds(group + SUB, SUB), :] for at in range(6)],
            stiff,
        )
        for at in range(6):
            value = fresh[at] if valid is None else jnp.where(valid, fresh[at], 0.0)
            first_stress_ref[at, pl.ds(group, SUB), :] = value

    velocity = velocity_update(
        first_stress_ref,
        [first_velocity_ref[at, 8:24, :] for at in range(3)],
        density[8:24],
        inside_rows(brick, bricks, 4, 16),
        16,
    )
    for at in range(3):
        last_velocity_ref[at] = velocity[at]
    stress = stress_update(
        last_velocity_ref, 4, [first_stress_ref[at, 8:16, :] for at in range(6)], own_stiff
    )
    own = row_part * 64 + layer * 8

    def put(out_ref, at, value):
        for y in range(4):
            turned = pltpu.roll(value, (LANES - own - y * 16) % LANES, 1)
            out_ref[pl.ds(at * 32 + y, SUB, stride=4), :] = turned[:, 0:8]

    for at in range(3):
        put(out_velocity_ref, at, last_velocity_ref[at, 4:12, :])
    for at in range(6):
        put(out_stress_ref, at, stress[at])


def on_plane(euler_table, crystal, orient, weight, cell_map, density, velocity, stress):
    part_x = lax.axis_size("gx")
    devices = part_x * lax.axis_size("gy") * lax.axis_size("ga")
    grains, cells = orient.shape[0], orient.shape[3]
    tiles = cells // LANES
    octets = grains // SUB
    vmem = pl.BlockSpec(memory_space=pltpu.VMEM)
    hbm = pl.BlockSpec(memory_space=pltpu.HBM)
    f32 = jnp.float32

    send = pl.pallas_call(
        grain_kernel,
        out_shape=jax.ShapeDtypeStruct((devices * BLOCK_ROWS, LANES), f32),
        in_specs=[hbm] * 8,
        out_specs=vmem,
        scratch_shapes=[
            pltpu.SMEM((21,), f32),
            pltpu.VMEM(euler_table.shape, f32),
            pltpu.VMEM((grains * tiles, LANES), jnp.int32),
            pltpu.VMEM((grains, cells), weight.dtype),
            pltpu.VMEM((1, cells), jnp.int32),
            pltpu.VMEM((SUB * 4, 8), f32),
            pltpu.VMEM((3 * SUB * 4, 8), f32),
            pltpu.VMEM((6 * SUB * 4, 8), f32),
            pltpu.VMEM((32, cells), f32),
            pltpu.VMEM((2 * cells, cells), jnp.bfloat16),
            pltpu.VMEM((22, SUB, LANES), f32),
            pltpu.VMEM((2, 2 * SUB, LANES), f32),
            pltpu.SemaphoreType.DMA((8,)),
        ],
        compiler_params=pltpu.CompilerParams(vmem_limit_bytes=8 * 2**20),
    )(*[pltpu.with_memory_space_constraint(x, pltpu.HBM) for x in (
        crystal,
        euler_table,
        orient.reshape(grains * tiles, LANES),
        weight.reshape(grains, cells),
        cell_map.reshape(1, cells),
        density.reshape(SUB * 4, 8),
        velocity.reshape(3 * SUB * 4, 8),
        stress.reshape(6 * SUB * 4, 8),
    )])
    got = lax.all_to_all(
        send.reshape(devices, 1, BLOCK_ROWS * LANES),
        ("ga", "gx", "gy"),
        split_axis=0,
        concat_axis=0,
        tiled=True,
    ).reshape(devices * BLOCK_ROWS, LANES)
    small = pltpu.CompilerParams(vmem_limit_bytes=8 * 2**20)
    own_part = pl.pallas_call(
        unpack_kernel,
        out_shape=jax.ShapeDtypeStruct((WIDE_AT + HALF * WIDE_ROWS, LANES), f32),
        in_specs=[vmem],
        out_specs=vmem,
        compiler_params=small,
    )(got)
    other_part = lax.ppermute(own_part, "gx", [(i, i ^ 1) for i in range(part_x)])
    stiffness = pl.pallas_call(
        stiffness_kernel,
        out_shape=jax.ShapeDtypeStruct((SUB * 4 * 8, 21), f32),
        in_specs=[vmem],
        out_specs=vmem,
        scratch_shapes=[pltpu.VMEM((LANES, 24), f32)],
        cost_estimate=pl.CostEstimate(flops=100000, bytes_accessed=200000, transcendentals=0),
        compiler_params=small,
    )(own_part)
    new_velocity, new_stress = pl.pallas_call(
        functools.partial(steps_kernel, bricks=part_x),
        out_shape=(
            jax.ShapeDtypeStruct((3 * SUB * 4, 8), f32),
            jax.ShapeDtypeStruct((6 * SUB * 4, 8), f32),
        ),
        in_specs=[vmem] * 2,
        out_specs=(vmem,) * 2,
        scratch_shapes=[
            pltpu.VMEM((FIELDS, 5 * SUB, LANES), f32),
            pltpu.VMEM((21, SUB, LANES), f32),
            pltpu.VMEM((3, 4 * SUB, LANES), f32),
            pltpu.VMEM((6, 3 * SUB, LANES), f32),
            pltpu.VMEM((3, 2 * SUB, LANES), f32),
        ],
        compiler_params=small,
    )(own_part, other_part)
    return (
        stiffness.reshape(SUB, 4, 8, 21).transpose(3, 0, 1, 2),
        new_velocity.reshape(3, SUB, 4, 8),
        new_stress.reshape(6, SUB, 4, 8),
    )


def on_device(euler_table, crystal, orient, weight, cell_map, density, velocity, stress):
    sizes = (lax.axis_size("gx"), lax.axis_size("gy"), lax.axis_size("ga"))
    form = on_plane if fits_plane(*sizes, orient, stress, euler_table) else on_device_general
    return form(euler_table, crystal, orient, weight, cell_map, density, velocity, stress)


def solution(mesh):
    return jax.shard_map(
        on_device,
        mesh=mesh,
        in_specs=(
            P(),
            P(),
            P("ga", "gx", "gy", None),
            P("ga", "gx", "gy", None),
            P("gx", "gy", None),
            P("gx", "gy", "ga"),
            P(None, "gx", "gy", "ga"),
            P(None, "gx", "gy", "ga"),
        ),
        out_specs=(P(None, "gx", "gy", "ga"), P(None, "gx", "gy", "ga"), P(None, "gx", "gy", "ga")),
        check_vma=False,
    )
```

```python
import functools

import jax
import jax.numpy as jnp
from jax import lax
from jax.experimental import pallas as pl
from jax.experimental.pallas import tpu as pltpu
from jax.sharding import PartitionSpec as P

STEPS = 2


stencil_weights = (0.8, -0.2, 4.0 / 105.0, -1.0 / 280.0)
time_step = 0.2
grain_block = 4
voigt_pairs = ((0, 0), (1, 1), (2, 2), (1, 2), (0, 2), (0, 1))
upper_pairs = [
    (row_index, col_index) for row_index in range(6) for col_index in range(row_index, 6)
]


def with_halo(cells, sides, width):
    for axis, dim in sides:
        count = lax.axis_size(axis)
        ends = count - 1
        head = lax.slice_in_dim(cells, 0, width, axis=dim)
        tail = lax.slice_in_dim(cells, cells.shape[dim] - width, cells.shape[dim], axis=dim)
        cells = jnp.concatenate(
            [
                lax.ppermute(tail, axis, [(i, (i + 1) % count) for i in range(ends)]),
                cells,
                lax.ppermute(head, axis, [((i + 1) % count, i) for i in range(ends)]),
            ],
            axis=dim,
        )
    return cells


def symmetric_index(first_index, second_index):
    return upper_pairs.index((min(first_index, second_index), max(first_index, second_index)))


def ordered_sum(summands):
    running = summands[0]
    for summand in summands[1:]:
        running = running + summand
    return running


def rotated_table(euler_table, crystal):
    cos_one, sin_one = (jnp.cos(euler_table[0]), jnp.sin(euler_table[0]))
    cos_mid, sin_mid = (jnp.cos(euler_table[1]), jnp.sin(euler_table[1]))
    cos_two, sin_two = (jnp.cos(euler_table[2]), jnp.sin(euler_table[2]))
    bunge = [
        [
            cos_one * cos_two - sin_one * sin_two * cos_mid,
            sin_one * cos_two + cos_one * sin_two * cos_mid,
            sin_two * sin_mid,
        ],
        [
            -cos_one * sin_two - sin_one * cos_two * cos_mid,
            -sin_one * sin_two + cos_one * cos_two * cos_mid,
            cos_two * sin_mid,
        ],
        [sin_one * sin_mid, -cos_one * sin_mid, cos_mid],
    ]
    rotation = [[bunge[col_index][row_index] for col_index in range(3)] for row_index in range(3)]
    bond = []
    for out_index in range(6):
        first, second = voigt_pairs[out_index]
        bond_row = []
        for in_index in range(6):
            third, fourth = voigt_pairs[in_index]
            if in_index < 3:
                bond_row.append(rotation[first][third] * rotation[second][third])
            else:
                bond_row.append(
                    rotation[first][third] * rotation[second][fourth]
                    + rotation[first][fourth] * rotation[second][third]
                )
        bond.append(bond_row)
    entries = [
        [crystal[symmetric_index(row_index, col_index)] for col_index in range(6)]
        for row_index in range(6)
    ]
    product = [
        [
            ordered_sum([bond[row_index][inner] * entries[inner][col_index] for inner in range(6)])
            for col_index in range(6)
        ]
        for row_index in range(6)
    ]
    rotated = [
        ordered_sum([product[row_index][inner] * bond[col_index][inner] for inner in range(6)])
        for row_index, col_index in upper_pairs
    ]
    return jnp.stack(rotated)


def accumulate(table, orient_rows, weight_rows):
    blocks = orient_rows.shape[0] // grain_block
    count_cells = orient_rows.shape[1]

    def absorb(carry, inputs):
        chosen, masses = inputs
        picked = jnp.take(table, chosen, axis=1)
        masses_wide = masses.astype(jnp.float32)
        return (
            (
                carry[0] + jnp.sum(picked * masses_wide[None], axis=1),
                carry[1] + jnp.sum(masses_wide, axis=0),
            ),
            None,
        )

    initial = (jnp.zeros((21, count_cells), jnp.float32), jnp.zeros((count_cells,), jnp.float32))
    result, unused = lax.scan(
        absorb,
        initial,
        (
            orient_rows.reshape(blocks, grain_block, count_cells),
            weight_rows.reshape(blocks, grain_block, count_cells),
        ),
    )
    return result


def derivative(padded, direction):
    interior = [padded.shape[0]] + [extent - 8 for extent in padded.shape[1:]]

    def window(offset):
        starts = [0, 4, 4, 4]
        starts[direction] = 4 + offset
        return lax.slice(
            padded, starts, [begin + extent for begin, extent in zip(starts, interior)]
        )

    result = stencil_weights[0] * (window(1) - window(-1))
    for order_index in range(1, 4):
        result = result + stencil_weights[order_index] * (
            window(order_index + 1) - window(-order_index - 1)
        )
    return result


def advance_velocity(velocity, padded_stress, density):
    along_x = derivative(jnp.stack([padded_stress[0], padded_stress[5], padded_stress[4]]), 1)
    along_y = derivative(jnp.stack([padded_stress[5], padded_stress[1], padded_stress[3]]), 2)
    along_z = derivative(jnp.stack([padded_stress[4], padded_stress[3], padded_stress[2]]), 3)
    return velocity + time_step * (along_x + along_y + along_z) / density[None]


def advance_stress(stress, padded_velocity, stiffness):
    grad_x = derivative(padded_velocity, 1)
    grad_y = derivative(padded_velocity, 2)
    grad_z = derivative(padded_velocity, 3)
    strain = [
        grad_x[0],
        grad_y[1],
        grad_z[2],
        grad_y[2] + grad_z[1],
        grad_x[2] + grad_z[0],
        grad_x[1] + grad_y[0],
    ]
    updated = []
    for row_index in range(6):
        change = ordered_sum(
            [
                stiffness[symmetric_index(row_index, col_index)] * strain[col_index]
                for col_index in range(6)
            ]
        )
        updated.append(stress[row_index] + time_step * change)
    return jnp.stack(updated)


def on_device_general(euler_table, crystal, orient, weight, cell_map, density, velocity, stress):
    part_x = lax.axis_size("gx")
    part_y = lax.axis_size("gy")
    layers = lax.axis_size("ga")
    brick_x, brick_y, brick_z = (stress.shape[1], stress.shape[2], stress.shape[3])
    sub_x = brick_x // part_x
    sub_y = brick_y // part_y
    depth = brick_z * layers
    grains = orient.shape[0]
    count_cells = orient.shape[3]
    table = rotated_table(euler_table, crystal)
    summed, total = accumulate(
        table, orient.reshape(grains, count_cells), weight.reshape(grains, count_cells)
    )
    slots = cell_map.reshape(count_cells)
    layer_pos = slots % depth
    remainder = slots // depth
    sub_y_pos = remainder % sub_y
    remainder = remainder // sub_y
    brick_y_pos = remainder % part_y
    remainder = remainder // part_y
    sub_x_pos = remainder % sub_x
    brick_x_pos = remainder // sub_x
    target = (
        ((brick_x_pos * part_y + brick_y_pos) * sub_x + sub_x_pos) * sub_y + sub_y_pos
    ) * depth + layer_pos
    placed = jnp.zeros((21, count_cells), jnp.float32).at[:, target].set(summed)
    counted = jnp.zeros((count_cells,), jnp.float32).at[target].set(total)
    placed = placed.reshape(21, part_x * part_y, sub_x, sub_y, depth)
    counted = counted.reshape(part_x * part_y, sub_x, sub_y, depth)
    placed, counted = (
        lax.psum_scatter(placed, "ga", scatter_dimension=4, tiled=True),
        lax.psum_scatter(counted, "ga", scatter_dimension=3, tiled=True),
    )
    averaged = placed / counted[None]
    moved = lax.all_to_all(averaged, ("gx", "gy"), split_axis=1, concat_axis=1, tiled=True)
    moved = moved.reshape(21, part_x, part_y, sub_x, sub_y, brick_z)
    stiffness = moved.transpose(0, 1, 3, 2, 4, 5).reshape(21, brick_x, brick_y, brick_z)
    for step_index in range(STEPS):
        padded_stress = with_halo(stress, (("gx", 1), ("gy", 2), ("ga", 3)), 4)
        velocity = advance_velocity(velocity, padded_stress, density)
        padded_velocity = with_halo(velocity, (("gx", 1), ("gy", 2), ("ga", 3)), 4)
        stress = advance_stress(stress, padded_velocity, stiffness)
    return (stiffness, velocity, stress)


SUB = 8
LANES = 128
SUM_ROWS = 11
EDGE_ROWS = 6
FIELD_AT = SUM_ROWS + EDGE_ROWS
BLOCK_ROWS = FIELD_AT + 10
STIFF_ROWS = 22
EDGE_AT = STIFF_ROWS * SUB
WIDE_AT = EDGE_AT + SUM_ROWS * SUB
WIDE_ROWS = 48
FIELDS = 10
HALF = FIELDS // 2
LOW_ROWS = tuple(range(8)) + (16, 17, 18)
HIGH_ROWS = tuple(range(8, 16)) + (19, 20, 21)


def fits_plane(part_x, part_y, layers, orient, stress, euler_table):
    brick_x, brick_y, brick_z = stress.shape[1:]
    return (
        part_x % 2 == 0
        and part_y == 2
        and layers == 2
        and brick_x == SUB
        and part_x == SUB
        and brick_y == 4
        and brick_z == 8
        and orient.shape[3] == part_x * 64
        and orient.shape[0] % 8 == 0
        and euler_table.shape[1] in [LANES << level for level in range(8)]
        and STEPS == 2
    )


def lanes_of(shape):
    return lax.broadcasted_iota(jnp.int32, shape, len(shape) - 1)


def rows_of(shape):
    return lax.broadcasted_iota(jnp.int32, shape, len(shape) - 2)


def other_layer(value, lane):
    return jnp.where(
        (lane // 8) % 2 == 0, pltpu.roll(value, LANES - 8, 1), pltpu.roll(value, 8, 1)
    )


def opposite_class(value, lane):
    return pltpu.roll(other_layer(value, lane), LANES // 2, 1)


def sublane_sums(values):
    row = rows_of((SUB, LANES))
    values = values + [None] * (SUB - len(values))
    for step in (1, 2, 4):
        keep = (row // step) % 2 == 0
        merged = []
        for one, two in zip(values[0::2], values[1::2]):
            if one is None:
                merged.append(None)
                continue
            two = jnp.zeros_like(one) if two is None else two
            merged.append(
                jnp.where(keep, one, two) + pltpu.roll(jnp.where(keep, two, one), step, 0)
            )
        values = merged
    return values[0]


def block_of(brick, inner, bricks):
    return (inner // 2) * bricks * 2 + brick * 2 + inner % 2


def near_lanes(lane, row_half, layer):
    return (lane // 64 == row_half) | ((lane // 8) % 2 == layer)


def cos_and_sin(angle):
    turns = jnp.floor(angle * 0.6366197723675814 + 0.5)
    rest = angle - turns * 1.5703125
    rest = rest - turns * 4.837512969970703e-4
    rest = rest - turns * 7.549789948768648e-8
    square = rest * rest
    sin_poly = (-1.9515295891e-4 * square + 8.3321608736e-3) * square - 1.6666654611e-1
    sin = rest + rest * square * sin_poly
    cos_poly = (2.443315711809948e-5 * square - 1.388731625493765e-3) * square
    cos = 1.0 - 0.5 * square + square * square * (cos_poly + 4.166664568298827e-2)
    quarter = turns.astype(jnp.int32)
    odd = (quarter & 1) == 1
    turned_cos, turned_sin = jnp.where(odd, sin, cos), jnp.where(odd, cos, sin)
    return (
        jnp.where(((quarter + 1) & 2) == 2, -turned_cos, turned_cos),
        jnp.where((quarter & 2) == 2, -turned_sin, turned_sin),
    )


def multiples(c, s):
    c2 = 2.0 * (c * c) - 1.0
    s2 = 2.0 * (c * s)
    return (
        (c, s),
        (c2, s2),
        (c2 * c - s2 * s, s2 * c + c2 * s),
        (2.0 * (c2 * c2) - 1.0, 2.0 * (c2 * s2)),
    )


def adapted(entries, axes):
    one, two, three, shear, first, second = axes
    at = lambda row, col: entries[(min(row, col), max(row, col))]
    mean = at(one, one) + at(two, two)
    cross = 2.0 * at(one, two)
    spread = mean - cross
    half_shear = 0.5 * at(shear, shear)
    half_spread = 0.5 * spread
    half_first = 0.5 * at(first, first)
    half_second = 0.5 * at(second, second)
    lone = lambda with_: (at(one, with_) + at(two, with_), at(one, with_) - at(two, with_))
    sum_three, diff_three = lone(three)
    sum_shear, diff_shear = lone(shear)
    sum_first, diff_first = lone(first)
    sum_second, diff_second = lone(second)
    fixed = (
        mean + cross,
        sum_three,
        at(three, three),
        half_spread + half_shear,
        half_first + half_second,
    )
    pairs = [
        (2, at(one, one) - at(two, two), sum_shear),
        (2, diff_three, at(three, shear)),
        (1, sum_first, sum_second),
        (1, at(three, first), at(three, second)),
        (4, half_spread - half_shear, diff_shear),
        (2, half_first - half_second, at(first, second)),
        (1, diff_first + at(shear, second), at(shear, first) - diff_second),
        (3, diff_first - at(shear, second), at(shear, first) + diff_second),
    ]
    return fixed, pairs


def turned(adapted_set, angles):
    fixed, pairs = adapted_set
    fresh = []
    for order, x, y in pairs:
        c, s = angles[order - 1]
        fresh.append((order, c * x - s * y, s * x + c * y))
    return fixed, fresh


def natural(adapted_set, axes):
    one, two, three, shear, first, second = axes
    (whole, sum_three, three_three, shear_mean, side_mean), pairs = adapted_set
    (
        (_, lean, sum_shear),
        (_, diff_three, three_shear),
        (_, sum_first, sum_second),
        (_, three_first, three_second),
        (_, shear_half, diff_shear),
        (_, side_half, first_second),
        (_, real_one, imag_one),
        (_, real_three, imag_three),
    ) = pairs
    spread = shear_mean + shear_half
    diff_first = 0.5 * (real_one + real_three)
    diff_second = 0.5 * (imag_three - imag_one)
    quarter = 0.25 * (whole + spread)
    half_lean = 0.5 * lean
    out = {}

    def put(row, col, value):
        out[(min(row, col), max(row, col))] = value

    put(one, one, quarter + half_lean)
    put(two, two, quarter - half_lean)
    put(one, two, 0.25 * (whole - spread))
    for with_, total, gap in (
        (three, sum_three, diff_three),
        (shear, sum_shear, diff_shear),
        (first, sum_first, diff_first),
        (second, sum_second, diff_second),
    ):
        put(one, with_, 0.5 * (total + gap))
        put(two, with_, 0.5 * (total - gap))
    put(three, three, three_three)
    put(three, shear, three_shear)
    put(three, first, three_first)
    put(three, second, three_second)
    put(shear, shear, shear_mean - shear_half)
    put(shear, first, 0.5 * (imag_one + imag_three))
    put(shear, second, 0.5 * (real_one - real_three))
    put(first, first, side_mean + side_half)
    put(second, second, side_mean - side_half)
    put(first, second, first_second)
    return out


about_z = (0, 1, 2, 5, 4, 3)
about_x = (1, 2, 0, 3, 5, 4)


def rotated_stiffness(entries, trig):
    cos_one, cos_mid, cos_two, sin_one, sin_mid, sin_two = trig
    first = turned(adapted(entries, about_z), multiples(cos_two, sin_two))
    middle = turned(adapted(natural(first, about_z), about_x), multiples(cos_mid, sin_mid))
    last = turned(adapted(natural(middle, about_x), about_z), multiples(cos_one, sin_one))
    return natural(last, about_z)


def grain_kernel(
    crystal_hbm,
    euler_hbm,
    orient_hbm,
    weight_hbm,
    map_hbm,
    density_hbm,
    velocity_hbm,
    stress_hbm,
    send_ref,
    crystal_ref,
    euler_ref,
    orient_ref,
    weight_ref,
    map_ref,
    density_ref,
    velocity_ref,
    stress_ref,
    sums_ref,
    place_ref,
    acc_ref,
    fields_ref,
    arrived,
):
    row_part = lax.axis_index("gy")
    layer = lax.axis_index("ga")
    grains = weight_ref.shape[0]
    cells = weight_ref.shape[1]
    tiles = cells // LANES
    octets = grains // SUB
    table_tiles = euler_ref.shape[1] // LANES
    destinations = send_ref.shape[0] // BLOCK_ROWS

    copies = [
        pltpu.make_async_copy(source, target, arrived.at[at])
        for at, (source, target) in enumerate(
            [
                (map_hbm, map_ref),
                (crystal_hbm, crystal_ref),
                (orient_hbm, orient_ref),
                (euler_hbm, euler_ref),
                (weight_hbm, weight_ref),
                (stress_hbm, stress_ref),
                (velocity_hbm, velocity_ref),
                (density_hbm, density_ref),
            ]
        )
    ]
    for copy in copies:
        copy.start()
    sums_ref[...] = jnp.zeros_like(sums_ref)
    place_ref[...] = jnp.zeros_like(place_ref)

    for copy in copies[:5]:
        copy.wait()
    scale = (1.0, 1.0, 1.0, 2.0, 2.0, 2.0)
    entries = {
        (row, col): (scale[row] * scale[col]) * crystal_ref[pair]
        for pair, (row, col) in enumerate(upper_pairs)
    }
    def pick(tile, octet):
        index = orient_ref[pl.ds(octet * SUB * tiles + tile, SUB, stride=tiles), :]
        low = index & (LANES - 1)
        bits = [(index & (LANES << level)) != 0 for level in range(table_tiles.bit_length() - 1)]

        def find(which, first, level):
            if level == 0:
                source = jnp.broadcast_to(
                    euler_ref[which : which + 1, first * LANES : (first + 1) * LANES], (SUB, LANES)
                )
                return jnp.take_along_axis(source, low, axis=1, mode="promise_in_bounds")
            lower = find(which, first, level - 1)
            upper = find(which, first + (1 << (level - 1)), level - 1)
            return jnp.where(bits[level - 1], upper, lower)

        values = [find(which, 0, len(bits)) for which in range(3)]
        return values

    held = [pick(0, octet) for octet in range(octets)]

    slots = map_ref[...]
    half = 32
    inner = jnp.where(
        jnp.broadcast_to(slots & (half - 1), (half, cells)) == rows_of((half, cells)), 1.0, 0.0
    ).astype(jnp.bfloat16)
    outer = jnp.broadcast_to(slots // half, (half, cells)).astype(jnp.bfloat16)
    for chunk in range(cells // half):
        start = pl.multiple_of(chunk * 2 * half + row_part * half, half)
        place_ref[pl.ds(start, half), :] = jnp.where(
            outer == jnp.bfloat16(chunk), inner, jnp.bfloat16(0.0)
        )

    def add_tile(tile, held):
        lanes = slice(tile * LANES, (tile + 1) * LANES)
        for octet in range(octets):
            turns = [cos_and_sin(angle) for angle in held[octet]]
            rotated = rotated_stiffness(entries, [turn[at] for at in range(2) for turn in turns])
            mass = weight_ref[octet * SUB : (octet + 1) * SUB, lanes].astype(jnp.float32)
            masses = {1.0: mass, 0.5: 0.5 * mass, 0.25: 0.25 * mass}
            for pair, (row, col) in enumerate(upper_pairs):
                value = rotated[row, col] * masses[1.0 / (scale[row] * scale[col])]
                acc_ref[pair] = value if octet == 0 else acc_ref[pair] + value
            acc_ref[21] = mass if octet == 0 else acc_ref[21] + mass
        for at, named in enumerate((LOW_ROWS, HIGH_ROWS)):
            for first in (0, SUB):
                summed = sublane_sums([acc_ref[pair] for pair in named[first : first + SUB]])
                sums_ref[at * 16 + first : at * 16 + first + SUB, lanes] = summed

    def one_tile(tile, held):
        fresh = [pick(tile + 1, octet) for octet in range(octets)]
        add_tile(tile, held)
        return fresh

    for tile in range(tiles // 2):
        held = one_tile(tile, held)

    for copy in copies[5:]:
        copy.wait()
    own = row_part * 2 + layer

    def field_rows(component, y):
        if component < 6:
            return stress_ref[pl.ds(component * 32 + y, SUB, stride=4), :]
        if component < 9:
            return velocity_ref[pl.ds((component - 6) * 32 + y, SUB, stride=4), :]
        return density_ref[pl.ds(y, SUB, stride=4), :]

    def spread(component, slot, into):
        goal = own ^ slot
        for y in range(4):
            start = (goal // 2) * 64 + y * 16 + (goal % 2) * 8
            narrow = jnp.concatenate(
                [field_rows(component, y), jnp.zeros((SUB, LANES - 8), jnp.float32)], axis=1
            )
            into = into + pltpu.roll(narrow, start, 1)
        return into

    nothing = jnp.zeros((SUB, LANES), jnp.float32)
    for half in range(2):
        group, tail = nothing, nothing
        for slot in (0, 1, 3, 2):
            group = spread(half * HALF + slot, slot, group)
            if slot == 0:
                piece = spread(half * HALF + 4, slot, nothing)
            elif slot == 3:
                piece = pltpu.roll(piece, LANES // 2, 1)
            else:
                piece = other_layer(piece, lanes_of((SUB, LANES)))
            tail = tail + (piece if slot == 0 else pltpu.roll(piece, SUB - 2 * slot, 0))
        fields_ref[half, 0:SUB, :] = group
        fields_ref[half, SUB : SUB + 2, :] = tail[0:2]

    for tile in range(tiles // 2, tiles - 1):
        held = one_tile(tile, held)
    add_tile(tiles - 1, held)

    sums = sums_ref[...]
    part_one = sums.astype(jnp.bfloat16)
    rest = sums - part_one.astype(jnp.float32)
    part_two = rest.astype(jnp.bfloat16)
    part_three = (rest - part_two.astype(jnp.float32)).astype(jnp.bfloat16)
    parts = jnp.concatenate([part_one, part_two, part_three], axis=0)
    placed = lax.dot_general(
        parts, place_ref[...], (((1,), (1,)), ((), ())), preferred_element_type=jnp.float32
    )
    placed = placed[0:32] + placed[32:64] + placed[64:96]

    shift = 32 + row_part * 64
    bricks = destinations // 4
    lane = lanes_of((SUB, LANES))
    upper = lax.axis_index("gx") >= SUB // 2
    own_sums, edge_sums = [], []
    for brick in range(bricks):
        halves = [
            placed[at : at + 16, brick * LANES : (brick + 1) * LANES] for at in (0, 16)
        ]
        own_sums.append(halves[0] + pltpu.roll(halves[1], shift, 1))
        edge_sums.append(
            [
                half[0:8] + pltpu.roll(pltpu.roll(half, 16 - EDGE_ROWS, 0)[0:8], shift, 1)
                for half in halves
            ]
        )
    for brick in range(bricks):
        side = brick % 2
        before, after = brick - side - 1, brick - side + 2
        before = edge_sums[before][side] if before >= 0 else nothing
        after = edge_sums[after][side] if after < bricks else nothing
        near = jnp.where(upper, before, after)
        far = opposite_class(jnp.where(upper, after, before), lane)
        for inner in range(4):
            at = block_of(brick, inner, bricks) * BLOCK_ROWS
            edge = jnp.where(near_lanes(lane, inner // 2, inner % 2), near, far)
            send_ref[at : at + SUM_ROWS, :] = own_sums[brick][0:SUM_ROWS]
            send_ref[at + SUM_ROWS : at + FIELD_AT, :] = edge[0:EDGE_ROWS]
            send_ref[at + FIELD_AT : at + FIELD_AT + SUB, :] = fields_ref[side, 0:SUB, :]
            send_ref[at + FIELD_AT + SUB : at + BLOCK_ROWS, :] = fields_ref[side, SUB : SUB + 2, :]


def plane_shifts(dim, count):
    lane = lanes_of((count, LANES))
    position, extent, unit = (lane // 16, 8, 16) if dim == 1 else (lane % 16, 16, 1)
    terms = {}
    for order in range(1, 5):
        weight = stencil_weights[order - 1]
        behind = jnp.where(position >= order, -weight, 0.0)
        ahead = jnp.where(position < extent - order, weight, 0.0)
        for shift, own in ((order * unit, behind), (LANES - order * unit, ahead)):
            terms[shift] = terms[shift] + own if shift in terms else own
    return list(terms.items())


def tree_sum(terms):
    while len(terms) > 1:
        paired = [one + two for one, two in zip(terms[0::2], terms[1::2])]
        terms = paired + terms[2 * len(paired) :]
    return terms[0]


def plane_derivative(field, shifts):
    return tree_sum([weights * pltpu.roll(field, shift, 1) for shift, weights in shifts])


def row_derivative(read, start, count):
    return tree_sum(
        [
            stencil_weights[order - 1] * (read(start + order, count) - read(start - order, count))
            for order in range(1, 5)
        ]
    )


def velocity_update(wide_stress, old_velocity, density, inside, count):
    shifts = {dim: plane_shifts(dim, count) for dim in (1, 2)}

    def along(component, dim):
        if dim == 0:
            return row_derivative(
                lambda at, size: wide_stress[component, at : at + size, :], 4, count
            )
        return plane_derivative(wide_stress[component, 4 : 4 + count, :], shifts[dim])

    sums = [
        along(0, 0) + along(5, 1) + along(4, 2),
        along(5, 0) + along(1, 1) + along(3, 2),
        along(4, 0) + along(3, 1) + along(2, 2),
    ]
    return [
        jnp.where(inside, old_velocity[at] + time_step * sums[at] / density, 0.0)
        for at in range(3)
    ]


def stress_update(wide_velocity, start, old_stress, stiff):
    shifts = {dim: plane_shifts(dim, SUB) for dim in (1, 2)}

    def along(component, dim):
        if dim == 0:
            return row_derivative(
                lambda at, size: wide_velocity[component, pl.ds(at, size), :], start, SUB
            )
        return plane_derivative(wide_velocity[component, pl.ds(start, SUB), :], shifts[dim])

    strain = [
        along(0, 0),
        along(1, 1),
        along(2, 2),
        along(2, 1) + along(1, 2),
        along(2, 0) + along(0, 2),
        along(1, 0) + along(0, 1),
    ]
    return [
        old_stress[row]
        + time_step
        * tree_sum([stiff(symmetric_index(row, col)) * strain[col] for col in range(6)])
        for row in range(6)
    ]


def inside_rows(brick, bricks, margin, count):
    place = rows_of((count, LANES)) - margin + brick * SUB
    return (place >= 0) & (place < bricks * SUB)


def unpack_kernel(got_ref, out_ref):
    brick = lax.axis_index("gx")
    bricks = got_ref.shape[0] // BLOCK_ROWS // 4

    def by_slot(zero, one):
        first_slot = (lanes_of(zero.shape) // 32) % 2 == 0
        low = jnp.where(first_slot, zero, one)
        high = jnp.where(first_slot, one, zero)
        high = jnp.where(first_slot, pltpu.roll(high, LANES - 32, 1), pltpu.roll(high, 32, 1))
        return low, high

    for p in range(bricks):

        def both_layers(part, offset, count):
            first, second = [
                block_of(p, part * 2 + layer, bricks) * BLOCK_ROWS + offset for layer in range(2)
            ]
            return got_ref[first : first + count, :] + got_ref[second : second + count, :]

        low, high = by_slot(both_layers(0, 0, SUM_ROWS), both_layers(1, 0, SUM_ROWS))
        total = jnp.broadcast_to(high[10:11], (SUB, LANES))
        at = p * STIFF_ROWS
        out_ref[at : at + 8, :] = low[0:8] / total
        out_ref[at + 8 : at + 16, :] = high[0:8] / total
        out_ref[at + 16 : at + 19, :] = low[8:11] / total[0:3]
        out_ref[at + 19 : at + 22, :] = high[8:11] / total[0:3]
        low, high = by_slot(
            both_layers(0, SUM_ROWS, EDGE_ROWS), both_layers(1, SUM_ROWS, EDGE_ROWS)
        )
        at = EDGE_AT + p * SUM_ROWS
        out_ref[at : at + EDGE_ROWS, :] = low
        out_ref[at + EDGE_ROWS : at + SUM_ROWS, :] = high[0 : SUM_ROWS - EDGE_ROWS]

    def collect(source, offset, count, slot):
        lane = lanes_of((count, LANES))
        kind = (lane // 64) * 2 + (lane // 8) % 2
        pieces = [
            got_ref[pl.ds(block_of(source, q ^ slot, bricks) * BLOCK_ROWS + offset, count), :]
            for q in range(4)
        ]
        value = jnp.where(
            kind < 2,
            jnp.where(kind == 0, pieces[0], pieces[1]),
            jnp.where(kind == 2, pieces[2], pieces[3]),
        )
        if slot & 1:
            value = jnp.where(
                (lane // 8) % 2 == 0,
                pltpu.roll(value, LANES - 8, 1),
                pltpu.roll(value, 8, 1),
            )
        if slot & 2:
            value = pltpu.roll(value, 64, 1)
        return value

    for side in range(WIDE_ROWS // SUB):
        wanted = (brick // 2) * 2 + side - 2
        source = jnp.clip(wanted, 0, bricks - 1)
        valid = source == wanted
        for slot in range(4):
            at = WIDE_AT + slot * WIDE_ROWS + side * SUB
            value = collect(source, FIELD_AT, SUB, slot)
            out_ref[at : at + SUB, :] = jnp.where(valid, value, 0.0)
            at = WIDE_AT + 4 * WIDE_ROWS + side * SUB + 2 * slot
            value = collect(source, FIELD_AT + SUB, 2, slot)
            out_ref[at : at + 2, :] = jnp.where(valid, value, 0.0)


def stiffness_kernel(stiff_ref, out_ref, turned_ref):
    own = lax.axis_index("gy") * 64 + lax.axis_index("ga") * 8
    for p in range(SUB):
        turned_ref[...] = jnp.transpose(stiff_ref[p * STIFF_ROWS : p * STIFF_ROWS + 24, :])
        for y in range(4):
            rows = pl.ds(pl.multiple_of(own + y * 16, 8), 8)
            out_ref[p * 32 + y * 8 : p * 32 + y * 8 + 8, :] = turned_ref[rows, 0:21]


def steps_kernel(
    own_ref,
    other_ref,
    out_velocity_ref,
    out_stress_ref,
    wide_ref,
    edge_ref,
    first_velocity_ref,
    first_stress_ref,
    last_velocity_ref,
    *,
    bricks,
):
    brick = lax.axis_index("gx")
    row_part, layer = lax.axis_index("gy"), lax.axis_index("ga")
    odd = brick % 2
    lane = lanes_of((SUB, LANES))
    row = rows_of((SUB, LANES))

    for at in range(HALF):
        rows = pl.ds(pl.multiple_of(WIDE_AT + at * WIDE_ROWS + odd * SUB, SUB), 5 * SUB)
        wide_ref[odd * HALF + at] = own_ref[rows, :]
        wide_ref[(1 - odd) * HALF + at] = other_ref[rows, :]

    edge_valid = jnp.where(odd == 0, brick - 1, brick + 1)
    edge_valid = (edge_valid >= 0) & (edge_valid < bricks)
    near_row = jnp.where(odd == 0, row, SUB - 1 - row) >= SUB // 2
    own_lane = (lane // 64 == row_part) & ((lane // 8) % 2 == layer)
    usable = (own_lane | (near_row & near_lanes(lane, row_part, layer))) & edge_valid

    def edge(half, k):
        rows = pl.ds(EDGE_AT + k, SUB, stride=SUM_ROWS)
        value = jnp.where(odd == half, own_ref[rows, :], other_ref[rows, :])
        return jnp.where(near_row, value, opposite_class(value, lane))

    total = jnp.where(usable, edge(1, 10), 1.0)
    for half, named in enumerate((LOW_ROWS, HIGH_ROWS)):
        for k, pair in enumerate(named):
            if pair < 21:
                edge_ref[pair] = edge(half, k) / total

    inside = inside_rows(brick, bricks, 12, 32)
    density = jnp.where(inside, wide_ref[9, 4:36, :], 1.0)
    fresh = velocity_update(
        wide_ref, [wide_ref[6 + at, 4:36, :] for at in range(3)], density, inside, 32
    )
    for at in range(3):
        first_velocity_ref[at] = fresh[at]
    own_stiff = lambda pair: own_ref[pl.ds(pair, SUB, stride=STIFF_ROWS), :]
    for group, stiff, valid in (
        (SUB, own_stiff, None),
        (2 * SUB - odd * 2 * SUB, lambda pair: other_ref[pl.ds(pair, SUB, stride=STIFF_ROWS), :], None),
        (odd * 2 * SUB, lambda pair: edge_ref[pair], edge_valid),
    ):
        fresh = stress_update(
            first_velocity_ref,
            group + 4,
            [wide_ref[at, pl.ds(group + SUB, SUB), :] for at in range(6)],
            stiff,
        )
        for at in range(6):
            value = fresh[at] if valid is None else jnp.where(valid, fresh[at], 0.0)
            first_stress_ref[at, pl.ds(group, SUB), :] = value

    velocity = velocity_update(
        first_stress_ref,
        [first_velocity_ref[at, 8:24, :] for at in range(3)],
        density[8:24],
        inside_rows(brick, bricks, 4, 16),
        16,
    )
    for at in range(3):
        last_velocity_ref[at] = velocity[at]
    stress = stress_update(
        last_velocity_ref, 4, [first_stress_ref[at, 8:16, :] for at in range(6)], own_stiff
    )
    own = row_part * 64 + layer * 8

    def put(out_ref, at, value):
        for y in range(4):
            turned = pltpu.roll(value, (LANES - own - y * 16) % LANES, 1)
            out_ref[pl.ds(at * 32 + y, SUB, stride=4), :] = turned[:, 0:8]

    for at in range(3):
        put(out_velocity_ref, at, last_velocity_ref[at, 4:12, :])
    for at in range(6):
        put(out_stress_ref, at, stress[at])


def on_plane(euler_table, crystal, orient, weight, cell_map, density, velocity, stress):
    part_x = lax.axis_size("gx")
    devices = part_x * lax.axis_size("gy") * lax.axis_size("ga")
    grains, cells = orient.shape[0], orient.shape[3]
    tiles = cells // LANES
    octets = grains // SUB
    vmem = pl.BlockSpec(memory_space=pltpu.VMEM)
    hbm = pl.BlockSpec(memory_space=pltpu.HBM)
    f32 = jnp.float32

    send = pl.pallas_call(
        grain_kernel,
        out_shape=jax.ShapeDtypeStruct((devices * BLOCK_ROWS, LANES), f32),
        in_specs=[hbm] * 8,
        out_specs=vmem,
        scratch_shapes=[
            pltpu.SMEM((21,), f32),
            pltpu.VMEM(euler_table.shape, f32),
            pltpu.VMEM((grains * tiles, LANES), jnp.int32),
            pltpu.VMEM((grains, cells), weight.dtype),
            pltpu.VMEM((1, cells), jnp.int32),
            pltpu.VMEM((SUB * 4, 8), f32),
            pltpu.VMEM((3 * SUB * 4, 8), f32),
            pltpu.VMEM((6 * SUB * 4, 8), f32),
            pltpu.VMEM((32, cells), f32),
            pltpu.VMEM((2 * cells, cells), jnp.bfloat16),
            pltpu.VMEM((22, SUB, LANES), f32),
            pltpu.VMEM((2, 2 * SUB, LANES), f32),
            pltpu.SemaphoreType.DMA((8,)),
        ],
        compiler_params=pltpu.CompilerParams(vmem_limit_bytes=8 * 2**20),
    )(*[pltpu.with_memory_space_constraint(x, pltpu.HBM) for x in (
        crystal,
        euler_table,
        orient.reshape(grains * tiles, LANES),
        weight.reshape(grains, cells),
        cell_map.reshape(1, cells),
        density.reshape(SUB * 4, 8),
        velocity.reshape(3 * SUB * 4, 8),
        stress.reshape(6 * SUB * 4, 8),
    )])
    got = lax.all_to_all(
        send.reshape(devices, 1, BLOCK_ROWS * LANES),
        ("gy", "gx", "ga"),
        split_axis=0,
        concat_axis=0,
        tiled=True,
    ).reshape(devices * BLOCK_ROWS, LANES)
    small = pltpu.CompilerParams(vmem_limit_bytes=8 * 2**20)
    own_part = pl.pallas_call(
        unpack_kernel,
        out_shape=jax.ShapeDtypeStruct((WIDE_AT + HALF * WIDE_ROWS, LANES), f32),
        in_specs=[vmem],
        out_specs=vmem,
        compiler_params=small,
    )(got)
    other_part = lax.ppermute(own_part, "gx", [(i, i ^ 1) for i in range(part_x)])
    stiffness = pl.pallas_call(
        stiffness_kernel,
        out_shape=jax.ShapeDtypeStruct((SUB * 4 * 8, 21), f32),
        in_specs=[vmem],
        out_specs=vmem,
        scratch_shapes=[pltpu.VMEM((LANES, 24), f32)],
        cost_estimate=pl.CostEstimate(flops=100000, bytes_accessed=200000, transcendentals=0),
        compiler_params=small,
    )(own_part)
    new_velocity, new_stress = pl.pallas_call(
        functools.partial(steps_kernel, bricks=part_x),
        out_shape=(
            jax.ShapeDtypeStruct((3 * SUB * 4, 8), f32),
            jax.ShapeDtypeStruct((6 * SUB * 4, 8), f32),
        ),
        in_specs=[vmem] * 2,
        out_specs=(vmem,) * 2,
        scratch_shapes=[
            pltpu.VMEM((FIELDS, 5 * SUB, LANES), f32),
            pltpu.VMEM((21, SUB, LANES), f32),
            pltpu.VMEM((3, 4 * SUB, LANES), f32),
            pltpu.VMEM((6, 3 * SUB, LANES), f32),
            pltpu.VMEM((3, 2 * SUB, LANES), f32),
        ],
        compiler_params=small,
    )(own_part, other_part)
    return (
        stiffness.reshape(SUB, 4, 8, 21).transpose(3, 0, 1, 2),
        new_velocity.reshape(3, SUB, 4, 8),
        new_stress.reshape(6, SUB, 4, 8),
    )


def on_device(euler_table, crystal, orient, weight, cell_map, density, velocity, stress):
    sizes = (lax.axis_size("gx"), lax.axis_size("gy"), lax.axis_size("ga"))
    form = on_plane if fits_plane(*sizes, orient, stress, euler_table) else on_device_general
    return form(euler_table, crystal, orient, weight, cell_map, density, velocity, stress)


def solution(mesh):
    return jax.shard_map(
        on_device,
        mesh=mesh,
        in_specs=(
            P(),
            P(),
            P("ga", "gx", "gy", None),
            P("ga", "gx", "gy", None),
            P("gx", "gy", None),
            P("gx", "gy", "ga"),
            P(None, "gx", "gy", "ga"),
            P(None, "gx", "gy", "ga"),
        ),
        out_specs=(P(None, "gx", "gy", "ga"), P(None, "gx", "gy", "ga"), P(None, "gx", "gy", "ga")),
        check_vma=False,
    )
```
